32 devices in a mesh: vel: 4 (over x, core), strip: 8 (over z, y).
Axes of the slice: x: 2, y: 2, z: 4, core: 2. Of those that a mesh axis runs over, the one named last changes fastest.
Arguments:
- dist: float32 [13824, 32, 128], P('vel', 'strip'), may hold values from -25 to 25
- cell_type: int32 [32, 128], P('strip'), may hold values 0 or 1
- collision_rate: float32 [32, 128], P('strip'), may hold values from 0.05 to 0.5
- vel_index: int32 [3, 13824], P(None, 'vel'), may hold values from 0 to 23, as said below
Outputs:
- dist_out: float32 [13824, 32, 128], P('vel', 'strip')
- state: float32 [5, 32, 128], P(None, 'strip')
The draws below stay inside these ranges and needn't reach their ends.
Inputs may be any that keep to these rules, and one draw needn't show every extreme that they name: `vel_index`: each point of the 24 x 24 x 24 velocity grid is listed once. In every aligned block of 3456 velocities, the first half have x index at least 12 and the second half below it.
All inputs are finite; a program needn't handle non-finite values. No bound on the sum of `cell_type` on one device may be relied on, other than what follows from the above.
Results may differ from the reference program's by a relative error of at most 0.0003.
Values sent between devices are 32-bit elements; how exact they have to be, the bound alone decides.
No kernel may reach another device: no remote copies, remote signals or barrier semaphores. Data moves between devices by JAX's collectives and lax.ppermute only.
A program may use at most 128 MiB of HBM per device.

```python
import math
import jax
import jax.numpy as jnp
from jax import lax

GV = 24
VELS = 13824
VEL_DEV = 3456
NY = 128
NX = 32
ITERS = 2
SWEEPS = 3


def grid_points(key):
    half_count = GV * GV * GV // 2
    plane = GV * GV
    order_fwd = jax.random.permutation(jax.random.fold_in(key, 11), half_count)
    order_back = jax.random.permutation(jax.random.fold_in(key, 12), half_count)

    def triples(order, offset):
        return jnp.stack([order // plane + offset, order // GV % GV, order % GV])
    forward = triples(order_fwd, GV // 2).reshape(3, VELS // VEL_DEV, VEL_DEV // 2)
    backward = triples(order_back, 0).reshape(3, VELS // VEL_DEV, VEL_DEV // 2)
    return jnp.concatenate([forward, backward], axis=2).reshape(3, VELS).astype(jnp.int32)


def draw_vel_index(key, part):
    return grid_points(key)


def draw_dist(key, part):
    points = grid_points(key).astype(jnp.float32)
    comps = (points - (GV - 1) / 2.0) * (8.0 / GV)
    energy = comps[0] * comps[0] + comps[1] * comps[1] + comps[2] * comps[2]
    basis = jnp.stack([jnp.ones_like(energy), 0.5 * comps[0], 0.5 * comps[1], 0.5 * comps[2], (energy - 1.5) / 6.0])
    key_coef = jax.random.fold_in(key, 21)
    key_noise = jax.random.fold_in(key, 22)
    coef = 0.5 * jax.random.truncated_normal(key_coef, -3.0, 3.0, (5, NX, NY), jnp.float32)
    noise = jax.random.truncated_normal(key_noise, -3.0, 3.0, (VELS, NX, NY), jnp.float32)
    return jnp.einsum('kv,kxy->vxy', basis, coef) + noise


def touch_ends(array, rng, smallest, top_value):
    longest = array.shape.index(max(array.shape))
    spots = []
    for shift in (0, 1):
        where = [jax.random.randint(jax.random.fold_in(rng, axis), (), 0, length) for axis, length in enumerate(array.shape)]
        where[longest] = (where[longest] + shift) % array.shape[longest]
        spots.append(tuple(where))
    return array.at[spots[0]].set(smallest).at[spots[1]].set(top_value)


def shard_levels(own_key, extent, shards, smallest, top_value):
    gain = 1.0
    for position, blocks in shards:
        draws = jax.random.uniform(jax.random.fold_in(jax.random.fold_in(own_key, 6), position), (blocks,), jnp.float32, smallest / len(shards), top_value / len(shards))
        gain = gain * jnp.repeat(jnp.exp(draws), extent[position] // blocks).reshape((-1,) + (1,) * (len(extent) - 1 - position))
    return gain


def setup_inputs(seed: int = 0) -> dict:
    keys = jax.random.split(jax.random.key(seed), 5)
    return {
        "dist": draw_dist(jax.random.fold_in(keys[4], 71), 0),
        "cell_type": touch_ends((jax.random.randint(keys[1], (NX, NY), 0, 8) < 1).astype(jnp.int32), jax.random.fold_in(keys[1], 1), 0, 1),
        "collision_rate": jnp.clip(jnp.exp(math.log(0.5) - 2.3025851 * jax.random.uniform(keys[2], (NX, NY), jnp.float32) ** shard_levels(keys[2], (NX, NY), ((0, 8),), -0.2, 0.2)), 0.05, 0.5),
        "vel_index": draw_vel_index(jax.random.fold_in(keys[4], 71), 0),
    }


STEP_RATIO = 0.1
SOURCE_WEIGHT = 0.5
HEAT_WEIGHT = 4.0 / 15.0
HIGH = lax.Precision.HIGHEST


def speeds(vel_index):
    return (vel_index.astype(jnp.float32) - (GV - 1) / 2.0) * (8.0 / GV)


def moment_table(comps):
    vel_x, vel_y, vel_z = comps[0], comps[1], comps[2]
    energy = vel_x * vel_x + vel_y * vel_y + vel_z * vel_z
    volume = (8.0 / GV) ** 3
    weight = volume * math.pi ** -1.5 * jnp.exp(-energy)
    rows = [jnp.ones_like(vel_x), vel_x, vel_y, vel_z, energy, vel_x * vel_x, vel_y * vel_y,
            vel_x * vel_y, vel_x * vel_z, vel_y * vel_z, energy * vel_x, energy * vel_y, energy * vel_z]
    return jnp.stack(rows) * weight


def state_table(comps):
    vel_x, vel_y, vel_z = comps[0], comps[1], comps[2]
    energy = vel_x * vel_x + vel_y * vel_y + vel_z * vel_z
    shape_heat = HEAT_WEIGHT * (energy - 2.5)
    columns = [jnp.ones_like(vel_x), 2.0 * vel_x, 2.0 * vel_y, 2.0 * vel_z, energy - 1.5,
               shape_heat * vel_x, shape_heat * vel_y, shape_heat * vel_z]
    return jnp.stack(columns, axis=1)


def macro_parts(moments):
    third = moments[4] * (2.0 / 3.0)
    start = jnp.stack([moments[0], moments[1], moments[2], moments[3], third - moments[0]])
    heat = jnp.stack([moments[10] - 2.5 * moments[1], moments[11] - 2.5 * moments[2], moments[12] - 2.5 * moments[3]])
    flux_fields = jnp.stack([moments[1], moments[2], 2.0 * moments[5] - third, 2.0 * moments[7],
                             2.0 * moments[6] - third, 2.0 * moments[8], 2.0 * moments[9], heat[0], heat[1]])
    return start, flux_fields, heat


def source_terms(start, framed):
    diff_x = 0.5 * (framed[:, 2:, 1:-1] - framed[:, :-2, 1:-1])
    diff_y = 0.5 * (framed[:, 1:-1, 2:] - framed[:, 1:-1, :-2])
    spread = jnp.stack([diff_x[0] + diff_y[1], diff_x[2] + diff_y[3], diff_x[3] + diff_y[4],
                        diff_x[5] + diff_y[6], diff_x[7] + diff_y[8]])
    return start - SOURCE_WEIGHT * spread


def neighbour_sum(framed):
    return framed[:, 2:, 1:-1] + framed[:, :-2, 1:-1] + framed[:, 1:-1, 2:] + framed[:, 1:-1, :-2]


def limiter(left, right):
    return jnp.where(left * right > 0, jnp.sign(left) * jnp.minimum(jnp.abs(left), jnp.abs(right)), 0.0)


def interface_diff(extended, speed, axis, count):
    def part(lower, upper):
        return lax.slice_in_dim(extended, lower, upper, axis=axis)
    left = part(1, count + 3) - part(0, count + 2)
    right = part(2, count + 4) - part(1, count + 3)
    slope = limiter(left, right)
    upwind = part(1, count + 2) + 0.5 * lax.slice_in_dim(slope, 0, count + 1, axis=axis)
    downwind = part(2, count + 3) - 0.5 * lax.slice_in_dim(slope, 1, count + 2, axis=axis)
    flux = speed * jnp.where(speed > 0, upwind, downwind)
    return lax.slice_in_dim(flux, 1, count + 1, axis=axis) - lax.slice_in_dim(flux, 0, count, axis=axis)


def relax(dist, extended, vel_x, vel_y, table, fields, wall, rate):
    count_x = dist.shape[1]
    count_y = dist.shape[2]
    wide = jnp.pad(dist, ((0, 0), (0, 0), (2, 2)))
    drift = interface_diff(extended, vel_x[:, None, None], 1, count_x)
    drift = drift + interface_diff(wide, vel_y[:, None, None], 2, count_y)
    target = jnp.dot(table, fields.reshape(8, -1), precision=HIGH).reshape(dist.shape)
    moved = dist - STEP_RATIO * drift + rate * (target - dist)
    return jnp.where(wall, target, moved)


def reference(dist, cell_type, collision_rate, vel_index):
    comps = speeds(vel_index)
    weights = moment_table(comps)
    table = state_table(comps)
    wall = cell_type == 1
    kappa = 0.5 / collision_rate
    block = VELS // GV

    def moment_sum(field):
        return jnp.dot(weights, field.reshape(VELS, NX * NY), precision=HIGH).reshape(13, NX, NY)

    start, flux_fields, heat = macro_parts(moment_sum(dist))
    fields = jnp.concatenate([start, heat])
    state = start
    for iteration in range(ITERS):
        def kinetic(pieces):
            piece, vel_x, vel_y, rows = pieces
            extended = jnp.pad(piece, ((0, 0), (2, 2), (0, 0)))
            return relax(piece, extended, vel_x, vel_y, rows, fields, wall, collision_rate)

        post = lax.map(kinetic, (dist.reshape(GV, block, NX, NY), comps[0].reshape(GV, block),
                                 comps[1].reshape(GV, block), table.reshape(GV, block, 8)))
        post = post.reshape(VELS, NX, NY)
        start, flux_fields, heat = macro_parts(moment_sum(post))
        source = source_terms(start, jnp.pad(flux_fields, ((0, 0), (1, 1), (1, 1))))
        state = start
        for sweep in range(SWEEPS):
            state = (source + kappa * neighbour_sum(jnp.pad(state, ((0, 0), (1, 1), (1, 1))))) / (1.0 + 4.0 * kappa)
        change = jnp.dot(table[:, :5], (state - start).reshape(5, NX * NY), precision=HIGH)
        dist = post + change.reshape(VELS, NX, NY)
        fields = jnp.concatenate([state, heat])
    return dist, state
```

```python
import functools
import math

import jax
import jax.numpy as jnp
import numpy as np
from jax import lax
from jax.experimental import pallas as pl
from jax.experimental.pallas import tpu as pltpu
from jax.sharding import PartitionSpec as P

STEP_RATIO = 0.1
SOURCE_WEIGHT = 0.5
HEAT_WEIGHT = 4.0 / 15.0
SWEEPS = 3
HIGH = lax.Precision.HIGHEST
LANES = 128
STRIP_ROWS = 4
BLOCK_ROWS = 2 * STRIP_ROWS
SPAN = 3 * BLOCK_ROWS
GROUP = 16
F32 = jnp.float32
BF16 = jnp.bfloat16


def params(**more):
    return pltpu.CompilerParams(vmem_limit_bytes=40 * 1024 * 1024, **more)


def moment_rows(vel_x, vel_y, vel_z, volume, lib):
    energy = vel_x * vel_x + vel_y * vel_y + vel_z * vel_z
    weight = volume * math.pi ** (-1.5) * lib.exp(-energy)
    rows = [
        lib.ones_like(vel_x),
        vel_x,
        vel_y,
        vel_z,
        energy,
        vel_x * vel_x,
        vel_y * vel_y,
        vel_x * vel_y,
        vel_x * vel_z,
        vel_y * vel_z,
        energy * vel_x,
        energy * vel_y,
        energy * vel_z,
    ]
    return lib.stack(rows) * weight


def state_rows(vel_x, vel_y, vel_z, lib):
    energy = vel_x * vel_x + vel_y * vel_y + vel_z * vel_z
    shape_heat = HEAT_WEIGHT * (energy - 2.5)
    rows = [
        lib.ones_like(vel_x),
        2.0 * vel_x,
        2.0 * vel_y,
        2.0 * vel_z,
        energy - 1.5,
        shape_heat * vel_x,
        shape_heat * vel_y,
        shape_heat * vel_z,
    ]
    return lib.stack(rows)


def target_moments(points):
    line = (np.arange(points) - (points - 1) / 2.0) * (8.0 / points)
    comps = [a.reshape(-1) for a in np.meshgrid(line, line, line, indexing="ij")]
    gram = moment_rows(*comps, (8.0 / points) ** 3, np) @ state_rows(*comps, np).T
    gram[np.abs(gram) < 1e-12] = 0.0
    full = np.zeros((16, 8), np.float32)
    full[:13] = gram
    return full


def macro_matrix():
    third = 2.0 / 3.0
    unit = np.eye(16, dtype=np.float64)
    start = [unit[0], unit[1], unit[2], unit[3], third * unit[4] - unit[0]]
    heat = [unit[10] - 2.5 * unit[1], unit[11] - 2.5 * unit[2], unit[12] - 2.5 * unit[3]]
    flux = [
        unit[1],
        unit[2],
        2.0 * unit[5] - third * unit[4],
        2.0 * unit[7],
        2.0 * unit[6] - third * unit[4],
        2.0 * unit[8],
        2.0 * unit[9],
        heat[0],
        heat[1],
    ]
    out = np.zeros((32, 16), np.float64)
    for row in range(5):
        out[row] = start[row]
        out[8 + row] = flux[(0, 2, 3, 5, 7)[row]]
        out[16 + row] = flux[(1, 3, 4, 6, 8)[row]]
    for row in range(3):
        out[24 + 5 + row] = heat[row]
    return out.astype(np.float32)


def rounded(value):
    return lax.reduce_precision(value, 8, 7)


def minmod(left, right):
    low = jnp.minimum(left, right)
    high = jnp.maximum(left, right)
    return jnp.maximum(low, 0.0) + jnp.minimum(high, 0.0)


def strided(start, count):
    return pl.ds(start, count, stride=STRIP_ROWS)


def pack_kernel(size, side_ref, far_ref, own_ref, mid_ref, edge_ref, down_ref):
    side = side_ref[0]
    for i in range(4):
        row = jnp.where(side == 1, i, 3 - i)
        part = far_ref[strided(row, size), :]
        if i < 2:
            mid_ref[i] = part
        else:
            edge_ref[i - 2] = part
    down_ref[...] = own_ref[strided(jnp.where(side == 1, 3, 0), size), :]


def pack(side, flat, half, chunk, first, size):
    steps = chunk // size
    shift = half // size
    begin = first // size
    return pl.pallas_call(
        functools.partial(pack_kernel, size),
        out_shape=(
            jax.ShapeDtypeStruct((2, chunk, LANES), F32),
            jax.ShapeDtypeStruct((2, chunk, LANES), F32),
            jax.ShapeDtypeStruct((chunk, LANES), F32),
        ),
        grid_spec=pltpu.PrefetchScalarGridSpec(
            num_scalar_prefetch=1,
            grid=(steps,),
            in_specs=[
                pl.BlockSpec((4 * size, LANES), lambda i, s: ((1 - s[0]) * shift + begin + i, 0)),
                pl.BlockSpec((4 * size, LANES), lambda i, s: (s[0] * shift + begin + i, 0)),
            ],
            out_specs=[
                pl.BlockSpec((2, size, LANES), lambda i, s: (0, i, 0)),
                pl.BlockSpec((2, size, LANES), lambda i, s: (0, i, 0)),
                pl.BlockSpec((size, LANES), lambda i, s: (i, 0)),
            ],
        ),
        compiler_params=params(),
        name="pack",
        cost_estimate=pl.CostEstimate(
            flops=0, transcendentals=0, bytes_accessed=chunk * LANES * 4 * 13
        ),
    )(side, flat, flat)


def split_store(value, first_ref, second_ref, rows, columns):
    first = value.astype(BF16)
    first_ref[rows, columns] = first
    second_ref[rows, columns] = (value - first.astype(F32)).astype(BF16)


def weighted(weights, first, second):
    both = jnp.dot(weights, first, preferred_element_type=F32)
    return both[:16] + both[16:] + jnp.dot(weights[:16], second, preferred_element_type=F32)


def moment_kernel(size, dist_ref, weight_ref, out_ref, first_ref, second_ref):
    @pl.when(pl.program_id(0) == 0)
    def _():
        out_ref[...] = jnp.zeros_like(out_ref)

    for row in range(STRIP_ROWS):
        columns = pl.ds(row * LANES, LANES)
        split_store(
            dist_ref[strided(row, size), :], first_ref, second_ref, pl.ds(0, size), columns
        )
    out_ref[...] += weighted(weight_ref[0], first_ref[...], second_ref[...])


def home_moments(flat, weights, size):
    count = flat.shape[0] // STRIP_ROWS
    width = STRIP_ROWS * LANES
    return pl.pallas_call(
        functools.partial(moment_kernel, size),
        out_shape=jax.ShapeDtypeStruct((16, width), F32),
        grid=(count // size,),
        in_specs=[
            pl.BlockSpec((4 * size, LANES), lambda i: (i, 0)),
            pl.BlockSpec((1, 32, size), lambda i: (i, 0, 0)),
        ],
        out_specs=pl.BlockSpec((16, width), lambda i: (0, 0)),
        scratch_shapes=[pltpu.VMEM((size, width), BF16), pltpu.VMEM((size, width), BF16)],
        compiler_params=params(),
        name="home_moments",
        cost_estimate=pl.CostEstimate(
            flops=2 * 48 * count * width, transcendentals=0, bytes_accessed=count * width * 4
        ),
    )(flat, weights)


def transport_kernel(size, second_pass, side_ref, *refs):
    if second_pass:
        (table_ref, change_ref, q_first, q_mid, q_edge, up_ref, down_ref, *rest) = refs
    else:
        (own_ref, mid_ref, edge_ref, up_ref, down_ref, *rest) = refs
    (const_ref, weight_ref, cell_ref, sum_in_ref, *rest) = rest
    if second_pass:
        (near_out, far_out, sum_ref, first_ref, second_ref, lift_ref) = rest
    else:
        (first_out, mid_out, edge_out, sum_ref, first_ref, second_ref) = rest
    side = side_ref[0]

    @pl.when(pl.program_id(0) == 0)
    def _():
        sum_ref[...] = sum_in_ref[...]

    if second_pass:
        lift_ref[...] = jnp.dot(table_ref[...], change_ref[...], preferred_element_type=F32)

    lane = lax.broadcasted_iota(jnp.int32, (GROUP, LANES), 1)
    inner_low = jnp.where(lane == 0, 0.0, 1.0)
    inner_high = jnp.where(lane == LANES - 1, 0.0, 1.0)

    def body(group, carry):
        base = pl.multiple_of(group * GROUP, GROUP)
        rows = pl.ds(base, GROUP)

        def load(row):
            if row < 0:
                value = up_ref[row + 2, rows, :]
            elif row == 8:
                value = down_ref[rows, :]
            elif second_pass:
                if row == 0:
                    value = q_first[rows, :]
                elif row < 6:
                    value = q_mid[row - 1, rows, :]
                else:
                    value = q_edge[row - 6, rows, :]
            elif row < 4:
                value = own_ref[
                    strided(base * STRIP_ROWS + jnp.where(side == 1, 3 - row, row), GROUP), :
                ]
            elif row < 6:
                value = mid_ref[row - 4, rows, :]
            else:
                value = edge_ref[row - 6, rows, :]
            if second_pass:
                value = value + lift_ref[rows, pl.ds((row + 2) * LANES, LANES)]
            return value

        def wide(column):
            return jnp.broadcast_to(const_ref[rows, column : column + 1], (GROUP, LANES))

        speed_x = wide(0)
        speed_y = wide(1)
        half_sign = wide(2)
        forward = half_sign > 0.0
        open_end = jnp.where(forward, inner_low, inner_high)

        behind = load(-2)
        here = load(-1)
        ahead = load(0)
        step = ahead - here
        upwind = here + 0.5 * minmod(here - behind, step)
        here = ahead
        for row in range(BLOCK_ROWS):
            ahead = load(row + 1)
            next_step = ahead - here
            next_upwind = here + 0.5 * minmod(step, next_step)
            drift = speed_x * (next_upwind - upwind)
            step = next_step
            upwind = next_upwind
            left = here - pltpu.roll(here, 1, 1) * inner_low
            right = pltpu.roll(here, LANES - 1, 1) * inner_high - here
            face = here + half_sign * minmod(left, right)
            other = jnp.where(forward, pltpu.roll(face, 1, 1), pltpu.roll(face, LANES - 1, 1))
            drift = drift + speed_y * (face - other * open_end)
            keep = jnp.broadcast_to(cell_ref[row : row + 1, :], (GROUP, LANES))
            fluid = jnp.broadcast_to(cell_ref[row + 8 : row + 9, :], (GROUP, LANES))
            value = keep * here - fluid * drift
            split_store(value, first_ref, second_ref, rows, pl.ds(row * LANES, LANES))
            if second_pass:
                if row < 4:
                    near_out[row, rows, :] = value
                else:
                    far_out[row - 4, rows, :] = value
            elif row == 0:
                first_out[rows, :] = value
            elif row < 6:
                mid_out[row - 1, rows, :] = value
            else:
                edge_out[row - 6, rows, :] = value
            here = ahead
        return carry

    lax.fori_loop(0, size // GROUP, body, 0)
    part = weighted(weight_ref[0], first_ref[...], second_ref[...])
    for row in range(BLOCK_ROWS):
        place = jnp.where(side == 1, 7 - row, row)
        columns = pl.ds(pl.multiple_of(place * LANES, LANES), LANES)
        sum_ref[:, columns] += part[:, row * LANES : (row + 1) * LANES]


def transport(side, sources, tables, cells, sums, half, chunk, first, size, change=None):
    second_pass = change is not None
    steps = chunk // size
    shift = half // size
    begin = first // size
    table, const, weights = tables
    width = BLOCK_ROWS * LANES

    def mine(i, s):
        return s[0] * shift + begin + i

    two = pl.BlockSpec((2, size, LANES), lambda i, s: (0, i, 0))
    one = pl.BlockSpec((size, LANES), lambda i, s: (i, 0))
    if second_pass:
        args = [table, change]
        specs = [
            pl.BlockSpec((size, 48), lambda i, s: (mine(i, s), 0)),
            pl.BlockSpec(change.shape, lambda i, s: (0, 0)),
            one,
            pl.BlockSpec((5, size, LANES), lambda i, s: (0, i, 0)),
            two,
            two,
            one,
        ]
        four = pl.BlockSpec((4, size, LANES), lambda i, s: (0, i, 0))
        outs = [jax.ShapeDtypeStruct((4, chunk, LANES), F32)] * 2
        out_specs = [four, four]
        scratch = [pltpu.VMEM((size, 11 * LANES), F32)]
    else:
        args = []
        specs = [
            pl.BlockSpec((4 * size, LANES), lambda i, s: (mine(i, s), 0)),
            two,
            two,
            two,
            one,
        ]
        outs = [
            jax.ShapeDtypeStruct((chunk, LANES), F32),
            jax.ShapeDtypeStruct((5, chunk, LANES), F32),
            jax.ShapeDtypeStruct((2, chunk, LANES), F32),
        ]
        out_specs = [one, pl.BlockSpec((5, size, LANES), lambda i, s: (0, i, 0)), two]
        scratch = []
    whole = pl.BlockSpec((16, width), lambda i, s: (0, 0))
    return pl.pallas_call(
        functools.partial(transport_kernel, size, second_pass),
        out_shape=(*outs, jax.ShapeDtypeStruct((16, width), F32)),
        grid_spec=pltpu.PrefetchScalarGridSpec(
            num_scalar_prefetch=1,
            grid=(steps,),
            in_specs=[
                *specs,
                pl.BlockSpec((size, 8), lambda i, s: (mine(i, s), 0)),
                pl.BlockSpec((1, 32, size), lambda i, s: (mine(i, s), 0, 0)),
                pl.BlockSpec((16, LANES), lambda i, s: (0, 0)),
                whole,
            ],
            out_specs=[*out_specs, whole],
            scratch_shapes=[
                pltpu.VMEM((size, width), BF16),
                pltpu.VMEM((size, width), BF16),
                *scratch,
            ],
        ),
        compiler_params=params(),
        name="transport_second" if second_pass else "transport_first",
        cost_estimate=pl.CostEstimate(
            flops=60 * chunk * width, transcendentals=0, bytes_accessed=chunk * LANES * 4 * 19
        ),
    )(side, *args, *sources, const, weights, cells, sums)


def sweep_block(inputs, relax, rate):
    start, flux_x, flux_y = inputs
    lane = lax.broadcasted_iota(jnp.int32, (8, LANES), 1)
    inner_low = jnp.where(lane == 0, 0.0, 1.0)
    inner_high = jnp.where(lane == LANES - 1, 0.0, 1.0)

    def block(array, row):
        if row < 0 or row >= SPAN:
            return jnp.zeros((8, LANES), F32)
        return array[:, row * LANES : (row + 1) * LANES]

    def lower(value):
        return pltpu.roll(value, 1, 1) * inner_low

    def upper(value):
        return pltpu.roll(value, LANES - 1, 1) * inner_high

    source = []
    for row in range(SPAN):
        diff_x = 0.5 * (block(flux_x, row + 1) - block(flux_x, row - 1))
        side = block(flux_y, row)
        diff_y = 0.5 * (upper(side) - lower(side))
        source.append(block(start, row) - SOURCE_WEIGHT * (diff_x + diff_y))
    zero = jnp.zeros((8, LANES), F32)
    kappa = [block(rate, row) for row in range(SPAN)]
    scale = [block(relax, row) for row in range(SPAN)]
    state = [block(start, row) for row in range(SPAN)]
    for _ in range(SWEEPS):
        near = [zero, *state, zero]
        state = [
            (source[row] + kappa[row] * (near[row] + near[row + 2] + lower(near[row + 1]) + upper(near[row + 1])))
            * scale[row]
            for row in range(SPAN)
        ]
    return jnp.concatenate(state, axis=1)


def stacked(value):
    first = value.astype(BF16)
    rest = value - first.astype(F32)
    second = rest.astype(BF16)
    third = (rest - second.astype(F32)).astype(BF16)
    return jnp.concatenate([first, second, third, first, second, first], axis=0)


def relax_rows(rate):
    inside = rate > 0.0
    kappa = jnp.where(inside, 0.5 / jnp.where(inside, rate, 1.0), 0.0)
    scale = jnp.where(inside, 1.0 / (1.0 + 4.0 * kappa), 0.0)
    width = rate.shape[1]
    return jnp.broadcast_to(kappa, (8, width)), jnp.broadcast_to(scale, (8, width))


def place_blocks(info_ref, span_ref, own, pair_a, pair_b):
    odd = info_ref[1]
    width = BLOCK_ROWS * LANES
    span_ref[:, width : 2 * width] = own
    place_a = pl.multiple_of((1 - odd) * 2 * width, width)
    place_b = pl.multiple_of(odd * 2 * width, width)
    span_ref[:, pl.ds(place_a, width)] = pair_a
    span_ref[:, pl.ds(place_b, width)] = pair_b


def first_macro_kernel(
    info_ref, sum_ref, sum_a_ref, sum_b_ref, near_ref, far_ref, gram_ref, mat_ref,
    change_ref, keep_ref, span_ref, home_ref,
):
    side = info_ref[0]
    odd = info_ref[1]
    width = BLOCK_ROWS * LANES
    part = STRIP_ROWS * LANES
    place_blocks(info_ref, span_ref, sum_ref[...], sum_a_ref[...], sum_b_ref[...])
    for ref, where in ((near_ref, side), (far_ref, 1 - side)):
        for index, block in enumerate((1, (1 - odd) * 2, odd * 2)):
            spot = pl.multiple_of(block * width + where * part, part)
            home_ref[:, pl.ds(spot, part)] = ref[index]
    home = home_ref[...]
    rate = home[13:14, :]
    ratio = jnp.where(home[14:15, :] > 0.5, 1.0, rate)
    mat = mat_ref[...]
    first = jnp.dot(mat, jnp.where(lax.broadcasted_iota(jnp.int32, home.shape, 0) < 13, home, 0.0), precision=HIGH)
    fields = first[:8] + first[24:]
    moments = span_ref[...] + ratio * jnp.dot(gram_ref[...], fields, precision=HIGH)
    all_parts = jnp.dot(mat, moments, precision=HIGH)
    start = all_parts[:8]
    kappa, scale = relax_rows(rate)
    state = sweep_block((start, all_parts[8:16], all_parts[16:24]), scale, kappa)
    change = ratio * fields + (state - start)
    span_ref[0:8, :] = change
    keep_ref[0:8, :] = state + all_parts[24:]
    keep_ref[8:9, :] = rate
    keep_ref[9:10, :] = ratio
    keep_ref[10:16, :] = jnp.zeros((6, SPAN * LANES), F32)
    for row in range(-2, 9):
        spot = jnp.where(side == 1, 15 - row, 8 + row)
        piece = span_ref[0:8, pl.ds(pl.multiple_of(spot * LANES, LANES), LANES)]
        change_ref[:, (row + 2) * LANES : (row + 3) * LANES] = stacked(piece)


def second_macro_kernel(
    info_ref, sum_ref, sum_a_ref, sum_b_ref, keep_ref, gram_ref, mat_ref,
    change_ref, state_ref, span_ref,
):
    side = info_ref[0]
    place_blocks(info_ref, span_ref, sum_ref[...], sum_a_ref[...], sum_b_ref[...])
    fields = keep_ref[0:8, :]
    rate = keep_ref[8:9, :]
    ratio = keep_ref[9:10, :]
    moments = span_ref[...] + ratio * jnp.dot(gram_ref[...], fields, precision=HIGH)
    all_parts = jnp.dot(mat_ref[...], moments, precision=HIGH)
    start = all_parts[:8]
    kappa, scale = relax_rows(rate)
    state = sweep_block((start, all_parts[8:16], all_parts[16:24]), scale, kappa)
    span_ref[0:8, :] = ratio * fields + (state - start)
    span_ref[8:16, :] = state
    part = STRIP_ROWS * LANES
    spot = pl.ds(pl.multiple_of(2 * part + side * part, part), part)
    change_ref[...] = stacked(span_ref[0:8, spot])
    state_ref[...] = span_ref[8:16, spot]


def macro(kernel, info, args, outs, scratch, name):
    vmem = pl.BlockSpec(memory_space=pltpu.VMEM)
    return pl.pallas_call(
        kernel,
        out_shape=outs,
        in_specs=[pl.BlockSpec(memory_space=pltpu.SMEM)] + [vmem] * len(args),
        out_specs=[vmem] * len(outs),
        scratch_shapes=scratch,
        compiler_params=params(),
        name=name,
        cost_estimate=pl.CostEstimate(flops=4000000, transcendentals=0, bytes_accessed=1000000),
    )(info, *args)


def finish_kernel(size, side_ref, near_ref, back_ref, table_ref, change_ref, *rest):
    out_ref = rest[-1]
    side = side_ref[0]
    lift = jnp.dot(table_ref[...], change_ref[...], preferred_element_type=F32)

    def write(ref, flipped):
        for row in range(STRIP_ROWS):
            index = jnp.where(side == flipped, 3 - row, row)
            out_ref[strided(row, size), :] = (
                ref[index] + lift[:, row * LANES : (row + 1) * LANES]
            )

    @pl.when(pl.program_id(0) == 0)
    def _():
        write(near_ref, 1)

    @pl.when(pl.program_id(0) == 1)
    def _():
        write(back_ref, 0)


def finish(side, out, near, back, table, change, half, chunk, first, size):
    steps = chunk // size
    shift = half // size
    begin = first // size

    def place(h, i, s):
        return jnp.where(h == 0, s[0], 1 - s[0]) * shift + begin + i

    specs = [
        pl.BlockSpec((4, size, LANES), lambda h, i, s: (0, jnp.where(h == 0, i, steps - 1), 0)),
        pl.BlockSpec((4, size, LANES), lambda h, i, s: (0, jnp.where(h == 0, 0, i), 0)),
        pl.BlockSpec((size, 48), lambda h, i, s: (place(h, i, s), 0)),
        pl.BlockSpec(change.shape, lambda h, i, s: (0, 0)),
    ]
    args = [side, near, back, table, change]
    aliases = {}
    if out is not None:
        specs.append(pl.BlockSpec(memory_space=pl.ANY))
        args.append(out)
        aliases = {5: 0}
    return pl.pallas_call(
        functools.partial(finish_kernel, size),
        out_shape=jax.ShapeDtypeStruct((2 * half * STRIP_ROWS, LANES), F32),
        grid_spec=pltpu.PrefetchScalarGridSpec(
            num_scalar_prefetch=1,
            grid=(2, steps),
            in_specs=specs,
            out_specs=pl.BlockSpec((4 * size, LANES), lambda h, i, s: (place(h, i, s), 0)),
        ),
        input_output_aliases=aliases,
        compiler_params=params(),
        name="finish",
        cost_estimate=pl.CostEstimate(
            flops=2 * 48 * 8 * LANES * chunk,
            transcendentals=0,
            bytes_accessed=chunk * LANES * 4 * 16,
        ),
    )(*args)


def per_device(points, dist, cell_type, collision_rate, vel_index):
    count, rows, cols = dist.shape
    half = count // 2
    strips = lax.axis_size("strip")
    groups = lax.axis_size("vel")
    strip = lax.axis_index("strip")
    size = 144
    pieces = next(k for k in (4, 3, 2, 1) if (half // size) % k == 0)
    chunk = half // pieces
    side = (strip % 2).astype(jnp.int32).reshape(1)
    info = jnp.stack([strip % 2, (strip // 2) % 2]).astype(jnp.int32)

    swap_pairs = [(s, s ^ 1) for s in range(strips)]
    down_pairs = [
        (s, s + (2 if s % 2 == 0 else -2))
        for s in range(strips)
        if 0 <= s + (2 if s % 2 == 0 else -2) < strips
    ]
    up_pairs = [(b, a) for a, b in down_pairs]
    pair_a = [
        (s, s + (2 if (s // 2) % 2 == 0 else -2))
        for s in range(strips)
        if 0 <= s + (2 if (s // 2) % 2 == 0 else -2) < strips
    ]
    pair_b = [
        (s, s + (-2 if (s // 2) % 2 == 0 else 2))
        for s in range(strips)
        if 0 <= s + (-2 if (s // 2) % 2 == 0 else 2) < strips
    ]

    def swap(value):
        return lax.ppermute(value, "strip", swap_pairs)

    def with_flow(value):
        return lax.ppermute(value, "strip", down_pairs)

    def against_flow(value):
        return lax.ppermute(value, "strip", up_pairs)

    def both_z(value):
        return lax.ppermute(value, "strip", pair_a), lax.ppermute(value, "strip", pair_b)

    def sum_groups(value):
        total = value
        for shift in range(1, groups):
            total = total + lax.ppermute(
                value, "vel", [(g, (g + shift) % groups) for g in range(groups)]
            )
        return total

    flat = dist.reshape(count * rows, cols)
    wall = (cell_type == 1).astype(F32)
    cell_pair = jnp.concatenate([collision_rate, wall])
    other_cells = swap(cell_pair)

    packed = [pack(side, flat, half, chunk, c * chunk, size) for c in range(pieces)]
    got = []
    for mid, edge, down in packed:
        edge_here = swap(edge)
        mid_here = swap(mid)
        got.append((mid_here, edge_here, with_flow(edge_here), against_flow(down)))

    comps = (vel_index.astype(F32) - (points - 1) / 2.0) * (8.0 / points)
    moment_table = jnp.pad(moment_rows(comps[0], comps[1], comps[2], (8.0 / points) ** 3, jnp), ((0, 3), (0, 0)))
    weight_high = rounded(moment_table)
    weight_low = rounded(moment_table - weight_high)
    weights = (
        jnp.concatenate([weight_high, weight_low])
        .astype(BF16)
        .reshape(32, count // size, size)
        .transpose(1, 0, 2)
    )
    shape_rows = state_rows(comps[0], comps[1], comps[2], jnp)
    part_a = rounded(shape_rows)
    part_b = rounded(shape_rows - part_a)
    part_c = rounded(shape_rows - part_a - part_b)
    table = jnp.concatenate([part_a, part_a, part_a, part_b, part_b, part_c]).astype(BF16).T
    zero = jnp.zeros_like(comps[0])
    const = jnp.stack(
        [
            STEP_RATIO * jnp.abs(comps[0]),
            STEP_RATIO * jnp.abs(comps[1]),
            jnp.where(comps[1] > 0, 0.5, -0.5),
            zero,
            zero,
            zero,
            zero,
            zero,
        ]
    ).T
    tables = (table, const, weights)
    gram = jnp.asarray(target_moments(points))
    mat = jnp.asarray(macro_matrix())

    def flow(own, other):
        odd = strip % 2 == 1
        return jnp.concatenate(
            [jnp.where(odd, own[::-1], own), jnp.where(odd, other[::-1], other)]
        )

    flow_rate = flow(collision_rate, other_cells[:rows])
    flow_fluid = 1.0 - flow(wall, other_cells[rows:])
    cells = jnp.concatenate([flow_fluid * (1.0 - flow_rate), flow_fluid])

    home = sum_groups(home_moments(flat, weights, size))
    home = jnp.concatenate(
        [home[:13], collision_rate.reshape(1, -1), wall.reshape(1, -1), jnp.zeros((1, rows * cols), F32)]
    )
    near_home = jnp.stack([home, *both_z(home)])
    far_home = swap(near_home)

    width = BLOCK_ROWS * LANES
    sums = jnp.zeros((16, width), F32)
    kept = []
    for c in range(pieces):
        mid_here, edge_here, above, below = got[c]
        first, middle, edge, sums = transport(
            side, [flat, mid_here, edge_here, above, below], tables, cells, sums,
            half, chunk, c * chunk, size,
        )
        kept.append((first, middle, edge, with_flow(edge), against_flow(first)))

    def exchange(value):
        value = sum_groups(value)
        value = value + swap(value)
        return value, both_z(value)

    own_sum, (sum_a, sum_b) = exchange(sums)
    change, keep = macro(
        first_macro_kernel, info,
        [own_sum, sum_a, sum_b, near_home, far_home, gram, mat],
        [
            jax.ShapeDtypeStruct((48, 11 * LANES), BF16),
            jax.ShapeDtypeStruct((16, SPAN * LANES), F32),
        ],
        [pltpu.VMEM((16, SPAN * LANES), F32)] * 2,
        "first_macro",
    )

    sums = jnp.zeros((16, width), F32)
    near, far = [], []
    for c in range(pieces):
        near_part, far_part, sums = transport(
            side, list(kept[c]), tables, cells, sums, half, chunk, c * chunk, size, change
        )
        near.append(near_part)
        far.append(far_part)
    back = [swap(part) for part in far[:-1]]
    own_sum, (sum_a, sum_b) = exchange(sums)
    last, own_sum = lax.optimization_barrier((far[-1], own_sum))
    back.append(swap(last))
    change, state = macro(
        second_macro_kernel, info,
        [own_sum, sum_a, sum_b, keep, gram, mat],
        [
            jax.ShapeDtypeStruct((48, STRIP_ROWS * LANES), BF16),
            jax.ShapeDtypeStruct((8, STRIP_ROWS * LANES), F32),
        ],
        [pltpu.VMEM((16, SPAN * LANES), F32)],
        "second_macro",
    )
    out = None
    for c in range(pieces):
        out = finish(side, out, near[c], back[c], table, change, half, chunk, c * chunk, size)
    return out.reshape(dist.shape), state[:5].reshape(5, rows, cols)


def solution(mesh):
    groups = mesh.shape["vel"]

    def whole(dist, cell_type, collision_rate, vel_index):
        points = round(vel_index.shape[1] ** (1.0 / 3.0))
        in_specs = (P("vel", "strip", None), P("strip", None), P("strip", None), P(None, "vel"))
        out_specs = (P("vel", "strip", None), P(None, "strip", None))
        return jax.shard_map(
            functools.partial(per_device, points),
            mesh=mesh,
            in_specs=in_specs,
            out_specs=out_specs,
            check_vma=False,
        )(dist, cell_type, collision_rate, vel_index)

    return whole
```

```python
import functools
import math

import jax
import jax.numpy as jnp
import numpy as np
from jax import lax
from jax.experimental import pallas as pl
from jax.experimental.pallas import tpu as pltpu
from jax.sharding import PartitionSpec as P


STEP_RATIO = 0.1
SOURCE_WEIGHT = 0.5
HEAT_WEIGHT = 4.0 / 15.0
SWEEPS = 3
HIGH = lax.Precision.HIGHEST
LANES = 128
STRIP_ROWS = 4
BLOCK_ROWS = 2 * STRIP_ROWS
SPAN = 3 * BLOCK_ROWS
GROUP = 16
BLOCK = 144
F32 = jnp.float32
BF16 = jnp.bfloat16


def params(**more):
    return pltpu.CompilerParams(vmem_limit_bytes=62 * 1024 * 1024, **more)


def chunk_blocks(blocks):
    if blocks % 12 == 0:
        unit = blocks // 12
        return [4 * unit, 4 * unit, 3 * unit, unit]
    return [1] * blocks if blocks < 4 else [blocks - blocks // 2, blocks // 2]


def moment_rows(vel_x, vel_y, vel_z, volume, lib):
    energy = vel_x * vel_x + vel_y * vel_y + vel_z * vel_z
    weight = volume * math.pi ** (-1.5) * lib.exp(-energy)
    rows = [
        lib.ones_like(vel_x),
        vel_x,
        vel_y,
        vel_z,
        energy,
        vel_x * vel_x,
        vel_y * vel_y,
        vel_x * vel_y,
        vel_x * vel_z,
        vel_y * vel_z,
        energy * vel_x,
        energy * vel_y,
        energy * vel_z,
    ]
    return lib.stack([row * weight for row in rows])


def state_rows(vel_x, vel_y, vel_z, lib):
    energy = vel_x * vel_x + vel_y * vel_y + vel_z * vel_z
    shape_heat = HEAT_WEIGHT * (energy - 2.5)
    rows = [
        lib.ones_like(vel_x),
        2.0 * vel_x,
        2.0 * vel_y,
        2.0 * vel_z,
        energy - 1.5,
        shape_heat * vel_x,
        shape_heat * vel_y,
        shape_heat * vel_z,
    ]
    return lib.stack(rows)


def target_moments(points):
    line = (np.arange(points) - (points - 1) / 2.0) * (8.0 / points)
    comps = [a.reshape(-1) for a in np.meshgrid(line, line, line, indexing="ij")]
    gram = moment_rows(*comps, (8.0 / points) ** 3, np) @ state_rows(*comps, np).T
    gram[np.abs(gram) < 1e-12] = 0.0
    full = np.zeros((16, 8), np.float32)
    full[:13] = gram
    return full


def macro_matrix():
    third = 2.0 / 3.0
    unit = np.eye(16, dtype=np.float64)
    start = [unit[0], unit[1], unit[2], unit[3], third * unit[4] - unit[0]]
    heat = [unit[10] - 2.5 * unit[1], unit[11] - 2.5 * unit[2], unit[12] - 2.5 * unit[3]]
    flux = [
        unit[1],
        unit[2],
        2.0 * unit[5] - third * unit[4],
        2.0 * unit[7],
        2.0 * unit[6] - third * unit[4],
        2.0 * unit[8],
        2.0 * unit[9],
        heat[0],
        heat[1],
    ]
    out = np.zeros((32, 16), np.float64)
    for row in range(5):
        out[row] = start[row]
        out[8 + row] = flux[(0, 2, 3, 5, 7)[row]]
        out[16 + row] = flux[(1, 3, 4, 6, 8)[row]]
    for row in range(3):
        out[24 + 5 + row] = heat[row]
    return out.astype(np.float32)


def minmod(left, right):
    low = jnp.minimum(left, right)
    high = jnp.maximum(left, right)
    return jnp.maximum(low, 0.0) + jnp.minimum(high, 0.0)


def strided(start, count):
    return pl.ds(start, count, stride=STRIP_ROWS)


def pack_kernel(size, side_ref, far_ref, own_ref, *rest):
    mid_ref, edge_ref, down_ref = rest[-3:]
    side = side_ref[0]
    for i in range(4):
        row = jnp.where(side == 1, i, 3 - i)
        part = far_ref[strided(row, size), :]
        if i < 2:
            mid_ref[i] = part
        else:
            edge_ref[i - 2] = part
    down_ref[...] = own_ref[strided(jnp.where(side == 1, 3, 0), size), :]


def pack(side, flat, half, chunk, first, size, earlier):
    steps = chunk // size
    shift = half // size
    begin = first // size
    return pl.pallas_call(
        functools.partial(pack_kernel, size),
        out_shape=(
            jax.ShapeDtypeStruct((2, chunk, LANES), F32),
            jax.ShapeDtypeStruct((2, chunk, LANES), F32),
            jax.ShapeDtypeStruct((chunk, LANES), F32),
        ),
        grid_spec=pltpu.PrefetchScalarGridSpec(
            num_scalar_prefetch=1,
            grid=(steps,),
            in_specs=[
                pl.BlockSpec((4 * size, LANES), lambda i, s: ((1 - s[0]) * shift + begin + i, 0)),
                pl.BlockSpec((4 * size, LANES), lambda i, s: (s[0] * shift + begin + i, 0)),
                *[pl.BlockSpec(memory_space=pl.ANY)] * len(earlier),
            ],
            out_specs=[
                pl.BlockSpec((2, size, LANES), lambda i, s: (0, i, 0)),
                pl.BlockSpec((2, size, LANES), lambda i, s: (0, i, 0)),
                pl.BlockSpec((size, LANES), lambda i, s: (i, 0)),
            ],
        ),
        compiler_params=params(),
        name="pack",
        cost_estimate=pl.CostEstimate(
            flops=0, transcendentals=0, bytes_accessed=chunk * LANES * 4 * 13
        ),
    )(side, flat, flat, *earlier)


def prepare_kernel(points, vel_ref, earlier_ref, table_ref, const_ref, weight_ref):
    comps = (vel_ref[0].astype(F32) - (points - 1) / 2.0) * (8.0 / points)
    vel_x, vel_y, vel_z = comps[0:1], comps[1:2], comps[2:3]
    moments = jnp.concatenate(
        [row[0] for row in moment_rows(vel_x, vel_y, vel_z, (8.0 / points) ** 3, jnp)[:, None]]
        + [jnp.zeros_like(vel_x)] * 3
    )
    high = moments.astype(BF16)
    weight_ref[0, 0:16] = high
    weight_ref[0, 16:32] = (moments - high.astype(F32)).astype(BF16)
    shapes = jnp.concatenate([row[0] for row in state_rows(vel_x, vel_y, vel_z, jnp)[:, None]])
    part_a = shapes.astype(BF16).astype(F32)
    part_b = (shapes - part_a).astype(BF16).astype(F32)
    part_c = shapes - part_a - part_b
    factors = jnp.concatenate(
        [
            STEP_RATIO * jnp.abs(vel_x),
            STEP_RATIO * jnp.abs(vel_y),
            jnp.where(vel_y > 0, 0.5, -0.5),
            jnp.zeros((13, vel_x.shape[1]), F32),
        ]
    )
    rows = jnp.concatenate([part_a, part_a, part_a, part_b, part_b, part_c, factors])
    columns = rows.T
    table_ref[...] = columns[:, :48].astype(BF16)
    const_ref[...] = columns[:, 48:56]


def prepare(points, vel_index, size, earlier):
    count = vel_index.shape[1]
    blocks = vel_index.reshape(3, count // size, size).transpose(1, 0, 2)
    return pl.pallas_call(
        functools.partial(prepare_kernel, points),
        out_shape=(
            jax.ShapeDtypeStruct((count, 48), BF16),
            jax.ShapeDtypeStruct((count, 8), F32),
            jax.ShapeDtypeStruct((count // size, 32, size), BF16),
        ),
        grid=(count // size,),
        in_specs=[
            pl.BlockSpec((1, 3, size), lambda i: (i, 0, 0)),
            pl.BlockSpec(memory_space=pl.ANY),
        ],
        out_specs=[
            pl.BlockSpec((size, 48), lambda i: (i, 0)),
            pl.BlockSpec((size, 8), lambda i: (i, 0)),
            pl.BlockSpec((1, 32, size), lambda i: (i, 0, 0)),
        ],
        compiler_params=params(),
        name="prepare",
        cost_estimate=pl.CostEstimate(
            flops=200 * count, transcendentals=count, bytes_accessed=count * 2000
        ),
    )(blocks, earlier)


def split_store(value, first_ref, second_ref, rows, columns):
    first = value.astype(BF16)
    first_ref[rows, columns] = first
    second_ref[rows, columns] = (value - first.astype(F32)).astype(BF16)


def weighted(weights, first, second):
    both = jnp.dot(weights, first, preferred_element_type=F32)
    return both[:16] + both[16:] + jnp.dot(weights[:16], second, preferred_element_type=F32)


def moment_kernel(size, dist_ref, weight_ref, out_ref, first_ref, second_ref):
    @pl.when(pl.program_id(0) == 0)
    def _():
        out_ref[...] = jnp.zeros_like(out_ref)

    for row in range(STRIP_ROWS):
        columns = pl.ds(row * LANES, LANES)
        split_store(
            dist_ref[strided(row, size), :], first_ref, second_ref, pl.ds(0, size), columns
        )
    out_ref[...] += weighted(weight_ref[0], first_ref[...], second_ref[...])


def home_moments(flat, weights, size):
    count = flat.shape[0] // STRIP_ROWS
    width = STRIP_ROWS * LANES
    return pl.pallas_call(
        functools.partial(moment_kernel, size),
        out_shape=jax.ShapeDtypeStruct((16, width), F32),
        grid=(count // size,),
        in_specs=[
            pl.BlockSpec((4 * size, LANES), lambda i: (i, 0)),
            pl.BlockSpec((1, 32, size), lambda i: (i, 0, 0)),
        ],
        out_specs=pl.BlockSpec((16, width), lambda i: (0, 0)),
        scratch_shapes=[pltpu.VMEM((size, width), BF16), pltpu.VMEM((size, width), BF16)],
        compiler_params=params(),
        name="home_moments",
        cost_estimate=pl.CostEstimate(
            flops=2 * 48 * count * width, transcendentals=0, bytes_accessed=count * width * 4
        ),
    )(flat, weights)


def transport_kernel(size, second_pass, side_ref, *refs):
    if second_pass:
        (table_ref, change_ref, q_first, q_mid, q_edge, up_ref, down_ref, *rest) = refs
    else:
        (own_ref, mid_ref, edge_ref, up_ref, down_ref, *rest) = refs
    (const_ref, weight_ref, cell_ref, sum_in_ref, *rest) = rest
    if second_pass:
        (near_out, far_out, sum_ref, first_ref, second_ref, lift_ref) = rest
    else:
        (first_out, mid_out, edge_out, sum_ref, first_ref, second_ref) = rest
    side = side_ref[0]

    @pl.when(pl.program_id(0) == 0)
    def _():
        sum_ref[...] = sum_in_ref[...]

    if second_pass:
        lift_ref[...] = jnp.dot(table_ref[...], change_ref[...], preferred_element_type=F32)

    lane = lax.broadcasted_iota(jnp.int32, (GROUP, LANES), 1)
    inner_low = jnp.where(lane == 0, 0.0, 1.0)
    inner_high = jnp.where(lane == LANES - 1, 0.0, 1.0)

    def body(group, carry):
        base = pl.multiple_of(group * GROUP, GROUP)
        rows = pl.ds(base, GROUP)

        def load(row):
            if row < 0:
                value = up_ref[row + 2, rows, :]
            elif row == 8:
                value = down_ref[rows, :]
            elif second_pass:
                if row == 0:
                    value = q_first[rows, :]
                elif row < 6:
                    value = q_mid[row - 1, rows, :]
                else:
                    value = q_edge[row - 6, rows, :]
            elif row < 4:
                value = own_ref[
                    strided(base * STRIP_ROWS + jnp.where(side == 1, 3 - row, row), GROUP), :
                ]
            elif row < 6:
                value = mid_ref[row - 4, rows, :]
            else:
                value = edge_ref[row - 6, rows, :]
            if second_pass:
                value = value + lift_ref[rows, pl.ds((row + 2) * LANES, LANES)]
            return value

        def wide(column):
            return jnp.broadcast_to(const_ref[rows, column : column + 1], (GROUP, LANES))

        speed_x = wide(0)
        speed_y = wide(1)
        half_sign = wide(2)
        forward = half_sign > 0.0
        open_end = jnp.where(forward, inner_low, inner_high)

        behind = load(-2)
        here = load(-1)
        ahead = load(0)
        step = ahead - here
        upwind = here + 0.5 * minmod(here - behind, step)
        here = ahead
        for row in range(BLOCK_ROWS):
            ahead = load(row + 1)
            next_step = ahead - here
            next_upwind = here + 0.5 * minmod(step, next_step)
            drift = speed_x * (next_upwind - upwind)
            step = next_step
            upwind = next_upwind
            left = here - pltpu.roll(here, 1, 1) * inner_low
            right = pltpu.roll(here, LANES - 1, 1) * inner_high - here
            face = here + half_sign * minmod(left, right)
            other = jnp.where(forward, pltpu.roll(face, 1, 1), pltpu.roll(face, LANES - 1, 1))
            drift = drift + speed_y * (face - other * open_end)
            keep = jnp.broadcast_to(cell_ref[row : row + 1, :], (GROUP, LANES))
            fluid = jnp.broadcast_to(cell_ref[row + 8 : row + 9, :], (GROUP, LANES))
            value = keep * here - fluid * drift
            split_store(value, first_ref, second_ref, rows, pl.ds(row * LANES, LANES))
            if second_pass:
                if row < 4:
                    near_out[row, rows, :] = value
                else:
                    far_out[row - 4, rows, :] = value
            elif row == 0:
                first_out[rows, :] = value
            elif row < 6:
                mid_out[row - 1, rows, :] = value
            else:
                edge_out[row - 6, rows, :] = value
            here = ahead
        return carry

    lax.fori_loop(0, size // GROUP, body, 0)
    part = weighted(weight_ref[0], first_ref[...], second_ref[...])
    for row in range(BLOCK_ROWS):
        place = jnp.where(side == 1, 7 - row, row)
        columns = pl.ds(pl.multiple_of(place * LANES, LANES), LANES)
        sum_ref[:, columns] += part[:, row * LANES : (row + 1) * LANES]


def transport(side, sources, tables, cells, sums, half, chunk, first, size, change=None):
    second_pass = change is not None
    steps = chunk // size
    shift = half // size
    begin = first // size
    table, const, weights = tables
    width = BLOCK_ROWS * LANES

    def mine(i, s):
        return s[0] * shift + begin + i

    two = pl.BlockSpec((2, size, LANES), lambda i, s: (0, i, 0))
    one = pl.BlockSpec((size, LANES), lambda i, s: (i, 0))
    if second_pass:
        args = [table, change]
        specs = [
            pl.BlockSpec((size, 48), lambda i, s: (mine(i, s), 0)),
            pl.BlockSpec(change.shape, lambda i, s: (0, 0)),
            one,
            pl.BlockSpec((5, size, LANES), lambda i, s: (0, i, 0)),
            two,
            two,
            one,
        ]
        four = pl.BlockSpec((4, size, LANES), lambda i, s: (0, i, 0))
        outs = [jax.ShapeDtypeStruct((4, chunk, LANES), F32)] * 2
        out_specs = [four, four]
        scratch = [pltpu.VMEM((size, 11 * LANES), F32)]
    else:
        args = []
        specs = [
            pl.BlockSpec((4 * size, LANES), lambda i, s: (mine(i, s), 0)),
            two,
            two,
            two,
            one,
        ]
        outs = [
            jax.ShapeDtypeStruct((chunk, LANES), F32),
            jax.ShapeDtypeStruct((5, chunk, LANES), F32),
            jax.ShapeDtypeStruct((2, chunk, LANES), F32),
        ]
        out_specs = [one, pl.BlockSpec((5, size, LANES), lambda i, s: (0, i, 0)), two]
        scratch = []
    whole = pl.BlockSpec((16, width), lambda i, s: (0, 0))
    return pl.pallas_call(
        functools.partial(transport_kernel, size, second_pass),
        out_shape=(*outs, jax.ShapeDtypeStruct((16, width), F32)),
        grid_spec=pltpu.PrefetchScalarGridSpec(
            num_scalar_prefetch=1,
            grid=(steps,),
            in_specs=[
                *specs,
                pl.BlockSpec((size, 8), lambda i, s: (mine(i, s), 0)),
                pl.BlockSpec((1, 32, size), lambda i, s: (mine(i, s), 0, 0)),
                pl.BlockSpec((16, LANES), lambda i, s: (0, 0)),
                whole,
            ],
            out_specs=[*out_specs, whole],
            scratch_shapes=[
                pltpu.VMEM((size, width), BF16),
                pltpu.VMEM((size, width), BF16),
                *scratch,
            ],
        ),
        compiler_params=params(),
        name="transport_second" if second_pass else "transport_first",
        cost_estimate=pl.CostEstimate(
            flops=60 * chunk * width, transcendentals=0, bytes_accessed=chunk * LANES * 4 * 19
        ),
    )(side, *args, *sources, const, weights, cells, sums)


def sweep_block(inputs, relax, rate):
    start, flux_x, flux_y = inputs
    lane = lax.broadcasted_iota(jnp.int32, (8, LANES), 1)
    inner_low = jnp.where(lane == 0, 0.0, 1.0)
    inner_high = jnp.where(lane == LANES - 1, 0.0, 1.0)

    def block(array, row):
        if row < 0 or row >= SPAN:
            return jnp.zeros((8, LANES), F32)
        return array[:, row * LANES : (row + 1) * LANES]

    def lower(value):
        return pltpu.roll(value, 1, 1) * inner_low

    def upper(value):
        return pltpu.roll(value, LANES - 1, 1) * inner_high

    source = []
    for row in range(SPAN):
        diff_x = 0.5 * (block(flux_x, row + 1) - block(flux_x, row - 1))
        side = block(flux_y, row)
        diff_y = 0.5 * (upper(side) - lower(side))
        source.append(block(start, row) - SOURCE_WEIGHT * (diff_x + diff_y))
    zero = jnp.zeros((8, LANES), F32)
    kappa = [block(rate, row) for row in range(SPAN)]
    scale = [block(relax, row) for row in range(SPAN)]
    state = [block(start, row) for row in range(SPAN)]
    for _ in range(SWEEPS):
        near = [zero, *state, zero]
        state = [
            (source[row] + kappa[row] * (near[row] + near[row + 2] + lower(near[row + 1]) + upper(near[row + 1])))
            * scale[row]
            for row in range(SPAN)
        ]
    return jnp.concatenate(state, axis=1)


def stacked(value):
    first = value.astype(BF16)
    rest = value - first.astype(F32)
    second = rest.astype(BF16)
    third = (rest - second.astype(F32)).astype(BF16)
    return jnp.concatenate([first, second, third, first, second, first], axis=0)


def relax_rows(rate):
    inside = rate > 0.0
    kappa = jnp.where(inside, 0.5 / jnp.where(inside, rate, 1.0), 0.0)
    scale = jnp.where(inside, 1.0 / (1.0 + 4.0 * kappa), 0.0)
    width = rate.shape[1]
    return jnp.broadcast_to(kappa, (8, width)), jnp.broadcast_to(scale, (8, width))


def place_blocks(info_ref, span_ref, own, pair_a, pair_b):
    odd = info_ref[1]
    width = BLOCK_ROWS * LANES
    span_ref[:, width : 2 * width] = own
    place_a = pl.multiple_of((1 - odd) * 2 * width, width)
    place_b = pl.multiple_of(odd * 2 * width, width)
    span_ref[:, pl.ds(place_a, width)] = pair_a
    span_ref[:, pl.ds(place_b, width)] = pair_b


def first_macro_kernel(
    info_ref, sum_ref, sum_a_ref, sum_b_ref, near_ref, far_ref, gram_ref, mat_ref,
    change_ref, keep_ref, span_ref, home_ref,
):
    side = info_ref[0]
    odd = info_ref[1]
    width = BLOCK_ROWS * LANES
    part = STRIP_ROWS * LANES
    place_blocks(info_ref, span_ref, sum_ref[...], sum_a_ref[...], sum_b_ref[...])
    for ref, where in ((near_ref, side), (far_ref, 1 - side)):
        for index, block in enumerate((1, (1 - odd) * 2, odd * 2)):
            spot = pl.multiple_of(block * width + where * part, part)
            home_ref[:, pl.ds(spot, part)] = ref[index]
    home = home_ref[...]
    rate = home[13:14, :]
    ratio = jnp.where(home[14:15, :] > 0.5, 1.0, rate)
    mat = mat_ref[...]
    first = jnp.dot(mat, jnp.where(lax.broadcasted_iota(jnp.int32, home.shape, 0) < 13, home, 0.0), precision=HIGH)
    fields = first[:8] + first[24:]
    moments = span_ref[...] + ratio * jnp.dot(gram_ref[...], fields, precision=HIGH)
    all_parts = jnp.dot(mat, moments, precision=HIGH)
    start = all_parts[:8]
    kappa, scale = relax_rows(rate)
    state = sweep_block((start, all_parts[8:16], all_parts[16:24]), scale, kappa)
    change = ratio * fields + (state - start)
    span_ref[0:8, :] = change
    keep_ref[0:8, :] = state + all_parts[24:]
    keep_ref[8:9, :] = rate
    keep_ref[9:10, :] = ratio
    keep_ref[10:16, :] = jnp.zeros((6, SPAN * LANES), F32)
    for row in range(-2, 9):
        spot = jnp.where(side == 1, 15 - row, 8 + row)
        piece = span_ref[0:8, pl.ds(pl.multiple_of(spot * LANES, LANES), LANES)]
        change_ref[:, (row + 2) * LANES : (row + 3) * LANES] = stacked(piece)


def second_macro_kernel(
    info_ref, sum_ref, sum_a_ref, sum_b_ref, keep_ref, gram_ref, mat_ref,
    change_ref, state_ref, span_ref,
):
    side = info_ref[0]
    place_blocks(info_ref, span_ref, sum_ref[...], sum_a_ref[...], sum_b_ref[...])
    fields = keep_ref[0:8, :]
    rate = keep_ref[8:9, :]
    ratio = keep_ref[9:10, :]
    moments = span_ref[...] + ratio * jnp.dot(gram_ref[...], fields, precision=HIGH)
    all_parts = jnp.dot(mat_ref[...], moments, precision=HIGH)
    start = all_parts[:8]
    kappa, scale = relax_rows(rate)
    state = sweep_block((start, all_parts[8:16], all_parts[16:24]), scale, kappa)
    span_ref[0:8, :] = ratio * fields + (state - start)
    span_ref[8:16, :] = state
    part = STRIP_ROWS * LANES
    spot = pl.ds(pl.multiple_of(2 * part + side * part, part), part)
    change_ref[...] = stacked(span_ref[0:8, spot])
    state_ref[...] = span_ref[8:16, spot]


def macro(kernel, info, args, outs, scratch):
    vmem = pl.BlockSpec(memory_space=pltpu.VMEM)
    return pl.pallas_call(
        kernel,
        out_shape=outs,
        in_specs=[pl.BlockSpec(memory_space=pltpu.SMEM)] + [vmem] * len(args),
        out_specs=[vmem] * len(outs),
        scratch_shapes=scratch,
        compiler_params=params(),
        cost_estimate=pl.CostEstimate(flops=4000000, transcendentals=0, bytes_accessed=1000000),
    )(info, *args)


def finish_kernel(size, side_ref, near_ref, back_ref, table_ref, change_ref, *rest):
    out_ref = rest[-1]
    side = side_ref[0]
    lift = jnp.dot(table_ref[...], change_ref[...], preferred_element_type=F32)

    def write(ref, flipped):
        for row in range(STRIP_ROWS):
            index = jnp.where(side == flipped, 3 - row, row)
            out_ref[strided(row, size), :] = (
                ref[index] + lift[:, row * LANES : (row + 1) * LANES]
            )

    @pl.when(pl.program_id(0) == 0)
    def _():
        write(near_ref, 1)

    @pl.when(pl.program_id(0) == 1)
    def _():
        write(back_ref, 0)


def finish(side, out, near, back, table, change, half, chunk, first, size):
    steps = chunk // size
    shift = half // size
    begin = first // size

    def place(h, i, s):
        return jnp.where(h == 0, s[0], 1 - s[0]) * shift + begin + i

    specs = [
        pl.BlockSpec((4, size, LANES), lambda h, i, s: (0, jnp.where(h == 0, i, steps - 1), 0)),
        pl.BlockSpec((4, size, LANES), lambda h, i, s: (0, jnp.where(h == 0, 0, i), 0)),
        pl.BlockSpec((size, 48), lambda h, i, s: (place(h, i, s), 0)),
        pl.BlockSpec(change.shape, lambda h, i, s: (0, 0)),
    ]
    args = [side, near, back, table, change]
    aliases = {}
    if out is not None:
        specs.append(pl.BlockSpec(memory_space=pl.ANY))
        args.append(out)
        aliases = {5: 0}
    return pl.pallas_call(
        functools.partial(finish_kernel, size),
        out_shape=jax.ShapeDtypeStruct((2 * half * STRIP_ROWS, LANES), F32),
        grid_spec=pltpu.PrefetchScalarGridSpec(
            num_scalar_prefetch=1,
            grid=(2, steps),
            in_specs=specs,
            out_specs=pl.BlockSpec((4 * size, LANES), lambda h, i, s: (place(h, i, s), 0)),
        ),
        input_output_aliases=aliases,
        compiler_params=params(),
        name="finish",
        cost_estimate=pl.CostEstimate(
            flops=2 * 48 * 8 * LANES * chunk,
            transcendentals=0,
            bytes_accessed=chunk * LANES * 4 * 16,
        ),
    )(*args)


def per_device(points, dist, cell_type, collision_rate, vel_index):
    count, rows, cols = dist.shape
    half = count // 2
    strips = lax.axis_size("strip")
    groups = lax.axis_size("vel")
    strip = lax.axis_index("strip")
    size = BLOCK
    chunks = [size * n for n in chunk_blocks(half // size)]
    firsts = [sum(chunks[:c]) for c in range(len(chunks))]
    order = range(len(chunks))
    side = (strip % 2).astype(jnp.int32).reshape(1)
    info = jnp.stack([strip % 2, (strip // 2) % 2]).astype(jnp.int32)

    swap_pairs = [(s, s ^ 1) for s in range(strips)]
    down_pairs = [
        (s, s + (2 if s % 2 == 0 else -2))
        for s in range(strips)
        if 0 <= s + (2 if s % 2 == 0 else -2) < strips
    ]
    up_pairs = [(b, a) for a, b in down_pairs]
    pair_a = [
        (s, s + (2 if (s // 2) % 2 == 0 else -2))
        for s in range(strips)
        if 0 <= s + (2 if (s // 2) % 2 == 0 else -2) < strips
    ]
    pair_b = [
        (s, s + (-2 if (s // 2) % 2 == 0 else 2))
        for s in range(strips)
        if 0 <= s + (-2 if (s // 2) % 2 == 0 else 2) < strips
    ]

    def swap(value):
        return lax.ppermute(value, "strip", swap_pairs)

    def with_flow(value):
        return lax.ppermute(value, "strip", down_pairs)

    def against_flow(value):
        return lax.ppermute(value, "strip", up_pairs)

    def both_z(value):
        return lax.ppermute(value, "strip", pair_a), lax.ppermute(value, "strip", pair_b)

    def sum_groups(value):
        total = value
        for shift in range(1, groups):
            total = total + lax.ppermute(
                value, "vel", [(g, (g + shift) % groups) for g in range(groups)]
            )
        return total

    flat = dist.reshape(count * rows, cols)
    wall = (cell_type == 1).astype(F32)
    cell_pair = jnp.concatenate([collision_rate, wall])
    other_cells = swap(cell_pair)

    got = []
    earlier = []
    for c in order:
        mid, edge, down = pack(side, flat, half, chunks[c], firsts[c], size, earlier)
        earlier = [down]
        edge_here = swap(edge)
        mid_here = swap(mid)
        below = against_flow(down)
        got.append((edge_here, mid_here, below))

    tables = prepare(points, vel_index, size, earlier[0])
    table, _, weights = tables
    gram = jnp.asarray(target_moments(points))
    mat = jnp.asarray(macro_matrix())

    def flow(own, other):
        odd = strip % 2 == 1
        return jnp.concatenate(
            [jnp.where(odd, own[::-1], own), jnp.where(odd, other[::-1], other)]
        )

    flow_rate = flow(collision_rate, other_cells[:rows])
    flow_fluid = 1.0 - flow(wall, other_cells[rows:])
    cells = jnp.concatenate([flow_fluid * (1.0 - flow_rate), flow_fluid])

    home = sum_groups(home_moments(flat, weights, size))
    home = jnp.concatenate(
        [home[:13], collision_rate.reshape(1, -1), wall.reshape(1, -1), jnp.zeros((1, rows * cols), F32)]
    )
    near_home = jnp.stack([home, *both_z(home)])
    far_home = swap(near_home)

    width = BLOCK_ROWS * LANES
    sums = jnp.zeros((16, width), F32)
    kept = []
    for c in order:
        edge_here, mid_here, below = got[c]
        above = with_flow(edge_here)
        first, middle, edge, sums = transport(
            side, [flat, mid_here, edge_here, above, below],
            tables, cells, sums, half, chunks[c], firsts[c], size,
        )
        above = with_flow(edge)
        below = against_flow(first)
        kept.append((first, middle, edge, above, below))

    total = sum_groups(sums)
    total = total + swap(total)
    sum_a, sum_b = both_z(total)
    change, keep = macro(
        first_macro_kernel, info,
        [total, sum_a, sum_b, near_home, far_home, gram, mat],
        [
            jax.ShapeDtypeStruct((48, 11 * LANES), BF16),
            jax.ShapeDtypeStruct((16, SPAN * LANES), F32),
        ],
        [pltpu.VMEM((16, SPAN * LANES), F32)] * 2,
    )

    sums = jnp.zeros((16, width), F32)
    near, far, back = {}, {}, {}
    for c in reversed(order):
        near[c], far[c], sums = transport(
            side, list(kept[c]), tables, cells, sums, half, chunks[c], firsts[c], size, change
        )
        back[c] = swap(far[c])
    total = sum_groups(sums)
    total = total + swap(total)
    sum_a, sum_b = both_z(total)
    change, state = macro(
        second_macro_kernel, info,
        [total, sum_a, sum_b, keep, gram, mat],
        [
            jax.ShapeDtypeStruct((48, STRIP_ROWS * LANES), BF16),
            jax.ShapeDtypeStruct((8, STRIP_ROWS * LANES), F32),
        ],
        [pltpu.VMEM((16, SPAN * LANES), F32)],
    )
    out = None
    for c in reversed(order):
        out = finish(side, out, near[c], back[c], table, change, half, chunks[c], firsts[c], size)
    return out.reshape(dist.shape), state[:5].reshape(5, rows, cols)


def solution(mesh):
    def whole(dist, cell_type, collision_rate, vel_index):
        points = round(vel_index.shape[1] ** (1.0 / 3.0))
        in_specs = (P("vel", "strip", None), P("strip", None), P("strip", None), P(None, "vel"))
        out_specs = (P("vel", "strip", None), P(None, "strip", None))

        def body(*args):
            return per_device(points, *args)

        run = jax.shard_map(
            body, mesh=mesh, in_specs=in_specs, out_specs=out_specs, check_vma=False
        )
        return run(dist, cell_type, collision_rate, vel_index)

    return whole
```

```python
import functools
import math

import jax
import jax.numpy as jnp
import numpy as np
from jax import lax
from jax.experimental import pallas as pl
from jax.experimental.pallas import tpu as pltpu
from jax.sharding import PartitionSpec as P


STEP_RATIO = 0.1
SOURCE_WEIGHT = 0.5
HEAT_WEIGHT = 4.0 / 15.0
SWEEPS = 3
HIGH = lax.Precision.HIGHEST
LANES = 128
STRIP_ROWS = 4
BLOCK_ROWS = 2 * STRIP_ROWS
SPAN = 3 * BLOCK_ROWS
GROUP = 16
F32 = jnp.float32
BF16 = jnp.bfloat16


def params(**more):
    return pltpu.CompilerParams(vmem_limit_bytes=62 * 1024 * 1024, **more)


def plan(half):
    block = 288 if half % 288 == 0 else 144
    blocks = half // block
    if blocks % 6 == 0:
        unit = block * (blocks // 6)
        return block, [unit, 2 * unit, 2 * unit, unit]
    return block, [block * (blocks - 2), block, block]


def moment_rows(vel_x, vel_y, vel_z, volume, lib):
    energy = vel_x * vel_x + vel_y * vel_y + vel_z * vel_z
    weight = volume * math.pi ** (-1.5) * lib.exp(-energy)
    rows = [
        lib.ones_like(vel_x),
        vel_x,
        vel_y,
        vel_z,
        energy,
        vel_x * vel_x,
        vel_y * vel_y,
        vel_x * vel_y,
        vel_x * vel_z,
        vel_y * vel_z,
        energy * vel_x,
        energy * vel_y,
        energy * vel_z,
    ]
    return lib.concatenate([(row * weight).reshape(1, -1) for row in rows])


def state_rows(vel_x, vel_y, vel_z, lib):
    energy = vel_x * vel_x + vel_y * vel_y + vel_z * vel_z
    shape_heat = HEAT_WEIGHT * (energy - 2.5)
    rows = [
        lib.ones_like(vel_x),
        2.0 * vel_x,
        2.0 * vel_y,
        2.0 * vel_z,
        energy - 1.5,
        shape_heat * vel_x,
        shape_heat * vel_y,
        shape_heat * vel_z,
    ]
    return lib.concatenate([row.reshape(1, -1) for row in rows])


def target_moments(points):
    line = (np.arange(points) - (points - 1) / 2.0) * (8.0 / points)
    comps = [a.reshape(-1) for a in np.meshgrid(line, line, line, indexing="ij")]
    gram = moment_rows(*comps, (8.0 / points) ** 3, np) @ state_rows(*comps, np).T
    gram[np.abs(gram) < 1e-12] = 0.0
    full = np.zeros((16, 8), np.float32)
    full[:13] = gram
    return full


def macro_matrix():
    third = 2.0 / 3.0
    unit = np.eye(16, dtype=np.float64)
    start = [unit[0], unit[1], unit[2], unit[3], third * unit[4] - unit[0]]
    heat = [unit[10] - 2.5 * unit[1], unit[11] - 2.5 * unit[2], unit[12] - 2.5 * unit[3]]
    flux = [
        unit[1],
        unit[2],
        2.0 * unit[5] - third * unit[4],
        2.0 * unit[7],
        2.0 * unit[6] - third * unit[4],
        2.0 * unit[8],
        2.0 * unit[9],
        heat[0],
        heat[1],
    ]
    out = np.zeros((32, 16), np.float64)
    for row in range(5):
        out[row] = start[row]
        out[8 + row] = flux[(0, 2, 3, 5, 7)[row]]
        out[16 + row] = flux[(1, 3, 4, 6, 8)[row]]
    for row in range(3):
        out[24 + 5 + row] = heat[row]
    return out.astype(np.float32)


def minmod(left, right):
    return jnp.maximum(jnp.minimum(right, jnp.maximum(left, 0.0)), jnp.minimum(left, 0.0))


def strided(start, count):
    return pl.ds(start, count, stride=STRIP_ROWS)


def pick_kernel(size, picks, side_ref, strip_ref, *rest):
    out_ref = rest[-1]
    side = side_ref[0]
    for index, (even, odd) in enumerate(picks):
        out_ref[index] = strip_ref[strided(jnp.where(side == 1, odd, even), size), :]


def pick(side, flat, start, count, size, picks, earlier=()):
    return pl.pallas_call(
        functools.partial(pick_kernel, size, picks),
        out_shape=jax.ShapeDtypeStruct((len(picks), count, LANES), F32),
        grid_spec=pltpu.PrefetchScalarGridSpec(
            num_scalar_prefetch=1,
            grid=(count // size,),
            in_specs=[
                pl.BlockSpec((4 * size, LANES), lambda i, s: (start(s[0]) + i, 0)),
                *[pl.BlockSpec(memory_space=pl.ANY)] * len(earlier),
            ],
            out_specs=pl.BlockSpec((len(picks), size, LANES), lambda i, s: (0, i, 0)),
        ),
        compiler_params=params(),
        cost_estimate=pl.CostEstimate(
            flops=0, transcendentals=0, bytes_accessed=count * LANES * 4 * (4 + len(picks))
        ),
    )(side, flat, *earlier)


def prepare_kernel(points, vel_ref, table_ref, const_ref, weight_ref):
    comps = (vel_ref[...].astype(F32) - (points - 1) / 2.0) * (8.0 / points)
    vel_x, vel_y, vel_z = comps[0:1], comps[1:2], comps[2:3]
    moments = moment_rows(vel_x, vel_y, vel_z, (8.0 / points) ** 3, jnp)
    high = moments.astype(BF16).astype(F32)
    shapes = state_rows(vel_x, vel_y, vel_z, jnp)
    part_a = shapes.astype(BF16).astype(F32)
    part_b = (shapes - part_a).astype(BF16).astype(F32)
    part_c = shapes - part_a - part_b
    width = vel_x.shape[1]
    rows = jnp.concatenate(
        [
            *[part_a] * 3,
            *[part_b] * 2,
            part_c,
            high,
            jnp.zeros((3, width), F32),
            moments - high,
            jnp.zeros((3, width), F32),
            STEP_RATIO * jnp.abs(vel_x),
            STEP_RATIO * jnp.abs(vel_y),
            jnp.where(vel_y > 0, 0.5, -0.5),
            jnp.zeros((45, width), F32),
        ]
    )
    columns = rows.T
    table_ref[...] = columns[:, :48].astype(BF16)
    weight_ref[...] = columns[:, 48:80].astype(BF16)
    const_ref[...] = columns[:, 80:88]


def prepare(points, vel_index):
    count = vel_index.shape[1]
    vmem = pl.BlockSpec(memory_space=pltpu.VMEM)
    return pl.pallas_call(
        functools.partial(prepare_kernel, points),
        out_shape=(
            jax.ShapeDtypeStruct((count, 48), BF16),
            jax.ShapeDtypeStruct((count, 8), F32),
            jax.ShapeDtypeStruct((count, 32), BF16),
        ),
        in_specs=[vmem],
        out_specs=[vmem] * 3,
        compiler_params=params(),
        name="prepare",
        cost_estimate=pl.CostEstimate(
            flops=200 * count, transcendentals=count, bytes_accessed=count * 1000
        ),
    )(vel_index)


def split_store(value, first_ref, second_ref, rows, columns):
    first = value.astype(BF16)
    first_ref[rows, columns] = first
    second_ref[rows, columns] = (value - first.astype(F32)).astype(BF16)


def weighted(weights, first, second):
    over_rows = (((0,), (0,)), ((), ()))
    both = lax.dot_general(weights, first, over_rows, preferred_element_type=F32)
    rest = lax.dot_general(weights, second, over_rows, preferred_element_type=F32)
    return both[:16] + both[16:] + rest[:16]


def moment_kernel(size, dist_ref, weight_ref, out_ref, first_ref, second_ref):
    @pl.when(pl.program_id(0) == 0)
    def _():
        out_ref[...] = jnp.zeros_like(out_ref)

    for row in range(STRIP_ROWS):
        columns = pl.ds(row * LANES, LANES)
        split_store(
            dist_ref[strided(row, size), :], first_ref, second_ref, pl.ds(0, size), columns
        )
    out_ref[...] += weighted(weight_ref[...], first_ref[...], second_ref[...])


def home_moments(flat, weights, size):
    count = flat.shape[0] // STRIP_ROWS
    width = STRIP_ROWS * LANES
    return pl.pallas_call(
        functools.partial(moment_kernel, size),
        out_shape=jax.ShapeDtypeStruct((16, width), F32),
        grid=(count // size,),
        in_specs=[
            pl.BlockSpec((4 * size, LANES), lambda i: (i, 0)),
            pl.BlockSpec((size, 32), lambda i: (i, 0)),
        ],
        out_specs=pl.BlockSpec((16, width), lambda i: (0, 0)),
        scratch_shapes=[pltpu.VMEM((size, width), BF16), pltpu.VMEM((size, width), BF16)],
        compiler_params=params(),
        name="home_moments",
        cost_estimate=pl.CostEstimate(
            flops=2 * 48 * count * width, transcendentals=0, bytes_accessed=count * width * 4
        ),
    )(flat, weights)


def transport_kernel(size, second_pass, side_ref, *refs):
    if second_pass:
        (table_ref, change_ref, q_first, q_mid, q_edge, up_ref, down_ref, *rest) = refs
    else:
        (own_ref, got_ref, up_ref, down_ref, *rest) = refs
    (const_ref, weight_ref, cell_ref, sum_in_ref, *rest) = rest
    if second_pass:
        (near_out, far_out, sum_ref, first_ref, second_ref, lift_ref) = rest
    else:
        (first_out, mid_out, edge_out, sum_ref, first_ref, second_ref) = rest[-6:]
    side = side_ref[0]

    @pl.when(pl.program_id(0) == 0)
    def _():
        sum_ref[...] = sum_in_ref[...]

    if second_pass:
        lift_ref[...] = jnp.dot(table_ref[...], change_ref[...], preferred_element_type=F32)

    lane = lax.broadcasted_iota(jnp.int32, (GROUP, LANES), 1)
    inner_low = jnp.where(lane == 0, 0.0, 1.0)
    inner_high = jnp.where(lane == LANES - 1, 0.0, 1.0)

    def body(group, carry):
        base = pl.multiple_of(group * GROUP, GROUP)
        rows = pl.ds(base, GROUP)

        def load(row):
            if row < 0:
                value = up_ref[row + 2, rows, :]
            elif row == 8:
                value = down_ref[rows, :]
            elif second_pass:
                if row == 0:
                    value = q_first[rows, :]
                elif row < 6:
                    value = q_mid[row - 1, rows, :]
                else:
                    value = q_edge[row - 6, rows, :]
            else:
                ref = own_ref if row < 4 else got_ref
                local = jnp.where(side == 1, 3 - row % 4, row % 4)
                value = ref[strided(base * STRIP_ROWS + local, GROUP), :]
            if second_pass:
                value = value + lift_ref[rows, pl.ds((row + 2) * LANES, LANES)]
            return value

        def wide(column):
            return jnp.broadcast_to(const_ref[rows, column : column + 1], (GROUP, LANES))

        speed_x = wide(0)
        speed_y = wide(1)
        half_sign = wide(2)
        forward = half_sign > 0.0
        open_end = jnp.where(forward, inner_low, inner_high)

        behind = load(-2)
        here = load(-1)
        ahead = load(0)
        step = ahead - here
        upwind = here + 0.5 * minmod(here - behind, step)
        here = ahead
        for row in range(BLOCK_ROWS):
            ahead = load(row + 1)
            next_step = ahead - here
            next_upwind = here + 0.5 * minmod(step, next_step)
            drift = speed_x * (next_upwind - upwind)
            step = next_step
            upwind = next_upwind
            left = here - pltpu.roll(here, 1, 1) * inner_low
            right = pltpu.roll(here, LANES - 1, 1) * inner_high - here
            face = here + half_sign * minmod(left, right)
            other = jnp.where(forward, pltpu.roll(face, 1, 1), pltpu.roll(face, LANES - 1, 1))
            drift = drift + speed_y * (face - other * open_end)
            keep = jnp.broadcast_to(cell_ref[row : row + 1, :], (GROUP, LANES))
            fluid = jnp.broadcast_to(cell_ref[row + 8 : row + 9, :], (GROUP, LANES))
            value = keep * here - fluid * drift
            split_store(value, first_ref, second_ref, rows, pl.ds(row * LANES, LANES))
            if second_pass:
                if row < 4:
                    near_out[row, rows, :] = value
                else:
                    far_out[row - 4, rows, :] = value
            elif row == 0:
                first_out[rows, :] = value
            elif row < 6:
                mid_out[row - 1, rows, :] = value
            else:
                edge_out[row - 6, rows, :] = value
            here = ahead
        return carry

    lax.fori_loop(0, size // GROUP, body, 0)
    part = weighted(weight_ref[...], first_ref[...], second_ref[...])
    for row in range(BLOCK_ROWS):
        place = jnp.where(side == 1, 7 - row, row)
        columns = pl.ds(pl.multiple_of(place * LANES, LANES), LANES)
        sum_ref[:, columns] += part[:, row * LANES : (row + 1) * LANES]


def transport(
    side, sources, tables, cells, sums, half, chunk, first, size, change=None, skip=0, group=None, into=None
):
    second_pass = change is not None
    steps = chunk // size
    shift = half // size
    begin = first // size
    offset = skip // size
    table, const, weights = tables
    width = BLOCK_ROWS * LANES

    def mine(i, s):
        return s[0] * shift + begin + i

    def stack_of(count, at):
        return pl.BlockSpec((count, size, LANES), lambda i, s: (0, at + i, 0))

    aliases = {}
    if second_pass:
        args = [table, change]
        specs = [
            pl.BlockSpec((size, 48), lambda i, s: (mine(i, s), 0)),
            pl.BlockSpec(change.shape, lambda i, s: (0, 0)),
            stack_of(None, offset),
            stack_of(5, offset),
            stack_of(2, offset),
            stack_of(2, offset),
            stack_of(None, offset),
        ]
        outs = [jax.ShapeDtypeStruct((4, chunk, LANES), F32)] * 2
        out_specs = [stack_of(4, 0)] * 2
        scratch = [pltpu.VMEM((size, 11 * LANES), F32)]
    else:
        args = []
        specs = [
            pl.BlockSpec((4 * size, LANES), lambda i, s: (mine(i, s), 0)),
            pl.BlockSpec((4 * size, LANES), lambda i, s: (i, 0)),
            stack_of(2, 0),
            stack_of(None, begin),
        ]
        outs = [jax.ShapeDtypeStruct((n, group, LANES), F32) for n in (1, 5, 2)]
        out_specs = [stack_of(None, offset), stack_of(5, offset), stack_of(2, offset)]
        scratch = []
    whole = pl.BlockSpec((16, width), lambda i, s: (0, 0))
    args = [side, *args, *sources, const, weights, cells, sums]
    specs = [
        *specs,
        pl.BlockSpec((size, 8), lambda i, s: (mine(i, s), 0)),
        pl.BlockSpec((size, 32), lambda i, s: (mine(i, s), 0)),
        pl.BlockSpec((16, LANES), lambda i, s: (0, 0)),
        whole,
    ]
    if into is not None:
        aliases = {len(args) + n: n for n in range(3)}
        args = [*args, *into]
        specs = [*specs, *[pl.BlockSpec(memory_space=pl.ANY)] * 3]
    return pl.pallas_call(
        functools.partial(transport_kernel, size, second_pass),
        out_shape=(*outs, jax.ShapeDtypeStruct((16, width), F32)),
        grid_spec=pltpu.PrefetchScalarGridSpec(
            num_scalar_prefetch=1,
            grid=(steps,),
            in_specs=specs,
            out_specs=[*out_specs, whole],
            scratch_shapes=[
                pltpu.VMEM((size, width), BF16),
                pltpu.VMEM((size, width), BF16),
                *scratch,
            ],
        ),
        input_output_aliases=aliases,
        compiler_params=params(),
        name="transport_second" if second_pass else "transport_first",
        cost_estimate=pl.CostEstimate(
            flops=60 * chunk * width, transcendentals=0, bytes_accessed=chunk * LANES * 4 * 19
        ),
    )(*args)


def sweep_block(inputs, relax, rate):
    start, flux_x, flux_y = inputs
    lane = lax.broadcasted_iota(jnp.int32, (8, LANES), 1)
    inner_low = jnp.where(lane == 0, 0.0, 1.0)
    inner_high = jnp.where(lane == LANES - 1, 0.0, 1.0)

    def block(array, row):
        if row < 0 or row >= SPAN:
            return jnp.zeros((8, LANES), F32)
        return array[:, row * LANES : (row + 1) * LANES]

    def lower(value):
        return pltpu.roll(value, 1, 1) * inner_low

    def upper(value):
        return pltpu.roll(value, LANES - 1, 1) * inner_high

    source = []
    for row in range(SPAN):
        diff_x = 0.5 * (block(flux_x, row + 1) - block(flux_x, row - 1))
        side = block(flux_y, row)
        diff_y = 0.5 * (upper(side) - lower(side))
        source.append(block(start, row) - SOURCE_WEIGHT * (diff_x + diff_y))
    zero = jnp.zeros((8, LANES), F32)
    kappa = [block(rate, row) for row in range(SPAN)]
    scale = [block(relax, row) for row in range(SPAN)]
    state = [block(start, row) for row in range(SPAN)]
    for _ in range(SWEEPS):
        near = [zero, *state, zero]
        state = [
            (source[row] + kappa[row] * (near[row] + near[row + 2] + lower(near[row + 1]) + upper(near[row + 1])))
            * scale[row]
            for row in range(SPAN)
        ]
    return jnp.concatenate(state, axis=1)


def stacked(value):
    first = value.astype(BF16)
    rest = value - first.astype(F32)
    second = rest.astype(BF16)
    third = (rest - second.astype(F32)).astype(BF16)
    return jnp.concatenate([first, second, third, first, second, first], axis=0)


def relax_rows(rate):
    inside = rate > 0.0
    kappa = jnp.where(inside, 0.5 / jnp.where(inside, rate, 1.0), 0.0)
    scale = jnp.where(inside, 1.0 / (1.0 + 4.0 * kappa), 0.0)
    width = rate.shape[1]
    return jnp.broadcast_to(kappa, (8, width)), jnp.broadcast_to(scale, (8, width))


def place_blocks(info_ref, span_ref, own, pair_a, pair_b):
    odd = info_ref[1]
    width = BLOCK_ROWS * LANES
    span_ref[:, width : 2 * width] = own
    place_a = pl.multiple_of((1 - odd) * 2 * width, width)
    place_b = pl.multiple_of(odd * 2 * width, width)
    span_ref[:, pl.ds(place_a, width)] = pair_a
    span_ref[:, pl.ds(place_b, width)] = pair_b


def first_macro_kernel(
    info_ref, sum_ref, sum_a_ref, sum_b_ref, near_ref, far_ref, gram_ref, mat_ref,
    change_ref, keep_ref, span_ref, home_ref,
):
    side = info_ref[0]
    odd = info_ref[1]
    width = BLOCK_ROWS * LANES
    part = STRIP_ROWS * LANES
    place_blocks(info_ref, span_ref, sum_ref[...], sum_a_ref[...], sum_b_ref[...])
    for ref, where in ((near_ref, side), (far_ref, 1 - side)):
        for index, block in enumerate((1, (1 - odd) * 2, odd * 2)):
            spot = pl.multiple_of(block * width + where * part, part)
            home_ref[:, pl.ds(spot, part)] = ref[index]
    home = home_ref[...]
    rate = home[13:14, :]
    ratio = jnp.where(home[14:15, :] > 0.5, 1.0, rate)
    mat = mat_ref[...]
    first = jnp.dot(mat, jnp.where(lax.broadcasted_iota(jnp.int32, home.shape, 0) < 13, home, 0.0), precision=HIGH)
    fields = first[:8] + first[24:]
    moments = span_ref[...] + ratio * jnp.dot(gram_ref[...], fields, precision=HIGH)
    all_parts = jnp.dot(mat, moments, precision=HIGH)
    start = all_parts[:8]
    kappa, scale = relax_rows(rate)
    state = sweep_block((start, all_parts[8:16], all_parts[16:24]), scale, kappa)
    change = ratio * fields + (state - start)
    span_ref[0:8, :] = change
    keep_ref[0:8, :] = state + all_parts[24:]
    keep_ref[8:9, :] = rate
    keep_ref[9:10, :] = ratio
    keep_ref[10:16, :] = jnp.zeros((6, SPAN * LANES), F32)
    for row in range(-2, 9):
        spot = jnp.where(side == 1, 15 - row, 8 + row)
        piece = span_ref[0:8, pl.ds(pl.multiple_of(spot * LANES, LANES), LANES)]
        change_ref[:, (row + 2) * LANES : (row + 3) * LANES] = stacked(piece)


def second_macro_kernel(
    info_ref, sum_ref, sum_a_ref, sum_b_ref, keep_ref, gram_ref, mat_ref,
    change_ref, state_ref, span_ref,
):
    side = info_ref[0]
    place_blocks(info_ref, span_ref, sum_ref[...], sum_a_ref[...], sum_b_ref[...])
    fields = keep_ref[0:8, :]
    rate = keep_ref[8:9, :]
    ratio = keep_ref[9:10, :]
    moments = span_ref[...] + ratio * jnp.dot(gram_ref[...], fields, precision=HIGH)
    all_parts = jnp.dot(mat_ref[...], moments, precision=HIGH)
    start = all_parts[:8]
    kappa, scale = relax_rows(rate)
    state = sweep_block((start, all_parts[8:16], all_parts[16:24]), scale, kappa)
    span_ref[0:8, :] = ratio * fields + (state - start)
    span_ref[8:16, :] = state
    part = STRIP_ROWS * LANES
    spot = pl.ds(pl.multiple_of(2 * part + side * part, part), part)
    change_ref[...] = stacked(span_ref[0:8, spot])
    state_ref[...] = span_ref[8:16, spot]


def macro(kernel, info, args, outs, scratch):
    vmem = pl.BlockSpec(memory_space=pltpu.VMEM)
    return pl.pallas_call(
        kernel,
        out_shape=outs,
        in_specs=[pl.BlockSpec(memory_space=pltpu.SMEM)] + [vmem] * len(args),
        out_specs=[vmem] * len(outs),
        scratch_shapes=scratch,
        compiler_params=params(),
        cost_estimate=pl.CostEstimate(flops=4000000, transcendentals=0, bytes_accessed=1000000),
    )(info, *args)


def finish_kernel(size, own, side_ref, rows_ref, table_ref, change_ref, *rest):
    out_ref = rest[-1]
    flipped = side_ref[0] == (1 if own else 0)
    lift = jnp.dot(table_ref[...], change_ref[...], preferred_element_type=F32)
    for row in range(STRIP_ROWS):
        index = jnp.where(flipped, 3 - row, row)
        out_ref[strided(row, size), :] = (
            rows_ref[index] + lift[:, row * LANES : (row + 1) * LANES]
        )


def finish(side, out, rows, own, table, change, half, chunk, first, size):
    shift = half // size
    begin = first // size

    def place(i, s):
        return (s[0] if own else 1 - s[0]) * shift + begin + i

    specs = [
        pl.BlockSpec((4, size, LANES), lambda i, s: (0, i, 0)),
        pl.BlockSpec((size, 48), lambda i, s: (place(i, s), 0)),
        pl.BlockSpec(change.shape, lambda i, s: (0, 0)),
    ]
    args = [side, rows, table, change]
    aliases = {}
    if out is not None:
        specs.append(pl.BlockSpec(memory_space=pl.ANY))
        args.append(out)
        aliases = {4: 0}
    return pl.pallas_call(
        functools.partial(finish_kernel, size, own),
        out_shape=jax.ShapeDtypeStruct((2 * half * STRIP_ROWS, LANES), F32),
        grid_spec=pltpu.PrefetchScalarGridSpec(
            num_scalar_prefetch=1,
            grid=(chunk // size,),
            in_specs=specs,
            out_specs=pl.BlockSpec((4 * size, LANES), lambda i, s: (place(i, s), 0)),
        ),
        input_output_aliases=aliases,
        compiler_params=params(),
        name="finish",
        cost_estimate=pl.CostEstimate(
            flops=2 * 48 * 4 * LANES * chunk, transcendentals=0, bytes_accessed=chunk * LANES * 4 * 8
        ),
    )(*args)


def per_device(points, dist, cell_type, collision_rate, vel_index):
    count, rows, cols = dist.shape
    half = count // 2
    strips = lax.axis_size("strip")
    groups = lax.axis_size("vel")
    strip = lax.axis_index("strip")
    size, chunks = plan(half)
    firsts = [sum(chunks[:c]) for c in range(len(chunks))]
    order = range(len(chunks))
    cut = len(chunks) // 2
    groups_of = [order[:cut], order[cut:]]
    side = (strip % 2).astype(jnp.int32).reshape(1)
    info = jnp.stack([strip % 2, (strip // 2) % 2]).astype(jnp.int32)

    swap_pairs = [(s, s ^ 1) for s in range(strips)]
    down_pairs = [
        (s, s + (2 if s % 2 == 0 else -2))
        for s in range(strips)
        if 0 <= s + (2 if s % 2 == 0 else -2) < strips
    ]
    up_pairs = [(b, a) for a, b in down_pairs]
    pair_a = [
        (s, s + (2 if (s // 2) % 2 == 0 else -2))
        for s in range(strips)
        if 0 <= s + (2 if (s // 2) % 2 == 0 else -2) < strips
    ]
    pair_b = [
        (s, s + (-2 if (s // 2) % 2 == 0 else 2))
        for s in range(strips)
        if 0 <= s + (-2 if (s // 2) % 2 == 0 else 2) < strips
    ]

    def swap(value):
        return lax.ppermute(value, "strip", swap_pairs)

    def with_flow(value):
        return lax.ppermute(value, "strip", down_pairs)

    def against_flow(value):
        return lax.ppermute(value, "strip", up_pairs)

    def both_z(value):
        return lax.ppermute(value, "strip", pair_a), lax.ppermute(value, "strip", pair_b)

    def sum_groups(value):
        total = value
        for shift in range(1, groups):
            total = total + lax.ppermute(
                value, "vel", [(g, (g + shift) % groups) for g in range(groups)]
            )
        return total

    flat = dist.reshape(count * rows, cols)
    wall = (cell_type == 1).astype(F32)
    cell_pair = jnp.concatenate([collision_rate, wall])
    other_cells = swap(cell_pair)

    got = []
    for c in order:
        far_start = ((1 - strip % 2) * half + firsts[c]) * rows
        part = lax.dynamic_slice_in_dim(flat, far_start, chunks[c] * rows, axis=0)
        got.append(swap(part))
    tables = prepare(points, vel_index)
    table, _, weights = tables
    lowest = pick(side, flat, lambda s: s * (half // size), half, size, [(0, 3)], [table])
    below = against_flow(lowest)
    gram = jnp.asarray(target_moments(points))
    mat = jnp.asarray(macro_matrix())

    def flow(own, other):
        odd = strip % 2 == 1
        return jnp.concatenate(
            [jnp.where(odd, own[::-1], own), jnp.where(odd, other[::-1], other)]
        )

    flow_rate = flow(collision_rate, other_cells[:rows])
    flow_fluid = 1.0 - flow(wall, other_cells[rows:])
    cells = jnp.concatenate([flow_fluid * (1.0 - flow_rate), flow_fluid])

    home = sum_groups(home_moments(flat, weights, 2 * size))
    home = jnp.concatenate(
        [home[:13], collision_rate.reshape(1, -1), wall.reshape(1, -1), jnp.zeros((1, rows * cols), F32)]
    )
    near_home = jnp.stack([home, *both_z(home)])
    far_home = swap(near_home)

    width = BLOCK_ROWS * LANES
    sums = jnp.zeros((16, width), F32)
    above = []
    for c in order:
        edges = pick(side, got[c], lambda s: 0, chunks[c], size, [(2, 1), (3, 0)])
        above.append(with_flow(edges))
    kept = []
    for number, members in enumerate(groups_of):
        start = firsts[members[0]]
        length = sum(chunks[c] for c in members)
        held = None
        for c in members:
            *held, sums = transport(
                side, [flat, got[c], above[c], below], tables, cells, sums, half,
                chunks[c], firsts[c], size, skip=firsts[c] - start, group=length, into=held,
            )
        next_above = with_flow(held[2])
        next_below = against_flow(held[0])
        kept.append((*held, next_above, next_below))

    total = sum_groups(sums)
    total = total + swap(total)
    sum_a, sum_b = both_z(total)
    change, keep = macro(
        first_macro_kernel, info,
        [total, sum_a, sum_b, near_home, far_home, gram, mat],
        [
            jax.ShapeDtypeStruct((48, 11 * LANES), BF16),
            jax.ShapeDtypeStruct((16, SPAN * LANES), F32),
        ],
        [pltpu.VMEM((16, SPAN * LANES), F32)] * 2,
    )

    sums = jnp.zeros((16, width), F32)
    near, back = {}, {}
    for c in order:
        number = int(c >= cut)
        start = firsts[groups_of[number][0]]
        near[c], far, sums = transport(
            side, list(kept[number]), tables, cells, sums, half,
            chunks[c], firsts[c], size, change, skip=firsts[c] - start,
        )
        back[c] = swap(far)
    total = sum_groups(sums)
    total = total + swap(total)
    sum_a, sum_b = both_z(total)
    change, state = macro(
        second_macro_kernel, info,
        [total, sum_a, sum_b, keep, gram, mat],
        [
            jax.ShapeDtypeStruct((48, STRIP_ROWS * LANES), BF16),
            jax.ShapeDtypeStruct((8, STRIP_ROWS * LANES), F32),
        ],
        [pltpu.VMEM((16, SPAN * LANES), F32)],
    )
    out = None
    for own, parts in ((True, near), (False, back)):
        for c in order:
            out = finish(
                side, out, parts[c], own, table, change, half, chunks[c], firsts[c], size
            )
    return out.reshape(dist.shape), state[:5].reshape(5, rows, cols)


def solution(mesh):
    def whole(dist, cell_type, collision_rate, vel_index):
        points = round(vel_index.shape[1] ** (1.0 / 3.0))
        in_specs = (P("vel", "strip", None), P("strip", None), P("strip", None), P(None, "vel"))
        out_specs = (P("vel", "strip", None), P(None, "strip", None))

        def body(*args):
            return per_device(points, *args)

        run = jax.shard_map(
            body, mesh=mesh, in_specs=in_specs, out_specs=out_specs, check_vma=False
        )
        return run(dist, cell_type, collision_rate, vel_index)

    return whole
```

```python
import functools
import math

import jax
import jax.numpy as jnp
import numpy as np
from jax import lax
from jax.experimental import pallas as pl
from jax.experimental.pallas import tpu as pltpu
from jax.sharding import PartitionSpec as P


STEP_RATIO = 0.1
SOURCE_WEIGHT = 0.5
HEAT_WEIGHT = 4.0 / 15.0
SWEEPS = 3
HIGH = lax.Precision.HIGHEST
LANES = 128
STRIP_ROWS = 4
BLOCK_ROWS = 2 * STRIP_ROWS
SPAN = 3 * BLOCK_ROWS
F32 = jnp.float32
BF16 = jnp.bfloat16


def params(**more):
    return pltpu.CompilerParams(vmem_limit_bytes=62 * 1024 * 1024, **more)


def plan(half):
    block = 288 if half % 288 == 0 else 144
    blocks = half // block
    if blocks % 6 == 0:
        unit = block * (blocks // 6)
        return block, [unit, 2 * unit, 2 * unit, unit]
    return block, [block * (blocks - 2), block, block]


def moment_rows(vel_x, vel_y, vel_z, volume, lib):
    energy = vel_x * vel_x + vel_y * vel_y + vel_z * vel_z
    weight = volume * math.pi ** (-1.5) * lib.exp(-energy)
    rows = [
        lib.ones_like(vel_x),
        vel_x,
        vel_y,
        vel_z,
        energy,
        vel_x * vel_x,
        vel_y * vel_y,
        vel_x * vel_y,
        vel_x * vel_z,
        vel_y * vel_z,
        energy * vel_x,
        energy * vel_y,
        energy * vel_z,
    ]
    return lib.concatenate([(row * weight).reshape(1, -1) for row in rows])


def state_rows(vel_x, vel_y, vel_z, lib):
    energy = vel_x * vel_x + vel_y * vel_y + vel_z * vel_z
    shape_heat = HEAT_WEIGHT * (energy - 2.5)
    rows = [
        lib.ones_like(vel_x),
        2.0 * vel_x,
        2.0 * vel_y,
        2.0 * vel_z,
        energy - 1.5,
        shape_heat * vel_x,
        shape_heat * vel_y,
        shape_heat * vel_z,
    ]
    return lib.concatenate([row.reshape(1, -1) for row in rows])


def target_moments(points):
    line = (np.arange(points) - (points - 1) / 2.0) * (8.0 / points)
    comps = [a.reshape(-1) for a in np.meshgrid(line, line, line, indexing="ij")]
    gram = moment_rows(*comps, (8.0 / points) ** 3, np) @ state_rows(*comps, np).T
    gram[np.abs(gram) < 1e-12] = 0.0
    full = np.zeros((16, 8), np.float32)
    full[:13] = gram
    return full


def macro_matrix():
    third = 2.0 / 3.0
    unit = np.eye(16, dtype=np.float64)
    start = [unit[0], unit[1], unit[2], unit[3], third * unit[4] - unit[0]]
    heat = [unit[10] - 2.5 * unit[1], unit[11] - 2.5 * unit[2], unit[12] - 2.5 * unit[3]]
    flux = [
        unit[1],
        unit[2],
        2.0 * unit[5] - third * unit[4],
        2.0 * unit[7],
        2.0 * unit[6] - third * unit[4],
        2.0 * unit[8],
        2.0 * unit[9],
        heat[0],
        heat[1],
    ]
    out = np.zeros((32, 16), np.float64)
    for row in range(5):
        out[row] = start[row]
        out[8 + row] = flux[(0, 2, 3, 5, 7)[row]]
        out[16 + row] = flux[(1, 3, 4, 6, 8)[row]]
    for row in range(3):
        out[24 + 5 + row] = heat[row]
    return out.astype(np.float32)


def minmod(left, right):
    return jnp.maximum(jnp.minimum(right, jnp.maximum(left, 0.0)), jnp.minimum(left, 0.0))


def strided(start, count):
    return pl.ds(start, count, stride=STRIP_ROWS)


def pick_kernel(size, picks, side_ref, strip_ref, *rest):
    out_ref = rest[-1]
    side = side_ref[0]
    for index, (even, odd) in enumerate(picks):
        out_ref[index] = strip_ref[strided(jnp.where(side == 1, odd, even), size), :]


def pick(side, flat, start, count, size, picks, earlier=()):
    return pl.pallas_call(
        functools.partial(pick_kernel, size, picks),
        out_shape=jax.ShapeDtypeStruct((len(picks), count, LANES), F32),
        grid_spec=pltpu.PrefetchScalarGridSpec(
            num_scalar_prefetch=1,
            grid=(count // size,),
            in_specs=[
                pl.BlockSpec((4 * size, LANES), lambda i, s: (start(s[0]) + i, 0)),
                *[pl.BlockSpec(memory_space=pl.ANY)] * len(earlier),
            ],
            out_specs=pl.BlockSpec((len(picks), size, LANES), lambda i, s: (0, i, 0)),
        ),
        compiler_params=params(),
        cost_estimate=pl.CostEstimate(
            flops=0, transcendentals=0, bytes_accessed=count * LANES * 4 * (4 + len(picks))
        ),
    )(side, flat, *earlier)


def prepare_kernel(points, vel_ref, table_ref, const_ref, weight_ref):
    comps = (vel_ref[...].astype(F32) - (points - 1) / 2.0) * (8.0 / points)
    vel_x, vel_y, vel_z = comps[0:1], comps[1:2], comps[2:3]
    moments = moment_rows(vel_x, vel_y, vel_z, (8.0 / points) ** 3, jnp)
    high = moments.astype(BF16).astype(F32)
    shapes = state_rows(vel_x, vel_y, vel_z, jnp)
    part_a = shapes.astype(BF16).astype(F32)
    part_b = (shapes - part_a).astype(BF16).astype(F32)
    part_c = shapes - part_a - part_b
    width = vel_x.shape[1]
    rows = jnp.concatenate(
        [
            *[part_a] * 3,
            *[part_b] * 2,
            part_c,
            high,
            jnp.zeros((3, width), F32),
            moments - high,
            jnp.zeros((3, width), F32),
            STEP_RATIO * jnp.abs(vel_x),
            STEP_RATIO * jnp.abs(vel_y),
            jnp.where(vel_y > 0, 0.5, -0.5),
            jnp.zeros((45, width), F32),
        ]
    )
    columns = rows.T
    table_ref[...] = columns[:, :48].astype(BF16)
    weight_ref[...] = columns[:, 48:80].astype(BF16)
    const_ref[...] = columns[:, 80:88]


def prepare(points, vel_index):
    count = vel_index.shape[1]
    vmem = pl.BlockSpec(memory_space=pltpu.VMEM)
    return pl.pallas_call(
        functools.partial(prepare_kernel, points),
        out_shape=(
            jax.ShapeDtypeStruct((count, 48), BF16),
            jax.ShapeDtypeStruct((count, 8), F32),
            jax.ShapeDtypeStruct((count, 32), BF16),
        ),
        in_specs=[vmem],
        out_specs=[vmem] * 3,
        compiler_params=params(),
        name="prepare",
        cost_estimate=pl.CostEstimate(
            flops=200 * count, transcendentals=count, bytes_accessed=count * 1000
        ),
    )(vel_index)


def weighted(weights, first, second):
    over_rows = (((0,), (0,)), ((), ()))
    both = lax.dot_general(weights, first, over_rows, preferred_element_type=F32)
    rest = lax.dot_general(weights, second, over_rows, preferred_element_type=F32)
    return both[:16] + both[16:] + rest[:16]


def moment_kernel(size, dist_ref, weight_ref, out_ref):
    @pl.when(pl.program_id(0) == 0)
    def _():
        out_ref[...] = jnp.zeros_like(out_ref)

    for pair in range(0, STRIP_ROWS, 2):
        value = jnp.concatenate(
            [dist_ref[strided(row, size), :] for row in (pair, pair + 1)], axis=1
        )
        high = value.astype(BF16)
        out_ref[:, pair * LANES : (pair + 2) * LANES] += weighted(
            weight_ref[...], high, (value - high.astype(F32)).astype(BF16)
        )


def home_moments(flat, weights, size):
    count = flat.shape[0] // STRIP_ROWS
    width = STRIP_ROWS * LANES
    return pl.pallas_call(
        functools.partial(moment_kernel, size),
        out_shape=jax.ShapeDtypeStruct((16, width), F32),
        grid=(count // size,),
        in_specs=[
            pl.BlockSpec((4 * size, LANES), lambda i: (i, 0)),
            pl.BlockSpec((size, 32), lambda i: (i, 0)),
        ],
        out_specs=pl.BlockSpec((16, width), lambda i: (0, 0)),
        compiler_params=params(),
        name="home_moments",
        cost_estimate=pl.CostEstimate(
            flops=2 * 48 * count * width, transcendentals=0, bytes_accessed=count * width * 4
        ),
    )(flat, weights)


def transport_kernel(size, second_pass, side_ref, *refs):
    if second_pass:
        (table_ref, change_ref, q_first, q_mid, q_edge, up_ref, down_ref, *rest) = refs
    else:
        (own_ref, got_ref, up_ref, down_ref, *rest) = refs
    (const_ref, weight_ref, cell_ref, sum_in_ref, *rest) = rest
    if second_pass:
        (near_out, far_out, sum_ref, lift_ref) = rest[-4:]
    else:
        (first_out, mid_out, edge_out, sum_ref) = rest[-4:]
    side = side_ref[0]
    group_size = 32 if size % 32 == 0 else 16

    @pl.when(pl.program_id(0) == 0)
    def _():
        sum_ref[...] = sum_in_ref[...]

    if second_pass:
        lift_ref[...] = jnp.dot(table_ref[...], change_ref[...], preferred_element_type=F32)

    def row_out(row):
        if second_pass:
            return near_out.at[row] if row < 4 else far_out.at[row - 4]
        if row == 0:
            return first_out
        return mid_out.at[row - 1] if row < 6 else edge_out.at[row - 6]

    lane = lax.broadcasted_iota(jnp.int32, (group_size, LANES), 1)
    inner_low = jnp.where(lane == 0, 0.0, 1.0)
    inner_high = jnp.where(lane == LANES - 1, 0.0, 1.0)

    def body(group, carry):
        base = pl.multiple_of(group * group_size, group_size)
        rows = pl.ds(base, group_size)

        def load(row):
            if row < 0:
                value = up_ref[row + 2, rows, :]
            elif row == 8:
                value = down_ref[rows, :]
            elif second_pass:
                if row == 0:
                    value = q_first[rows, :]
                elif row < 6:
                    value = q_mid[row - 1, rows, :]
                else:
                    value = q_edge[row - 6, rows, :]
            else:
                ref = own_ref if row < 4 else got_ref
                local = jnp.where(side == 1, 3 - row % 4, row % 4)
                value = ref[strided(base * STRIP_ROWS + local, group_size), :]
            if second_pass:
                value = value + lift_ref[rows, pl.ds((row + 2) * LANES, LANES)]
            return value

        def wide(column):
            return jnp.broadcast_to(const_ref[rows, column : column + 1], (group_size, LANES))

        speed_x = wide(0)
        speed_y = wide(1)
        half_sign = wide(2)
        forward = half_sign > 0.0
        open_end = jnp.where(forward, inner_low, inner_high)

        behind = load(-2)
        here = load(-1)
        ahead = load(0)
        step = ahead - here
        upwind = here + 0.5 * minmod(here - behind, step)
        here = ahead
        for row in range(BLOCK_ROWS):
            ahead = load(row + 1)
            next_step = ahead - here
            next_upwind = here + 0.5 * minmod(step, next_step)
            drift = speed_x * (next_upwind - upwind)
            step = next_step
            upwind = next_upwind
            left = here - pltpu.roll(here, 1, 1) * inner_low
            right = pltpu.roll(here, LANES - 1, 1) * inner_high - here
            face = here + half_sign * minmod(left, right)
            other = jnp.where(forward, pltpu.roll(face, 1, 1), pltpu.roll(face, LANES - 1, 1))
            drift = drift + speed_y * (face - other * open_end)
            keep = jnp.broadcast_to(cell_ref[row : row + 1, :], (group_size, LANES))
            fluid = jnp.broadcast_to(cell_ref[row + 8 : row + 9, :], (group_size, LANES))
            value = keep * here - fluid * drift
            row_out(row)[rows, :] = value
            here = ahead
        return carry

    lax.fori_loop(0, size // group_size, body, 0)
    for pair in range(0, BLOCK_ROWS, 2):
        value = jnp.concatenate([row_out(pair)[...], row_out(pair + 1)[...]], axis=1)
        high = value.astype(BF16)
        part = weighted(weight_ref[...], high, (value - high.astype(F32)).astype(BF16))
        for row in (pair, pair + 1):
            place = jnp.where(side == 1, 7 - row, row)
            columns = pl.ds(pl.multiple_of(place * LANES, LANES), LANES)
            sum_ref[:, columns] += part[:, (row - pair) * LANES : (row - pair + 1) * LANES]


def transport(
    side, sources, tables, cells, sums, half, chunk, first, size, change=None, skip=0, group=None, into=None
):
    second_pass = change is not None
    steps = chunk // size
    shift = half // size
    begin = first // size
    offset = skip // size
    table, const, weights = tables
    width = BLOCK_ROWS * LANES

    def mine(i, s):
        return s[0] * shift + begin + i

    def stack_of(count, at):
        return pl.BlockSpec((count, size, LANES), lambda i, s: (0, at + i, 0))

    aliases = {}
    if second_pass:
        args = [table, change]
        specs = [
            pl.BlockSpec((size, 48), lambda i, s: (mine(i, s), 0)),
            pl.BlockSpec(change.shape, lambda i, s: (0, 0)),
            stack_of(None, offset),
            stack_of(5, offset),
            stack_of(2, offset),
            stack_of(2, offset),
            stack_of(None, offset),
        ]
        outs = [jax.ShapeDtypeStruct((4, n, LANES), F32) for n in (half, chunk)]
        out_specs = [stack_of(4, begin), stack_of(4, 0)]
        scratch = [pltpu.VMEM((size, 11 * LANES), F32)]
    else:
        args = []
        specs = [
            pl.BlockSpec((4 * size, LANES), lambda i, s: (mine(i, s), 0)),
            pl.BlockSpec((4 * size, LANES), lambda i, s: (i, 0)),
            stack_of(2, 0),
            stack_of(None, begin),
        ]
        outs = [jax.ShapeDtypeStruct((n, group, LANES), F32) for n in (1, 5, 2)]
        out_specs = [stack_of(None, offset), stack_of(5, offset), stack_of(2, offset)]
        scratch = []
    whole = pl.BlockSpec((16, width), lambda i, s: (0, 0))
    args = [side, *args, *sources, const, weights, cells, sums]
    specs = [
        *specs,
        pl.BlockSpec((size, 8), lambda i, s: (mine(i, s), 0)),
        pl.BlockSpec((size, 32), lambda i, s: (mine(i, s), 0)),
        pl.BlockSpec((16, LANES), lambda i, s: (0, 0)),
        whole,
    ]
    if into is not None:
        aliases = {len(args) + n: n for n in range(len(into))}
        args = [*args, *into]
        specs = [*specs, *[pl.BlockSpec(memory_space=pl.ANY)] * len(into)]
    return pl.pallas_call(
        functools.partial(transport_kernel, size, second_pass),
        out_shape=(*outs, jax.ShapeDtypeStruct((16, width), F32)),
        grid_spec=pltpu.PrefetchScalarGridSpec(
            num_scalar_prefetch=1,
            grid=(steps,),
            in_specs=specs,
            out_specs=[*out_specs, whole],
            scratch_shapes=scratch,
        ),
        input_output_aliases=aliases,
        compiler_params=params(),
        name="transport_second" if second_pass else "transport_first",
        cost_estimate=pl.CostEstimate(
            flops=60 * chunk * width, transcendentals=0, bytes_accessed=chunk * LANES * 4 * 19
        ),
    )(*args)


def sweep_block(inputs, relax, rate):
    start, flux_x, flux_y = inputs
    lane = lax.broadcasted_iota(jnp.int32, (8, LANES), 1)
    inner_low = jnp.where(lane == 0, 0.0, 1.0)
    inner_high = jnp.where(lane == LANES - 1, 0.0, 1.0)

    def block(array, row):
        if row < 0 or row >= SPAN:
            return jnp.zeros((8, LANES), F32)
        return array[:, row * LANES : (row + 1) * LANES]

    def lower(value):
        return pltpu.roll(value, 1, 1) * inner_low

    def upper(value):
        return pltpu.roll(value, LANES - 1, 1) * inner_high

    source = []
    for row in range(SPAN):
        diff_x = 0.5 * (block(flux_x, row + 1) - block(flux_x, row - 1))
        side = block(flux_y, row)
        diff_y = 0.5 * (upper(side) - lower(side))
        source.append(block(start, row) - SOURCE_WEIGHT * (diff_x + diff_y))
    zero = jnp.zeros((8, LANES), F32)
    kappa = [block(rate, row) for row in range(SPAN)]
    scale = [block(relax, row) for row in range(SPAN)]
    state = [block(start, row) for row in range(SPAN)]
    for _ in range(SWEEPS):
        near = [zero, *state, zero]
        state = [
            (source[row] + kappa[row] * (near[row] + near[row + 2] + lower(near[row + 1]) + upper(near[row + 1])))
            * scale[row]
            for row in range(SPAN)
        ]
    return jnp.concatenate(state, axis=1)


def stacked(value):
    first = value.astype(BF16)
    rest = value - first.astype(F32)
    second = rest.astype(BF16)
    third = (rest - second.astype(F32)).astype(BF16)
    return jnp.concatenate([first, second, third, first, second, first], axis=0)


def relax_rows(rate):
    inside = rate > 0.0
    kappa = jnp.where(inside, 0.5 / jnp.where(inside, rate, 1.0), 0.0)
    scale = jnp.where(inside, 1.0 / (1.0 + 4.0 * kappa), 0.0)
    width = rate.shape[1]
    return jnp.broadcast_to(kappa, (8, width)), jnp.broadcast_to(scale, (8, width))


def place_blocks(info_ref, span_ref, own, pair_a, pair_b):
    odd = info_ref[1]
    width = BLOCK_ROWS * LANES
    span_ref[:, width : 2 * width] = own
    place_a = pl.multiple_of((1 - odd) * 2 * width, width)
    place_b = pl.multiple_of(odd * 2 * width, width)
    span_ref[:, pl.ds(place_a, width)] = pair_a
    span_ref[:, pl.ds(place_b, width)] = pair_b


def first_macro_kernel(
    info_ref, sum_ref, sum_a_ref, sum_b_ref, near_ref, far_ref, gram_ref, mat_ref,
    change_ref, keep_ref, span_ref, home_ref,
):
    side = info_ref[0]
    odd = info_ref[1]
    width = BLOCK_ROWS * LANES
    part = STRIP_ROWS * LANES
    place_blocks(info_ref, span_ref, sum_ref[...], sum_a_ref[...], sum_b_ref[...])
    for ref, where in ((near_ref, side), (far_ref, 1 - side)):
        for index, block in enumerate((1, (1 - odd) * 2, odd * 2)):
            spot = pl.multiple_of(block * width + where * part, part)
            home_ref[:, pl.ds(spot, part)] = ref[index]
    home = home_ref[...]
    rate = home[13:14, :]
    ratio = jnp.where(home[14:15, :] > 0.5, 1.0, rate)
    mat = mat_ref[...]
    first = jnp.dot(mat, jnp.where(lax.broadcasted_iota(jnp.int32, home.shape, 0) < 13, home, 0.0), precision=HIGH)
    fields = first[:8] + first[24:]
    moments = span_ref[...] + ratio * jnp.dot(gram_ref[...], fields, precision=HIGH)
    all_parts = jnp.dot(mat, moments, precision=HIGH)
    start = all_parts[:8]
    kappa, scale = relax_rows(rate)
    state = sweep_block((start, all_parts[8:16], all_parts[16:24]), scale, kappa)
    change = ratio * fields + (state - start)
    span_ref[0:8, :] = change
    keep_ref[0:8, :] = state + all_parts[24:]
    keep_ref[8:9, :] = rate
    keep_ref[9:10, :] = ratio
    keep_ref[10:16, :] = jnp.zeros((6, SPAN * LANES), F32)
    for row in range(-2, 9):
        spot = jnp.where(side == 1, 15 - row, 8 + row)
        piece = span_ref[0:8, pl.ds(pl.multiple_of(spot * LANES, LANES), LANES)]
        change_ref[:, (row + 2) * LANES : (row + 3) * LANES] = stacked(piece)


def second_macro_kernel(
    info_ref, sum_ref, sum_a_ref, sum_b_ref, keep_ref, gram_ref, mat_ref,
    change_ref, state_ref, span_ref,
):
    side = info_ref[0]
    place_blocks(info_ref, span_ref, sum_ref[...], sum_a_ref[...], sum_b_ref[...])
    fields = keep_ref[0:8, :]
    rate = keep_ref[8:9, :]
    ratio = keep_ref[9:10, :]
    moments = span_ref[...] + ratio * jnp.dot(gram_ref[...], fields, precision=HIGH)
    all_parts = jnp.dot(mat_ref[...], moments, precision=HIGH)
    start = all_parts[:8]
    kappa, scale = relax_rows(rate)
    state = sweep_block((start, all_parts[8:16], all_parts[16:24]), scale, kappa)
    span_ref[0:8, :] = ratio * fields + (state - start)
    span_ref[8:16, :] = state
    part = STRIP_ROWS * LANES
    spot = pl.ds(pl.multiple_of(2 * part + side * part, part), part)
    change_ref[...] = stacked(span_ref[0:8, spot])
    state_ref[...] = span_ref[8:16, spot]


def macro(kernel, info, args, outs, scratch):
    vmem = pl.BlockSpec(memory_space=pltpu.VMEM)
    return pl.pallas_call(
        kernel,
        out_shape=outs,
        in_specs=[pl.BlockSpec(memory_space=pltpu.SMEM)] + [vmem] * len(args),
        out_specs=[vmem] * len(outs),
        scratch_shapes=scratch,
        compiler_params=params(),
        cost_estimate=pl.CostEstimate(flops=4000000, transcendentals=0, bytes_accessed=1000000),
    )(info, *args)


def finish_kernel(size, own, side_ref, rows_ref, table_ref, change_ref, *rest):
    out_ref = rest[-1]
    flipped = side_ref[0] == (1 if own else 0)
    lift = jnp.dot(table_ref[...], change_ref[...], preferred_element_type=F32)
    for row in range(STRIP_ROWS):
        index = jnp.where(flipped, 3 - row, row)
        out_ref[strided(row, size), :] = (
            rows_ref[index] + lift[:, row * LANES : (row + 1) * LANES]
        )


def finish(side, out, rows, own, table, change, half, chunk, first, size):
    shift = half // size
    begin = first // size

    def place(i, s):
        return (s[0] if own else 1 - s[0]) * shift + begin + i

    specs = [
        pl.BlockSpec((4, size, LANES), lambda i, s: (0, i, 0)),
        pl.BlockSpec((size, 48), lambda i, s: (place(i, s), 0)),
        pl.BlockSpec(change.shape, lambda i, s: (0, 0)),
    ]
    args = [side, rows, table, change]
    aliases = {}
    if out is not None:
        specs.append(pl.BlockSpec(memory_space=pl.ANY))
        args.append(out)
        aliases = {4: 0}
    return pl.pallas_call(
        functools.partial(finish_kernel, size, own),
        out_shape=jax.ShapeDtypeStruct((2 * half * STRIP_ROWS, LANES), F32),
        grid_spec=pltpu.PrefetchScalarGridSpec(
            num_scalar_prefetch=1,
            grid=(chunk // size,),
            in_specs=specs,
            out_specs=pl.BlockSpec((4 * size, LANES), lambda i, s: (place(i, s), 0)),
        ),
        input_output_aliases=aliases,
        compiler_params=params(),
        name="finish",
        cost_estimate=pl.CostEstimate(
            flops=2 * 48 * 4 * LANES * chunk, transcendentals=0, bytes_accessed=chunk * LANES * 4 * 8
        ),
    )(*args)


def per_device(points, dist, cell_type, collision_rate, vel_index):
    count, rows, cols = dist.shape
    half = count // 2
    strips = lax.axis_size("strip")
    groups = lax.axis_size("vel")
    strip = lax.axis_index("strip")
    size, chunks = plan(half)
    firsts = [sum(chunks[:c]) for c in range(len(chunks))]
    order = range(len(chunks))
    cut = len(chunks) // 2
    groups_of = [order[:cut], order[cut:]]
    side = (strip % 2).astype(jnp.int32).reshape(1)
    info = jnp.stack([strip % 2, (strip // 2) % 2]).astype(jnp.int32)

    swap_pairs = [(s, s ^ 1) for s in range(strips)]
    down_pairs = [
        (s, s + (2 if s % 2 == 0 else -2))
        for s in range(strips)
        if 0 <= s + (2 if s % 2 == 0 else -2) < strips
    ]
    up_pairs = [(b, a) for a, b in down_pairs]
    pair_a = [
        (s, s + (2 if (s // 2) % 2 == 0 else -2))
        for s in range(strips)
        if 0 <= s + (2 if (s // 2) % 2 == 0 else -2) < strips
    ]
    pair_b = [
        (s, s + (-2 if (s // 2) % 2 == 0 else 2))
        for s in range(strips)
        if 0 <= s + (-2 if (s // 2) % 2 == 0 else 2) < strips
    ]

    def swap(value):
        return lax.ppermute(value, "strip", swap_pairs)

    def with_flow(value):
        return lax.ppermute(value, "strip", down_pairs)

    def against_flow(value):
        return lax.ppermute(value, "strip", up_pairs)

    def both_z(value):
        return lax.ppermute(value, "strip", pair_a), lax.ppermute(value, "strip", pair_b)

    def sum_groups(value):
        total = value
        for shift in range(1, groups):
            total = total + lax.ppermute(
                value, "vel", [(g, (g + shift) % groups) for g in range(groups)]
            )
        return total

    flat = dist.reshape(count * rows, cols)
    wall = (cell_type == 1).astype(F32)
    cell_pair = jnp.concatenate([collision_rate, wall])
    other_cells = swap(cell_pair)

    got = []
    for c in order:
        far_start = ((1 - strip % 2) * half + firsts[c]) * rows
        part = lax.dynamic_slice_in_dim(flat, far_start, chunks[c] * rows, axis=0)
        got.append(swap(part))
    lowest = pick(side, flat, lambda s: s * (half // size), half, size, [(0, 3)])
    below = against_flow(lowest)
    tables = prepare(points, vel_index)
    table, _, weights = tables
    gram = jnp.asarray(target_moments(points))
    mat = jnp.asarray(macro_matrix())

    def flow(own, other):
        odd = strip % 2 == 1
        return jnp.concatenate(
            [jnp.where(odd, own[::-1], own), jnp.where(odd, other[::-1], other)]
        )

    flow_rate = flow(collision_rate, other_cells[:rows])
    flow_fluid = 1.0 - flow(wall, other_cells[rows:])
    cells = jnp.concatenate([flow_fluid * (1.0 - flow_rate), flow_fluid])

    home = sum_groups(home_moments(flat, weights, 2 * size))
    home = jnp.concatenate(
        [home[:13], collision_rate.reshape(1, -1), wall.reshape(1, -1), jnp.zeros((1, rows * cols), F32)]
    )
    near_home = jnp.stack([home, *both_z(home)])
    far_home = swap(near_home)

    width = BLOCK_ROWS * LANES
    sums = jnp.zeros((16, width), F32)
    above = []
    for c in order:
        edges = pick(side, got[c], lambda s: 0, chunks[c], size, [(2, 1), (3, 0)])
        above.append(with_flow(edges))
    kept = []
    for number, members in enumerate(groups_of):
        start = firsts[members[0]]
        length = sum(chunks[c] for c in members)
        held = None
        for c in members:
            *held, sums = transport(
                side, [flat, got[c], above[c], below], tables, cells, sums, half,
                chunks[c], firsts[c], size, skip=firsts[c] - start, group=length, into=held,
            )
        next_above = with_flow(held[2])
        next_below = against_flow(held[0])
        kept.append((*held, next_above, next_below))

    total = sum_groups(sums)
    total = total + swap(total)
    sum_a, sum_b = both_z(total)
    change, keep = macro(
        first_macro_kernel, info,
        [total, sum_a, sum_b, near_home, far_home, gram, mat],
        [
            jax.ShapeDtypeStruct((48, 11 * LANES), BF16),
            jax.ShapeDtypeStruct((16, SPAN * LANES), F32),
        ],
        [pltpu.VMEM((16, SPAN * LANES), F32)] * 2,
    )

    sums = jnp.zeros((16, width), F32)
    near, back = None, []
    for c in order:
        number = int(c >= cut)
        start = firsts[groups_of[number][0]]
        near, far, sums = transport(
            side, list(kept[number]), tables, cells, sums, half,
            chunks[c], firsts[c], size, change, skip=firsts[c] - start,
            into=None if near is None else [near],
        )
        back.append(swap(far))
    total = sum_groups(sums)
    total = total + swap(total)
    sum_a, sum_b = both_z(total)
    change, state = macro(
        second_macro_kernel, info,
        [total, sum_a, sum_b, keep, gram, mat],
        [
            jax.ShapeDtypeStruct((48, STRIP_ROWS * LANES), BF16),
            jax.ShapeDtypeStruct((8, STRIP_ROWS * LANES), F32),
        ],
        [pltpu.VMEM((16, SPAN * LANES), F32)],
    )
    out = finish(side, None, near, True, table, change, half, half, 0, size)
    for c in order:
        out = finish(side, out, back[c], False, table, change, half, chunks[c], firsts[c], size)
    return out.reshape(dist.shape), state[:5].reshape(5, rows, cols)


def solution(mesh):
    def whole(dist, cell_type, collision_rate, vel_index):
        points = round(vel_index.shape[1] ** (1.0 / 3.0))
        in_specs = (P("vel", "strip", None), P("strip", None), P("strip", None), P(None, "vel"))
        out_specs = (P("vel", "strip", None), P(None, "strip", None))

        def body(*args):
            return per_device(points, *args)

        run = jax.shard_map(
            body, mesh=mesh, in_specs=in_specs, out_specs=out_specs, check_vma=False
        )
        return run(dist, cell_type, collision_rate, vel_index)

    return whole
```

```python
import functools
import math

import jax
import jax.numpy as jnp
import numpy as np
from jax import lax
from jax.experimental import pallas as pl
from jax.experimental.pallas import tpu as pltpu
from jax.sharding import PartitionSpec as P


STEP_RATIO = 0.1
SOURCE_WEIGHT = 0.5
HEAT_WEIGHT = 4.0 / 15.0
SWEEPS = 3
HIGH = lax.Precision.HIGHEST
LANES = 128
STRIP_ROWS = 4
BLOCK_ROWS = 2 * STRIP_ROWS
SPAN = 3 * BLOCK_ROWS
F32 = jnp.float32
BF16 = jnp.bfloat16


def params(**more):
    return pltpu.CompilerParams(vmem_limit_bytes=62 * 1024 * 1024, **more)


def plan(half):
    block = 288 if half % 288 == 0 else 144
    blocks = half // block
    if blocks % 6 == 0:
        unit = block * (blocks // 6)
        return block, [2 * unit, unit, unit, unit, unit]
    return block, [block * (blocks - 2), block, block]


def second_order(pieces):
    cut = (pieces + 1) // 2
    return [*range(1, cut), 0, *range(cut, pieces)], cut


def moment_rows(vel_x, vel_y, vel_z, volume, lib):
    energy = vel_x * vel_x + vel_y * vel_y + vel_z * vel_z
    weight = volume * math.pi ** (-1.5) * lib.exp(-energy)
    rows = [
        lib.ones_like(vel_x),
        vel_x,
        vel_y,
        vel_z,
        energy,
        vel_x * vel_x,
        vel_y * vel_y,
        vel_x * vel_y,
        vel_x * vel_z,
        vel_y * vel_z,
        energy * vel_x,
        energy * vel_y,
        energy * vel_z,
    ]
    return lib.concatenate([(row * weight).reshape(1, -1) for row in rows])


def state_rows(vel_x, vel_y, vel_z, lib):
    energy = vel_x * vel_x + vel_y * vel_y + vel_z * vel_z
    shape_heat = HEAT_WEIGHT * (energy - 2.5)
    rows = [
        lib.ones_like(vel_x),
        2.0 * vel_x,
        2.0 * vel_y,
        2.0 * vel_z,
        energy - 1.5,
        shape_heat * vel_x,
        shape_heat * vel_y,
        shape_heat * vel_z,
    ]
    return lib.concatenate([row.reshape(1, -1) for row in rows])


def target_moments(points):
    line = (np.arange(points) - (points - 1) / 2.0) * (8.0 / points)
    comps = [a.reshape(-1) for a in np.meshgrid(line, line, line, indexing="ij")]
    gram = moment_rows(*comps, (8.0 / points) ** 3, np) @ state_rows(*comps, np).T
    gram[np.abs(gram) < 1e-12] = 0.0
    full = np.zeros((16, 8), np.float32)
    full[:13] = gram
    return full


def macro_matrix():
    third = 2.0 / 3.0
    unit = np.eye(16, dtype=np.float64)
    start = [unit[0], unit[1], unit[2], unit[3], third * unit[4] - unit[0]]
    heat = [unit[10] - 2.5 * unit[1], unit[11] - 2.5 * unit[2], unit[12] - 2.5 * unit[3]]
    flux = [
        unit[1],
        unit[2],
        2.0 * unit[5] - third * unit[4],
        2.0 * unit[7],
        2.0 * unit[6] - third * unit[4],
        2.0 * unit[8],
        2.0 * unit[9],
        heat[0],
        heat[1],
    ]
    out = np.zeros((32, 16), np.float64)
    for row in range(5):
        out[row] = start[row]
        out[8 + row] = flux[(0, 2, 3, 5, 7)[row]]
        out[16 + row] = flux[(1, 3, 4, 6, 8)[row]]
    for row in range(3):
        out[24 + 5 + row] = heat[row]
    return out.astype(np.float32)


def minmod(left, right):
    return jnp.maximum(jnp.minimum(right, jnp.maximum(left, 0.0)), jnp.minimum(left, 0.0))


def strided(start, count):
    return pl.ds(start, count, stride=STRIP_ROWS)


def pick_kernel(size, picks, side_ref, strip_ref, *rest):
    out_ref = rest[-1]
    side = side_ref[0]
    for index, (even, odd) in enumerate(picks):
        out_ref[index] = strip_ref[strided(jnp.where(side == 1, odd, even), size), :]


def pick(side, flat, start, count, size, picks, earlier=()):
    return pl.pallas_call(
        functools.partial(pick_kernel, size, picks),
        out_shape=jax.ShapeDtypeStruct((len(picks), count, LANES), F32),
        grid_spec=pltpu.PrefetchScalarGridSpec(
            num_scalar_prefetch=1,
            grid=(count // size,),
            in_specs=[
                pl.BlockSpec((4 * size, LANES), lambda i, s: (start(s[0]) + i, 0)),
                *[pl.BlockSpec(memory_space=pl.ANY)] * len(earlier),
            ],
            out_specs=pl.BlockSpec((len(picks), size, LANES), lambda i, s: (0, i, 0)),
        ),
        compiler_params=params(),
        cost_estimate=pl.CostEstimate(
            flops=0, transcendentals=0, bytes_accessed=count * LANES * 4 * (4 + len(picks))
        ),
    )(side, flat, *earlier)


def prepare_kernel(points, vel_ref, table_ref, const_ref, weight_ref):
    comps = (vel_ref[...].astype(F32) - (points - 1) / 2.0) * (8.0 / points)
    vel_x, vel_y, vel_z = comps[0:1], comps[1:2], comps[2:3]
    moments = moment_rows(vel_x, vel_y, vel_z, (8.0 / points) ** 3, jnp)
    high = moments.astype(BF16).astype(F32)
    shapes = state_rows(vel_x, vel_y, vel_z, jnp)
    part_a = shapes.astype(BF16).astype(F32)
    part_b = (shapes - part_a).astype(BF16).astype(F32)
    part_c = shapes - part_a - part_b
    width = vel_x.shape[1]
    rows = jnp.concatenate(
        [
            *[part_a] * 3,
            *[part_b] * 2,
            part_c,
            high,
            jnp.zeros((3, width), F32),
            moments - high,
            jnp.zeros((3, width), F32),
            STEP_RATIO * jnp.abs(vel_x),
            STEP_RATIO * jnp.abs(vel_y),
            jnp.where(vel_y > 0, 0.5, -0.5),
            jnp.zeros((45, width), F32),
        ]
    )
    columns = rows.T
    table_ref[...] = columns[:, :48].astype(BF16)
    weight_ref[...] = columns[:, 48:80].astype(BF16)
    const_ref[...] = columns[:, 80:88]


def prepare(points, vel_index):
    count = vel_index.shape[1]
    vmem = pl.BlockSpec(memory_space=pltpu.VMEM)
    return pl.pallas_call(
        functools.partial(prepare_kernel, points),
        out_shape=(
            jax.ShapeDtypeStruct((count, 48), BF16),
            jax.ShapeDtypeStruct((count, 8), F32),
            jax.ShapeDtypeStruct((count, 32), BF16),
        ),
        in_specs=[vmem],
        out_specs=[vmem] * 3,
        compiler_params=params(),
        name="prepare",
        cost_estimate=pl.CostEstimate(
            flops=200 * count, transcendentals=count, bytes_accessed=count * 1000
        ),
    )(vel_index)


def weighted(weights, first, second):
    over_rows = (((0,), (0,)), ((), ()))
    both = lax.dot_general(weights, first, over_rows, preferred_element_type=F32)
    rest = lax.dot_general(weights, second, over_rows, preferred_element_type=F32)
    return both[:16] + both[16:] + rest[:16]


def moment_kernel(size, side_ref, dist_ref, weight_ref, out_ref, lowest_ref):
    side = side_ref[0]
    step = pl.program_id(0)
    half_steps = pl.num_programs(0) // 2

    @pl.when(step == 0)
    def _():
        out_ref[...] = jnp.zeros_like(out_ref)

    @pl.when(jnp.where(step >= half_steps, 1, 0) == side)
    def _():
        lowest_ref[...] = dist_ref[strided(jnp.where(side == 1, 3, 0), size), :]

    for pair in range(0, STRIP_ROWS, 2):
        value = jnp.concatenate(
            [dist_ref[strided(row, size), :] for row in (pair, pair + 1)], axis=1
        )
        high = value.astype(BF16)
        out_ref[:, pair * LANES : (pair + 2) * LANES] += weighted(
            weight_ref[...], high, (value - high.astype(F32)).astype(BF16)
        )


def home_moments(side, flat, weights, size):
    count = flat.shape[0] // STRIP_ROWS
    width = STRIP_ROWS * LANES
    half_steps = count // size // 2
    return pl.pallas_call(
        functools.partial(moment_kernel, size),
        out_shape=(
            jax.ShapeDtypeStruct((16, width), F32),
            jax.ShapeDtypeStruct((count // 2, LANES), F32),
        ),
        grid_spec=pltpu.PrefetchScalarGridSpec(
            num_scalar_prefetch=1,
            grid=(2 * half_steps,),
            in_specs=[
                pl.BlockSpec((4 * size, LANES), lambda i, s: (i, 0)),
                pl.BlockSpec((size, 32), lambda i, s: (i, 0)),
            ],
            out_specs=[
                pl.BlockSpec((16, width), lambda i, s: (0, 0)),
                pl.BlockSpec(
                    (size, LANES), lambda i, s: (jnp.clip(i - s[0] * half_steps, 0, half_steps - 1), 0)
                ),
            ],
        ),
        compiler_params=params(),
        name="home_moments",
        cost_estimate=pl.CostEstimate(
            flops=2 * 64 * count * width, transcendentals=0, bytes_accessed=count * width * 4
        ),
    )(side, flat, weights)


def transport_kernel(size, second_pass, side_ref, *refs):
    if second_pass:
        (table_ref, change_ref, q_first, q_mid, q_edge, up_ref, down_ref, *rest) = refs
    else:
        (own_ref, got_ref, up_ref, down_ref, *rest) = refs
    (const_ref, weight_ref, cell_ref, sum_in_ref, *rest) = rest
    if second_pass:
        (near_out, far_out, sum_ref, lift_ref) = rest[-4:]
    else:
        (first_out, mid_out, edge_out, sum_ref) = rest[-4:]
    side = side_ref[0]
    group_size = 32 if size % 32 == 0 else 16

    @pl.when(pl.program_id(0) == 0)
    def _():
        sum_ref[...] = sum_in_ref[...]

    if second_pass:
        lift_ref[...] = jnp.dot(table_ref[...], change_ref[...], preferred_element_type=F32)

    def row_out(row):
        if second_pass:
            return near_out.at[row] if row < 4 else far_out.at[row - 4]
        if row == 0:
            return first_out
        return mid_out.at[row - 1] if row < 6 else edge_out.at[row - 6]

    lane = lax.broadcasted_iota(jnp.int32, (group_size, LANES), 1)
    inner_low = jnp.where(lane == 0, 0.0, 1.0)
    inner_high = jnp.where(lane == LANES - 1, 0.0, 1.0)

    def body(group, carry):
        base = pl.multiple_of(group * group_size, group_size)
        rows = pl.ds(base, group_size)

        def load(row):
            if row < 0:
                value = up_ref[row + 2, rows, :]
            elif row == 8:
                value = down_ref[rows, :]
            elif second_pass:
                if row == 0:
                    value = q_first[rows, :]
                elif row < 6:
                    value = q_mid[row - 1, rows, :]
                else:
                    value = q_edge[row - 6, rows, :]
            else:
                ref = own_ref if row < 4 else got_ref
                local = jnp.where(side == 1, 3 - row % 4, row % 4)
                value = ref[strided(base * STRIP_ROWS + local, group_size), :]
            if second_pass:
                value = value + lift_ref[rows, pl.ds((row + 2) * LANES, LANES)]
            return value

        def wide(column):
            return jnp.broadcast_to(const_ref[rows, column : column + 1], (group_size, LANES))

        speed_x = wide(0)
        speed_y = wide(1)
        half_sign = wide(2)
        forward = half_sign > 0.0
        open_end = jnp.where(forward, inner_low, inner_high)

        behind = load(-2)
        here = load(-1)
        ahead = load(0)
        step = ahead - here
        upwind = here + 0.5 * minmod(here - behind, step)
        here = ahead
        for row in range(BLOCK_ROWS):
            ahead = load(row + 1)
            next_step = ahead - here
            next_upwind = here + 0.5 * minmod(step, next_step)
            drift = speed_x * (next_upwind - upwind)
            step = next_step
            upwind = next_upwind
            left = here - pltpu.roll(here, 1, 1) * inner_low
            right = pltpu.roll(here, LANES - 1, 1) * inner_high - here
            face = here + half_sign * minmod(left, right)
            other = jnp.where(forward, pltpu.roll(face, 1, 1), pltpu.roll(face, LANES - 1, 1))
            drift = drift + speed_y * (face - other * open_end)
            keep = jnp.broadcast_to(cell_ref[row : row + 1, :], (group_size, LANES))
            fluid = jnp.broadcast_to(cell_ref[row + 8 : row + 9, :], (group_size, LANES))
            value = keep * here - fluid * drift
            row_out(row)[rows, :] = value
            here = ahead
        return carry

    lax.fori_loop(0, size // group_size, body, 0)
    for pair in range(0, BLOCK_ROWS, 2):
        value = jnp.concatenate([row_out(pair)[...], row_out(pair + 1)[...]], axis=1)
        high = value.astype(BF16)
        part = weighted(weight_ref[...], high, (value - high.astype(F32)).astype(BF16))
        for row in (pair, pair + 1):
            place = jnp.where(side == 1, 7 - row, row)
            columns = pl.ds(pl.multiple_of(place * LANES, LANES), LANES)
            sum_ref[:, columns] += part[:, (row - pair) * LANES : (row - pair + 1) * LANES]


def transport(
    side, sources, tables, cells, sums, half, chunk, first, size, change=None, skip=0, group=None, into=None
):
    second_pass = change is not None
    steps = chunk // size
    shift = half // size
    begin = first // size
    offset = skip // size
    table, const, weights = tables
    width = BLOCK_ROWS * LANES

    def mine(i, s):
        return s[0] * shift + begin + i

    def stack_of(count, at):
        return pl.BlockSpec((count, size, LANES), lambda i, s: (0, at + i, 0))

    aliases = {}
    if second_pass:
        args = [table, change]
        specs = [
            pl.BlockSpec((size, 48), lambda i, s: (mine(i, s), 0)),
            pl.BlockSpec(change.shape, lambda i, s: (0, 0)),
            stack_of(None, offset),
            stack_of(5, offset),
            stack_of(2, offset),
            stack_of(2, offset),
            stack_of(None, offset),
        ]
        outs = [jax.ShapeDtypeStruct((4, n, LANES), F32) for n in (half, chunk)]
        out_specs = [stack_of(4, begin), stack_of(4, 0)]
        scratch = [pltpu.VMEM((size, 11 * LANES), F32)]
    else:
        args = []
        specs = [
            pl.BlockSpec((4 * size, LANES), lambda i, s: (mine(i, s), 0)),
            pl.BlockSpec((4 * size, LANES), lambda i, s: (i, 0)),
            stack_of(2, 0),
            pl.BlockSpec((size, LANES), lambda i, s: (begin + i, 0)),
        ]
        outs = [jax.ShapeDtypeStruct((n, group, LANES), F32) for n in (1, 5, 2)]
        out_specs = [stack_of(None, offset), stack_of(5, offset), stack_of(2, offset)]
        scratch = []
    whole = pl.BlockSpec((16, width), lambda i, s: (0, 0))
    args = [side, *args, *sources, const, weights, cells, sums]
    specs = [
        *specs,
        pl.BlockSpec((size, 8), lambda i, s: (mine(i, s), 0)),
        pl.BlockSpec((size, 32), lambda i, s: (mine(i, s), 0)),
        pl.BlockSpec((16, LANES), lambda i, s: (0, 0)),
        whole,
    ]
    if into is not None:
        aliases = {len(args) + n: n for n in range(len(into))}
        args = [*args, *into]
        specs = [*specs, *[pl.BlockSpec(memory_space=pl.ANY)] * len(into)]
    return pl.pallas_call(
        functools.partial(transport_kernel, size, second_pass),
        out_shape=(*outs, jax.ShapeDtypeStruct((16, width), F32)),
        grid_spec=pltpu.PrefetchScalarGridSpec(
            num_scalar_prefetch=1,
            grid=(steps,),
            in_specs=specs,
            out_specs=[*out_specs, whole],
            scratch_shapes=scratch,
        ),
        input_output_aliases=aliases,
        compiler_params=params(),
        name="transport_second" if second_pass else "transport_first",
        cost_estimate=pl.CostEstimate(
            flops=60 * chunk * width, transcendentals=0, bytes_accessed=chunk * LANES * 4 * 19
        ),
    )(*args)


def sweep_block(inputs, relax, rate):
    start, flux_x, flux_y = inputs
    lane = lax.broadcasted_iota(jnp.int32, (8, LANES), 1)
    inner_low = jnp.where(lane == 0, 0.0, 1.0)
    inner_high = jnp.where(lane == LANES - 1, 0.0, 1.0)

    def block(array, row):
        if row < 0 or row >= SPAN:
            return jnp.zeros((8, LANES), F32)
        return array[:, row * LANES : (row + 1) * LANES]

    def lower(value):
        return pltpu.roll(value, 1, 1) * inner_low

    def upper(value):
        return pltpu.roll(value, LANES - 1, 1) * inner_high

    source = []
    for row in range(SPAN):
        diff_x = 0.5 * (block(flux_x, row + 1) - block(flux_x, row - 1))
        side = block(flux_y, row)
        diff_y = 0.5 * (upper(side) - lower(side))
        source.append(block(start, row) - SOURCE_WEIGHT * (diff_x + diff_y))
    zero = jnp.zeros((8, LANES), F32)
    kappa = [block(rate, row) for row in range(SPAN)]
    scale = [block(relax, row) for row in range(SPAN)]
    state = [block(start, row) for row in range(SPAN)]
    for _ in range(SWEEPS):
        near = [zero, *state, zero]
        state = [
            (source[row] + kappa[row] * (near[row] + near[row + 2] + lower(near[row + 1]) + upper(near[row + 1])))
            * scale[row]
            for row in range(SPAN)
        ]
    return jnp.concatenate(state, axis=1)


def stacked(value):
    first = value.astype(BF16)
    rest = value - first.astype(F32)
    second = rest.astype(BF16)
    third = (rest - second.astype(F32)).astype(BF16)
    return jnp.concatenate([first, second, third, first, second, first], axis=0)


def relax_rows(rate):
    inside = rate > 0.0
    kappa = jnp.where(inside, 0.5 / jnp.where(inside, rate, 1.0), 0.0)
    scale = jnp.where(inside, 1.0 / (1.0 + 4.0 * kappa), 0.0)
    width = rate.shape[1]
    return jnp.broadcast_to(kappa, (8, width)), jnp.broadcast_to(scale, (8, width))


def place_blocks(info_ref, span_ref, own, pair_a, pair_b):
    odd = info_ref[1]
    width = BLOCK_ROWS * LANES
    span_ref[:, width : 2 * width] = own
    place_a = pl.multiple_of((1 - odd) * 2 * width, width)
    place_b = pl.multiple_of(odd * 2 * width, width)
    span_ref[:, pl.ds(place_a, width)] = pair_a
    span_ref[:, pl.ds(place_b, width)] = pair_b


def first_macro_kernel(
    info_ref, sum_ref, sum_a_ref, sum_b_ref, near_ref, far_ref, gram_ref, mat_ref,
    change_ref, keep_ref, span_ref, home_ref,
):
    side = info_ref[0]
    odd = info_ref[1]
    width = BLOCK_ROWS * LANES
    part = STRIP_ROWS * LANES
    place_blocks(info_ref, span_ref, sum_ref[...], sum_a_ref[...], sum_b_ref[...])
    for ref, where in ((near_ref, side), (far_ref, 1 - side)):
        for index, block in enumerate((1, (1 - odd) * 2, odd * 2)):
            spot = pl.multiple_of(block * width + where * part, part)
            home_ref[:, pl.ds(spot, part)] = ref[index]
    home = home_ref[...]
    rate = home[13:14, :]
    ratio = jnp.where(home[14:15, :] > 0.5, 1.0, rate)
    mat = mat_ref[...]
    first = jnp.dot(mat, jnp.where(lax.broadcasted_iota(jnp.int32, home.shape, 0) < 13, home, 0.0), precision=HIGH)
    fields = first[:8] + first[24:]
    moments = span_ref[...] + ratio * jnp.dot(gram_ref[...], fields, precision=HIGH)
    all_parts = jnp.dot(mat, moments, precision=HIGH)
    start = all_parts[:8]
    kappa, scale = relax_rows(rate)
    state = sweep_block((start, all_parts[8:16], all_parts[16:24]), scale, kappa)
    change = ratio * fields + (state - start)
    span_ref[0:8, :] = change
    keep_ref[0:8, :] = state + all_parts[24:]
    keep_ref[8:9, :] = rate
    keep_ref[9:10, :] = ratio
    keep_ref[10:16, :] = jnp.zeros((6, SPAN * LANES), F32)
    for row in range(-2, 9):
        spot = jnp.where(side == 1, 15 - row, 8 + row)
        piece = span_ref[0:8, pl.ds(pl.multiple_of(spot * LANES, LANES), LANES)]
        change_ref[:, (row + 2) * LANES : (row + 3) * LANES] = stacked(piece)


def second_macro_kernel(
    info_ref, sum_ref, sum_a_ref, sum_b_ref, keep_ref, gram_ref, mat_ref,
    change_ref, state_ref, span_ref,
):
    side = info_ref[0]
    place_blocks(info_ref, span_ref, sum_ref[...], sum_a_ref[...], sum_b_ref[...])
    fields = keep_ref[0:8, :]
    rate = keep_ref[8:9, :]
    ratio = keep_ref[9:10, :]
    moments = span_ref[...] + ratio * jnp.dot(gram_ref[...], fields, precision=HIGH)
    all_parts = jnp.dot(mat_ref[...], moments, precision=HIGH)
    start = all_parts[:8]
    kappa, scale = relax_rows(rate)
    state = sweep_block((start, all_parts[8:16], all_parts[16:24]), scale, kappa)
    span_ref[0:8, :] = ratio * fields + (state - start)
    span_ref[8:16, :] = state
    part = STRIP_ROWS * LANES
    spot = pl.ds(pl.multiple_of(2 * part + side * part, part), part)
    change_ref[...] = stacked(span_ref[0:8, spot])
    state_ref[...] = span_ref[8:16, spot]


def macro(kernel, info, args, outs, scratch):
    vmem = pl.BlockSpec(memory_space=pltpu.VMEM)
    return pl.pallas_call(
        kernel,
        out_shape=outs,
        in_specs=[pl.BlockSpec(memory_space=pltpu.SMEM)] + [vmem] * len(args),
        out_specs=[vmem] * len(outs),
        scratch_shapes=scratch,
        compiler_params=params(),
        cost_estimate=pl.CostEstimate(flops=4000000, transcendentals=0, bytes_accessed=1000000),
    )(info, *args)


def finish_kernel(size, own, side_ref, rows_ref, table_ref, change_ref, *rest):
    out_ref = rest[-1]
    flipped = side_ref[0] == (1 if own else 0)
    lift = jnp.dot(table_ref[...], change_ref[...], preferred_element_type=F32)
    for row in range(STRIP_ROWS):
        index = jnp.where(flipped, 3 - row, row)
        out_ref[strided(row, size), :] = (
            rows_ref[index] + lift[:, row * LANES : (row + 1) * LANES]
        )


def finish(side, out, rows, own, table, change, half, chunk, first, size):
    shift = half // size
    begin = first // size

    def place(i, s):
        return (s[0] if own else 1 - s[0]) * shift + begin + i

    specs = [
        pl.BlockSpec((4, size, LANES), lambda i, s: (0, i, 0)),
        pl.BlockSpec((size, 48), lambda i, s: (place(i, s), 0)),
        pl.BlockSpec(change.shape, lambda i, s: (0, 0)),
    ]
    args = [side, rows, table, change]
    aliases = {}
    if out is not None:
        specs.append(pl.BlockSpec(memory_space=pl.ANY))
        args.append(out)
        aliases = {4: 0}
    return pl.pallas_call(
        functools.partial(finish_kernel, size, own),
        out_shape=jax.ShapeDtypeStruct((2 * half * STRIP_ROWS, LANES), F32),
        grid_spec=pltpu.PrefetchScalarGridSpec(
            num_scalar_prefetch=1,
            grid=(chunk // size,),
            in_specs=specs,
            out_specs=pl.BlockSpec((4 * size, LANES), lambda i, s: (place(i, s), 0)),
        ),
        input_output_aliases=aliases,
        compiler_params=params(),
        name="finish",
        cost_estimate=pl.CostEstimate(
            flops=2 * 48 * 4 * LANES * chunk, transcendentals=0, bytes_accessed=chunk * LANES * 4 * 8
        ),
    )(*args)


def per_device(points, dist, cell_type, collision_rate, vel_index):
    count, rows, cols = dist.shape
    half = count // 2
    strips = lax.axis_size("strip")
    groups = lax.axis_size("vel")
    strip = lax.axis_index("strip")
    size, chunks = plan(half)
    firsts = [sum(chunks[:c]) for c in range(len(chunks))]
    order = range(len(chunks))
    later, cut = second_order(len(chunks))
    groups_of = [order[:cut], order[cut:]]
    side = (strip % 2).astype(jnp.int32).reshape(1)
    info = jnp.stack([strip % 2, (strip // 2) % 2]).astype(jnp.int32)

    swap_pairs = [(s, s ^ 1) for s in range(strips)]
    down_pairs = [
        (s, s + (2 if s % 2 == 0 else -2))
        for s in range(strips)
        if 0 <= s + (2 if s % 2 == 0 else -2) < strips
    ]
    up_pairs = [(b, a) for a, b in down_pairs]
    pair_a = [
        (s, s + (2 if (s // 2) % 2 == 0 else -2))
        for s in range(strips)
        if 0 <= s + (2 if (s // 2) % 2 == 0 else -2) < strips
    ]
    pair_b = [
        (s, s + (-2 if (s // 2) % 2 == 0 else 2))
        for s in range(strips)
        if 0 <= s + (-2 if (s // 2) % 2 == 0 else 2) < strips
    ]

    def swap(value):
        return lax.ppermute(value, "strip", swap_pairs)

    def with_flow(value):
        return lax.ppermute(value, "strip", down_pairs)

    def against_flow(value):
        return lax.ppermute(value, "strip", up_pairs)

    def both_z(value):
        return lax.ppermute(value, "strip", pair_a), lax.ppermute(value, "strip", pair_b)

    def sum_groups(value):
        total = value
        for shift in range(1, groups):
            total = total + lax.ppermute(
                value, "vel", [(g, (g + shift) % groups) for g in range(groups)]
            )
        return total

    flat = dist.reshape(count * rows, cols)
    wall = (cell_type == 1).astype(F32)
    cell_pair = jnp.concatenate([collision_rate, wall])
    other_cells = swap(cell_pair)

    got = []
    for c in order:
        far_start = ((1 - strip % 2) * half + firsts[c]) * rows
        part = lax.dynamic_slice_in_dim(flat, far_start, chunks[c] * rows, axis=0)
        got.append(swap(part))
    tables = prepare(points, vel_index)
    table, _, weights = tables
    home, lowest = home_moments(side, flat, weights, size)
    below = against_flow(lowest)
    gram = jnp.asarray(target_moments(points))
    mat = jnp.asarray(macro_matrix())

    def flow(own, other):
        odd = strip % 2 == 1
        return jnp.concatenate(
            [jnp.where(odd, own[::-1], own), jnp.where(odd, other[::-1], other)]
        )

    flow_rate = flow(collision_rate, other_cells[:rows])
    flow_fluid = 1.0 - flow(wall, other_cells[rows:])
    cells = jnp.concatenate([flow_fluid * (1.0 - flow_rate), flow_fluid])

    home = sum_groups(home)
    home = jnp.concatenate(
        [home[:13], collision_rate.reshape(1, -1), wall.reshape(1, -1), jnp.zeros((1, rows * cols), F32)]
    )
    near_home = jnp.stack([home, *both_z(home)])
    far_home = swap(near_home)

    width = BLOCK_ROWS * LANES
    sums = jnp.zeros((16, width), F32)
    above = []
    for c in order:
        edges = pick(side, got[c], lambda s: 0, chunks[c], size, [(2, 1), (3, 0)])
        above.append(with_flow(edges))
    kept = []
    for number, members in enumerate(groups_of):
        start = firsts[members[0]]
        length = sum(chunks[c] for c in members)
        held = None
        for c in members:
            *held, sums = transport(
                side, [flat, got[c], above[c], below], tables, cells, sums, half,
                chunks[c], firsts[c], size, skip=firsts[c] - start, group=length, into=held,
            )
        next_above = with_flow(held[2])
        next_below = against_flow(held[0])
        kept.append((*held, next_above, next_below))

    total = sum_groups(sums)
    total = total + swap(total)
    sum_a, sum_b = both_z(total)
    change, keep = macro(
        first_macro_kernel, info,
        [total, sum_a, sum_b, near_home, far_home, gram, mat],
        [
            jax.ShapeDtypeStruct((48, 11 * LANES), BF16),
            jax.ShapeDtypeStruct((16, SPAN * LANES), F32),
        ],
        [pltpu.VMEM((16, SPAN * LANES), F32)] * 2,
    )

    sums = jnp.zeros((16, width), F32)
    near, back = None, {}
    for c in later:
        number = int(c >= cut)
        start = firsts[groups_of[number][0]]
        near, far, sums = transport(
            side, list(kept[number]), tables, cells, sums, half,
            chunks[c], firsts[c], size, change, skip=firsts[c] - start,
            into=None if near is None else [near],
        )
        back[c] = swap(far)
    total = sum_groups(sums)
    total = total + swap(total)
    sum_a, sum_b = both_z(total)
    change, state = macro(
        second_macro_kernel, info,
        [total, sum_a, sum_b, keep, gram, mat],
        [
            jax.ShapeDtypeStruct((48, STRIP_ROWS * LANES), BF16),
            jax.ShapeDtypeStruct((8, STRIP_ROWS * LANES), F32),
        ],
        [pltpu.VMEM((16, SPAN * LANES), F32)],
    )
    out = finish(side, None, near, True, table, change, half, half, 0, size)
    for c in later:
        out = finish(side, out, back[c], False, table, change, half, chunks[c], firsts[c], size)
    return out.reshape(dist.shape), state[:5].reshape(5, rows, cols)


def solution(mesh):
    def whole(dist, cell_type, collision_rate, vel_index):
        points = round(vel_index.shape[1] ** (1.0 / 3.0))
        in_specs = (P("vel", "strip", None), P("strip", None), P("strip", None), P(None, "vel"))
        out_specs = (P("vel", "strip", None), P(None, "strip", None))

        def body(*args):
            return per_device(points, *args)

        run = jax.shard_map(
            body, mesh=mesh, in_specs=in_specs, out_specs=out_specs, check_vma=False
        )
        return run(dist, cell_type, collision_rate, vel_index)

    return whole
```

```python
import functools
import math

import jax
import jax.numpy as jnp
import numpy as np
from jax import lax
from jax.experimental import pallas as pl
from jax.experimental.pallas import tpu as pltpu
from jax.sharding import PartitionSpec as P


STEP_RATIO = 0.1
SOURCE_WEIGHT = 0.5
HEAT_WEIGHT = 4.0 / 15.0
SWEEPS = 3
HIGH = lax.Precision.HIGHEST
LANES = 128
STRIP_ROWS = 4
BLOCK_ROWS = 2 * STRIP_ROWS
SPAN = 3 * BLOCK_ROWS
F32 = jnp.float32
BF16 = jnp.bfloat16


def params(**more):
    return pltpu.CompilerParams(vmem_limit_bytes=62 * 1024 * 1024, **more)


def plan(half):
    block = 288 if half % 288 == 0 else 144
    blocks = half // block
    if blocks % 6 == 0:
        unit = block * (blocks // 6)
        return block, [2 * unit, unit, unit, unit, unit]
    return block, [block * (blocks - 2), block, block]


def second_order(pieces):
    cut = (pieces + 1) // 2
    return [*range(1, cut), 0, *range(cut, pieces)], cut


def moment_rows(vel_x, vel_y, vel_z, volume, lib):
    energy = vel_x * vel_x + vel_y * vel_y + vel_z * vel_z
    weight = volume * math.pi ** (-1.5) * lib.exp(-energy)
    rows = [
        lib.ones_like(vel_x),
        vel_x,
        vel_y,
        vel_z,
        energy,
        vel_x * vel_x,
        vel_y * vel_y,
        vel_x * vel_y,
        vel_x * vel_z,
        vel_y * vel_z,
        energy * vel_x,
        energy * vel_y,
        energy * vel_z,
    ]
    return lib.concatenate([(row * weight).reshape(1, -1) for row in rows])


def state_rows(vel_x, vel_y, vel_z, lib):
    energy = vel_x * vel_x + vel_y * vel_y + vel_z * vel_z
    shape_heat = HEAT_WEIGHT * (energy - 2.5)
    rows = [
        lib.ones_like(vel_x),
        2.0 * vel_x,
        2.0 * vel_y,
        2.0 * vel_z,
        energy - 1.5,
        shape_heat * vel_x,
        shape_heat * vel_y,
        shape_heat * vel_z,
    ]
    return lib.concatenate([row.reshape(1, -1) for row in rows])


def target_moments(points):
    line = (np.arange(points) - (points - 1) / 2.0) * (8.0 / points)
    comps = [a.reshape(-1) for a in np.meshgrid(line, line, line, indexing="ij")]
    gram = moment_rows(*comps, (8.0 / points) ** 3, np) @ state_rows(*comps, np).T
    gram[np.abs(gram) < 1e-12] = 0.0
    full = np.zeros((16, 8), np.float32)
    full[:13] = gram
    return full


def macro_matrix():
    third = 2.0 / 3.0
    unit = np.eye(16, dtype=np.float64)
    start = [unit[0], unit[1], unit[2], unit[3], third * unit[4] - unit[0]]
    heat = [unit[10] - 2.5 * unit[1], unit[11] - 2.5 * unit[2], unit[12] - 2.5 * unit[3]]
    flux = [
        unit[1],
        unit[2],
        2.0 * unit[5] - third * unit[4],
        2.0 * unit[7],
        2.0 * unit[6] - third * unit[4],
        2.0 * unit[8],
        2.0 * unit[9],
        heat[0],
        heat[1],
    ]
    out = np.zeros((32, 16), np.float64)
    for row in range(5):
        out[row] = start[row]
        out[8 + row] = flux[(0, 2, 3, 5, 7)[row]]
        out[16 + row] = flux[(1, 3, 4, 6, 8)[row]]
    for row in range(3):
        out[24 + 5 + row] = heat[row]
    return out.astype(np.float32)


def minmod(left, right):
    return jnp.maximum(jnp.minimum(right, jnp.maximum(left, 0.0)), jnp.minimum(left, 0.0))


def strided(start, count):
    return pl.ds(start, count, stride=STRIP_ROWS)


def pack_kernel(size, begins, counts, side_ref, far_ref, *rest):
    outs = rest[-2 * len(begins) :]
    side = side_ref[0]
    step = pl.program_id(0)
    for c, (begin, count) in enumerate(zip(begins, counts)):

        @pl.when((step >= begin) & (step < begin + count))
        def _():
            for i in range(STRIP_ROWS):
                row = jnp.where(side == 1, i, 3 - i)
                outs[2 * c + (1 if i < 2 else 0)][i % 2] = far_ref[strided(row, size), :]


def pack(side, flat, half, chunks, first, size):
    counts = [n // size for n in chunks]
    begins = [sum(counts[:c]) for c in range(len(chunks))]
    shift = half // size
    start = first // size

    def out_spec(c):
        return pl.BlockSpec(
            (2, size, LANES), lambda i, s: (0, jnp.clip(i - begins[c], 0, counts[c] - 1), 0)
        )

    outs = pl.pallas_call(
        functools.partial(pack_kernel, size, begins, counts),
        out_shape=[
            jax.ShapeDtypeStruct((2, n, LANES), F32) for n in chunks for _ in range(2)
        ],
        grid_spec=pltpu.PrefetchScalarGridSpec(
            num_scalar_prefetch=1,
            grid=(sum(counts),),
            in_specs=[
                pl.BlockSpec((4 * size, LANES), lambda i, s: ((1 - s[0]) * shift + start + i, 0))
            ],
            out_specs=[out_spec(c) for c in range(len(chunks)) for _ in range(2)],
        ),
        compiler_params=params(),
        name="pack",
        cost_estimate=pl.CostEstimate(
            flops=0, transcendentals=0, bytes_accessed=sum(chunks) * LANES * 4 * 8
        ),
    )(side, flat)
    return [(outs[2 * c], outs[2 * c + 1]) for c in range(len(chunks))]


def prepare_kernel(points, vel_ref, table_ref, const_ref, weight_ref):
    comps = (vel_ref[...].astype(F32) - (points - 1) / 2.0) * (8.0 / points)
    vel_x, vel_y, vel_z = comps[0:1], comps[1:2], comps[2:3]
    moments = moment_rows(vel_x, vel_y, vel_z, (8.0 / points) ** 3, jnp)
    high = moments.astype(BF16).astype(F32)
    shapes = state_rows(vel_x, vel_y, vel_z, jnp)
    part_a = shapes.astype(BF16).astype(F32)
    part_b = (shapes - part_a).astype(BF16).astype(F32)
    part_c = shapes - part_a - part_b
    width = vel_x.shape[1]
    rows = jnp.concatenate(
        [
            *[part_a] * 3,
            *[part_b] * 2,
            part_c,
            high,
            jnp.zeros((3, width), F32),
            moments - high,
            jnp.zeros((3, width), F32),
            STEP_RATIO * jnp.abs(vel_x),
            STEP_RATIO * jnp.abs(vel_y),
            jnp.where(vel_y > 0, 0.5, -0.5),
            jnp.zeros((45, width), F32),
        ]
    )
    columns = rows.T
    table_ref[...] = columns[:, :48].astype(BF16)
    weight_ref[...] = columns[:, 48:80].astype(BF16)
    const_ref[...] = columns[:, 80:88]


def prepare(points, vel_index):
    count = vel_index.shape[1]
    vmem = pl.BlockSpec(memory_space=pltpu.VMEM)
    return pl.pallas_call(
        functools.partial(prepare_kernel, points),
        out_shape=(
            jax.ShapeDtypeStruct((count, 48), BF16),
            jax.ShapeDtypeStruct((count, 8), F32),
            jax.ShapeDtypeStruct((count, 32), BF16),
        ),
        in_specs=[vmem],
        out_specs=[vmem] * 3,
        compiler_params=params(),
        name="prepare",
        cost_estimate=pl.CostEstimate(
            flops=200 * count, transcendentals=count, bytes_accessed=count * 1000
        ),
    )(vel_index)


def weighted(weight_ref, values):
    over_rows = (((0,), (0,)), ((), ()))
    total = None
    for start in range(0, weight_ref.shape[0], 144):
        weights = weight_ref[start : start + 144, :]
        value = jnp.concatenate(values(start), axis=1)
        high = value.astype(BF16)
        low = (value - high.astype(F32)).astype(BF16)
        both = lax.dot_general(weights, high, over_rows, preferred_element_type=F32)
        rest = lax.dot_general(weights, low, over_rows, preferred_element_type=F32)
        part = both[:16] + both[16:] + rest[:16]
        total = part if total is None else total + part
    return total


def moment_kernel(size, side_ref, dist_ref, weight_ref, out_ref, lowest_ref):
    side = side_ref[0]
    step = pl.program_id(0)
    half_steps = pl.num_programs(0) // 2

    @pl.when(step == 0)
    def _():
        out_ref[...] = jnp.zeros_like(out_ref)

    @pl.when(jnp.where(step >= half_steps, 1, 0) == side)
    def _():
        lowest_ref[...] = dist_ref[strided(jnp.where(side == 1, 3, 0), size), :]

    for pair in range(0, STRIP_ROWS, 2):
        def values(start, pair=pair):
            return [
                dist_ref[strided(STRIP_ROWS * start + row, 144), :] for row in (pair, pair + 1)
            ]

        out_ref[:, pair * LANES : (pair + 2) * LANES] += weighted(weight_ref, values)


def home_moments(side, flat, weights, size):
    count = flat.shape[0] // STRIP_ROWS
    width = STRIP_ROWS * LANES
    half_steps = count // size // 2
    return pl.pallas_call(
        functools.partial(moment_kernel, size),
        out_shape=(
            jax.ShapeDtypeStruct((16, width), F32),
            jax.ShapeDtypeStruct((count // 2, LANES), F32),
        ),
        grid_spec=pltpu.PrefetchScalarGridSpec(
            num_scalar_prefetch=1,
            grid=(2 * half_steps,),
            in_specs=[
                pl.BlockSpec((4 * size, LANES), lambda i, s: (i, 0)),
                pl.BlockSpec((size, 32), lambda i, s: (i, 0)),
            ],
            out_specs=[
                pl.BlockSpec((16, width), lambda i, s: (0, 0)),
                pl.BlockSpec(
                    (size, LANES), lambda i, s: (jnp.clip(i - s[0] * half_steps, 0, half_steps - 1), 0)
                ),
            ],
        ),
        compiler_params=params(),
        name="home_moments",
        cost_estimate=pl.CostEstimate(
            flops=2 * 64 * count * width, transcendentals=0, bytes_accessed=count * width * 4
        ),
    )(side, flat, weights)


def transport_kernel(size, second_pass, side_ref, *refs):
    if second_pass:
        (table_ref, change_ref, q_first, q_mid, q_edge, up_ref, down_ref, *rest) = refs
    else:
        (own_ref, mid_ref, edge_ref, up_ref, down_ref, *rest) = refs
    (const_ref, weight_ref, cell_ref, sum_in_ref, *rest) = rest
    if second_pass:
        (near_out, far_out, sum_ref, lift_ref) = rest[-4:]
    else:
        (first_out, mid_out, edge_out, sum_ref) = rest[-4:]
    side = side_ref[0]
    group_size = 32 if size % 32 == 0 else 16

    @pl.when(pl.program_id(0) == 0)
    def _():
        sum_ref[...] = sum_in_ref[...]

    if second_pass:
        lift_ref[...] = jnp.dot(table_ref[...], change_ref[...], preferred_element_type=F32)

    def row_out(row):
        if second_pass:
            return near_out.at[row] if row < 4 else far_out.at[row - 4]
        if row == 0:
            return first_out
        return mid_out.at[row - 1] if row < 6 else edge_out.at[row - 6]

    lane = lax.broadcasted_iota(jnp.int32, (group_size, LANES), 1)
    inner_low = jnp.where(lane == 0, 0.0, 1.0)
    inner_high = jnp.where(lane == LANES - 1, 0.0, 1.0)

    def body(group, carry):
        base = pl.multiple_of(group * group_size, group_size)
        rows = pl.ds(base, group_size)

        def load(row):
            if row < 0:
                value = up_ref[row + 2, rows, :]
            elif row == 8:
                value = down_ref[rows, :]
            elif second_pass:
                if row == 0:
                    value = q_first[rows, :]
                elif row < 6:
                    value = q_mid[row - 1, rows, :]
                else:
                    value = q_edge[row - 6, rows, :]
            elif row < 4:
                local = jnp.where(side == 1, 3 - row, row)
                value = own_ref[strided(base * STRIP_ROWS + local, group_size), :]
            elif row < 6:
                value = mid_ref[row - 4, rows, :]
            else:
                value = edge_ref[row - 6, rows, :]
            if second_pass:
                value = value + lift_ref[rows, pl.ds((row + 2) * LANES, LANES)]
            return value

        def wide(column):
            return jnp.broadcast_to(const_ref[rows, column : column + 1], (group_size, LANES))

        speed_x = wide(0)
        speed_y = wide(1)
        half_sign = wide(2)
        forward = half_sign > 0.0
        open_end = jnp.where(forward, inner_low, inner_high)

        behind = load(-2)
        here = load(-1)
        ahead = load(0)
        step = ahead - here
        upwind = here + 0.5 * minmod(here - behind, step)
        here = ahead
        for row in range(BLOCK_ROWS):
            ahead = load(row + 1)
            next_step = ahead - here
            next_upwind = here + 0.5 * minmod(step, next_step)
            drift = speed_x * (next_upwind - upwind)
            step = next_step
            upwind = next_upwind
            left = here - pltpu.roll(here, 1, 1) * inner_low
            right = pltpu.roll(here, LANES - 1, 1) * inner_high - here
            face = here + half_sign * minmod(left, right)
            other = jnp.where(forward, pltpu.roll(face, 1, 1), pltpu.roll(face, LANES - 1, 1))
            drift = drift + speed_y * (face - other * open_end)
            keep = jnp.broadcast_to(cell_ref[row : row + 1, :], (group_size, LANES))
            fluid = jnp.broadcast_to(cell_ref[row + 8 : row + 9, :], (group_size, LANES))
            value = keep * here - fluid * drift
            row_out(row)[rows, :] = value
            here = ahead
        return carry

    lax.fori_loop(0, size // group_size, body, 0)
    for pair in range(0, BLOCK_ROWS, 2):
        def values(start, pair=pair):
            return [row_out(row)[start : start + 144, :] for row in (pair, pair + 1)]

        part = weighted(weight_ref, values)
        for row in (pair, pair + 1):
            place = jnp.where(side == 1, 7 - row, row)
            columns = pl.ds(pl.multiple_of(place * LANES, LANES), LANES)
            sum_ref[:, columns] += part[:, (row - pair) * LANES : (row - pair + 1) * LANES]


def transport(
    side, sources, tables, cells, sums, half, chunk, first, size, change=None, skip=0, group=None, into=None
):
    second_pass = change is not None
    steps = chunk // size
    shift = half // size
    begin = first // size
    offset = skip // size
    table, const, weights = tables
    width = BLOCK_ROWS * LANES

    def mine(i, s):
        return s[0] * shift + begin + i

    def stack_of(count, at):
        return pl.BlockSpec((count, size, LANES), lambda i, s: (0, at + i, 0))

    aliases = {}
    if second_pass:
        args = [table, change]
        specs = [
            pl.BlockSpec((size, 48), lambda i, s: (mine(i, s), 0)),
            pl.BlockSpec(change.shape, lambda i, s: (0, 0)),
            stack_of(None, offset),
            stack_of(5, offset),
            stack_of(2, offset),
            stack_of(2, offset),
            stack_of(None, offset),
        ]
        outs = [jax.ShapeDtypeStruct((4, n, LANES), F32) for n in (half, chunk)]
        out_specs = [stack_of(4, begin), stack_of(4, 0)]
        scratch = [pltpu.VMEM((size, 11 * LANES), F32)]
    else:
        args = []
        specs = [
            pl.BlockSpec((4 * size, LANES), lambda i, s: (mine(i, s), 0)),
            stack_of(2, 0),
            stack_of(2, 0),
            stack_of(2, 0),
            pl.BlockSpec((size, LANES), lambda i, s: (begin + i, 0)),
        ]
        outs = [jax.ShapeDtypeStruct((n, group, LANES), F32) for n in (1, 5, 2)]
        out_specs = [stack_of(None, offset), stack_of(5, offset), stack_of(2, offset)]
        scratch = []
    whole = pl.BlockSpec((16, width), lambda i, s: (0, 0))
    args = [side, *args, *sources, const, weights, cells, sums]
    specs = [
        *specs,
        pl.BlockSpec((size, 8), lambda i, s: (mine(i, s), 0)),
        pl.BlockSpec((size, 32), lambda i, s: (mine(i, s), 0)),
        pl.BlockSpec((16, LANES), lambda i, s: (0, 0)),
        whole,
    ]
    if into is not None:
        aliases = {len(args) + n: n for n in range(len(into))}
        args = [*args, *into]
        specs = [*specs, *[pl.BlockSpec(memory_space=pl.ANY)] * len(into)]
    return pl.pallas_call(
        functools.partial(transport_kernel, size, second_pass),
        out_shape=(*outs, jax.ShapeDtypeStruct((16, width), F32)),
        grid_spec=pltpu.PrefetchScalarGridSpec(
            num_scalar_prefetch=1,
            grid=(steps,),
            in_specs=specs,
            out_specs=[*out_specs, whole],
            scratch_shapes=scratch,
        ),
        input_output_aliases=aliases,
        compiler_params=params(),
        name="transport_second" if second_pass else "transport_first",
        cost_estimate=pl.CostEstimate(
            flops=60 * chunk * width, transcendentals=0, bytes_accessed=chunk * LANES * 4 * 19
        ),
    )(*args)


def sweep_block(inputs, relax, rate):
    start, flux_x, flux_y = inputs
    lane = lax.broadcasted_iota(jnp.int32, (8, LANES), 1)
    inner_low = jnp.where(lane == 0, 0.0, 1.0)
    inner_high = jnp.where(lane == LANES - 1, 0.0, 1.0)

    def block(array, row):
        if row < 0 or row >= SPAN:
            return jnp.zeros((8, LANES), F32)
        return array[:, row * LANES : (row + 1) * LANES]

    def lower(value):
        return pltpu.roll(value, 1, 1) * inner_low

    def upper(value):
        return pltpu.roll(value, LANES - 1, 1) * inner_high

    source = []
    for row in range(SPAN):
        diff_x = 0.5 * (block(flux_x, row + 1) - block(flux_x, row - 1))
        side = block(flux_y, row)
        diff_y = 0.5 * (upper(side) - lower(side))
        source.append(block(start, row) - SOURCE_WEIGHT * (diff_x + diff_y))
    zero = jnp.zeros((8, LANES), F32)
    kappa = [block(rate, row) for row in range(SPAN)]
    scale = [block(relax, row) for row in range(SPAN)]
    state = [block(start, row) for row in range(SPAN)]
    for _ in range(SWEEPS):
        near = [zero, *state, zero]
        state = [
            (source[row] + kappa[row] * (near[row] + near[row + 2] + lower(near[row + 1]) + upper(near[row + 1])))
            * scale[row]
            for row in range(SPAN)
        ]
    return jnp.concatenate(state, axis=1)


def stacked(value):
    first = value.astype(BF16)
    rest = value - first.astype(F32)
    second = rest.astype(BF16)
    third = (rest - second.astype(F32)).astype(BF16)
    return jnp.concatenate([first, second, third, first, second, first], axis=0)


def relax_rows(rate):
    inside = rate > 0.0
    kappa = jnp.where(inside, 0.5 / jnp.where(inside, rate, 1.0), 0.0)
    scale = jnp.where(inside, 1.0 / (1.0 + 4.0 * kappa), 0.0)
    width = rate.shape[1]
    return jnp.broadcast_to(kappa, (8, width)), jnp.broadcast_to(scale, (8, width))


def place_blocks(info_ref, span_ref, own, pair_a, pair_b):
    odd = info_ref[1]
    width = BLOCK_ROWS * LANES
    span_ref[:, width : 2 * width] = own
    place_a = pl.multiple_of((1 - odd) * 2 * width, width)
    place_b = pl.multiple_of(odd * 2 * width, width)
    span_ref[:, pl.ds(place_a, width)] = pair_a
    span_ref[:, pl.ds(place_b, width)] = pair_b


def first_macro_kernel(
    info_ref, sum_ref, sum_a_ref, sum_b_ref, near_ref, far_ref, gram_ref, mat_ref,
    change_ref, keep_ref, span_ref, home_ref,
):
    side = info_ref[0]
    odd = info_ref[1]
    width = BLOCK_ROWS * LANES
    part = STRIP_ROWS * LANES
    place_blocks(info_ref, span_ref, sum_ref[...], sum_a_ref[...], sum_b_ref[...])
    for ref, where in ((near_ref, side), (far_ref, 1 - side)):
        for index, block in enumerate((1, (1 - odd) * 2, odd * 2)):
            spot = pl.multiple_of(block * width + where * part, part)
            home_ref[:, pl.ds(spot, part)] = ref[index]
    home = home_ref[...]
    rate = home[13:14, :]
    ratio = jnp.where(home[14:15, :] > 0.5, 1.0, rate)
    mat = mat_ref[...]
    first = jnp.dot(mat, jnp.where(lax.broadcasted_iota(jnp.int32, home.shape, 0) < 13, home, 0.0), precision=HIGH)
    fields = first[:8] + first[24:]
    moments = span_ref[...] + ratio * jnp.dot(gram_ref[...], fields, precision=HIGH)
    all_parts = jnp.dot(mat, moments, precision=HIGH)
    start = all_parts[:8]
    kappa, scale = relax_rows(rate)
    state = sweep_block((start, all_parts[8:16], all_parts[16:24]), scale, kappa)
    change = ratio * fields + (state - start)
    span_ref[0:8, :] = change
    keep_ref[0:8, :] = state + all_parts[24:]
    keep_ref[8:9, :] = rate
    keep_ref[9:10, :] = ratio
    keep_ref[10:16, :] = jnp.zeros((6, SPAN * LANES), F32)
    for row in range(-2, 9):
        spot = jnp.where(side == 1, 15 - row, 8 + row)
        piece = span_ref[0:8, pl.ds(pl.multiple_of(spot * LANES, LANES), LANES)]
        change_ref[:, (row + 2) * LANES : (row + 3) * LANES] = stacked(piece)


def second_macro_kernel(
    info_ref, sum_ref, sum_a_ref, sum_b_ref, keep_ref, gram_ref, mat_ref,
    change_ref, state_ref, span_ref,
):
    side = info_ref[0]
    place_blocks(info_ref, span_ref, sum_ref[...], sum_a_ref[...], sum_b_ref[...])
    fields = keep_ref[0:8, :]
    rate = keep_ref[8:9, :]
    ratio = keep_ref[9:10, :]
    moments = span_ref[...] + ratio * jnp.dot(gram_ref[...], fields, precision=HIGH)
    all_parts = jnp.dot(mat_ref[...], moments, precision=HIGH)
    start = all_parts[:8]
    kappa, scale = relax_rows(rate)
    state = sweep_block((start, all_parts[8:16], all_parts[16:24]), scale, kappa)
    span_ref[0:8, :] = ratio * fields + (state - start)
    span_ref[8:16, :] = state
    part = STRIP_ROWS * LANES
    spot = pl.ds(pl.multiple_of(2 * part + side * part, part), part)
    change_ref[...] = stacked(span_ref[0:8, spot])
    state = span_ref[8:16, spot]
    for row in range(STRIP_ROWS):
        state_ref[:, row, :] = state[:5, row * LANES : (row + 1) * LANES]


def macro(kernel, info, args, outs, scratch):
    vmem = pl.BlockSpec(memory_space=pltpu.VMEM)
    return pl.pallas_call(
        kernel,
        out_shape=outs,
        in_specs=[pl.BlockSpec(memory_space=pltpu.SMEM)] + [vmem] * len(args),
        out_specs=[vmem] * len(outs),
        scratch_shapes=scratch,
        compiler_params=params(),
        cost_estimate=pl.CostEstimate(flops=4000000, transcendentals=0, bytes_accessed=1000000),
    )(info, *args)


def finish_kernel(size, parts, side_ref, *refs):
    out_ref = refs[-1]
    rows = refs[: len(parts)]
    table_ref, change_ref = refs[len(parts) : len(parts) + 2]
    side = side_ref[0]
    step = pl.program_id(0)
    lift = jnp.dot(table_ref[...], change_ref[...], preferred_element_type=F32)
    for ref, (own, begin, count, _) in zip(rows, parts):

        @pl.when((step >= begin) & (step < begin + count))
        def _(ref=ref, flipped=(side == (1 if own else 0))):
            for row in range(STRIP_ROWS):
                index = jnp.where(flipped, 3 - row, row)
                out_ref[strided(row, size), :] = (
                    ref[index] + lift[:, row * LANES : (row + 1) * LANES]
                )


def finish(side, out, pieces, table, change, half, size):
    shift = half // size
    parts = []
    steps = 0
    for rows, own, first in pieces:
        count = rows.shape[1] // size
        parts.append((own, steps, count, first // size))
        steps += count

    def place(i, s):
        spot = 0
        for own, begin, count, at in parts:
            here = (s[0] if own else 1 - s[0]) * shift + at + i - begin
            spot = jnp.where(i >= begin, here, spot)
        return spot

    def rows_spec(begin, count):
        return pl.BlockSpec(
            (4, size, LANES), lambda i, s: (0, jnp.clip(i - begin, 0, count - 1), 0)
        )

    specs = [
        *[rows_spec(begin, count) for _, begin, count, _ in parts],
        pl.BlockSpec((size, 48), lambda i, s: (place(i, s), 0)),
        pl.BlockSpec(change.shape, lambda i, s: (0, 0)),
    ]
    args = [side, *[rows for rows, _, _ in pieces], table, change]
    aliases = {}
    if out is not None:
        specs.append(pl.BlockSpec(memory_space=pl.ANY))
        aliases = {len(args): 0}
        args.append(out)
    return pl.pallas_call(
        functools.partial(finish_kernel, size, parts),
        out_shape=jax.ShapeDtypeStruct((2 * half * STRIP_ROWS, LANES), F32),
        grid_spec=pltpu.PrefetchScalarGridSpec(
            num_scalar_prefetch=1,
            grid=(steps,),
            in_specs=specs,
            out_specs=pl.BlockSpec((4 * size, LANES), lambda i, s: (place(i, s), 0)),
        ),
        input_output_aliases=aliases,
        compiler_params=params(),
        name="finish",
        cost_estimate=pl.CostEstimate(
            flops=2 * 48 * 4 * LANES * steps * size,
            transcendentals=0,
            bytes_accessed=steps * size * LANES * 4 * 8,
        ),
    )(*args)


def per_device(points, dist, cell_type, collision_rate, vel_index):
    count, rows, cols = dist.shape
    half = count // 2
    strips = lax.axis_size("strip")
    groups = lax.axis_size("vel")
    strip = lax.axis_index("strip")
    size, chunks = plan(half)
    firsts = [sum(chunks[:c]) for c in range(len(chunks))]
    order = range(len(chunks))
    later, cut = second_order(len(chunks))
    groups_of = [order[:cut], order[cut:]]
    side = (strip % 2).astype(jnp.int32).reshape(1)
    info = jnp.stack([strip % 2, (strip // 2) % 2]).astype(jnp.int32)

    swap_pairs = [(s, s ^ 1) for s in range(strips)]
    down_pairs = [
        (s, s + (2 if s % 2 == 0 else -2))
        for s in range(strips)
        if 0 <= s + (2 if s % 2 == 0 else -2) < strips
    ]
    up_pairs = [(b, a) for a, b in down_pairs]
    pair_a = [
        (s, s + (2 if (s // 2) % 2 == 0 else -2))
        for s in range(strips)
        if 0 <= s + (2 if (s // 2) % 2 == 0 else -2) < strips
    ]
    pair_b = [
        (s, s + (-2 if (s // 2) % 2 == 0 else 2))
        for s in range(strips)
        if 0 <= s + (-2 if (s // 2) % 2 == 0 else 2) < strips
    ]

    def swap(value):
        return lax.ppermute(value, "strip", swap_pairs)

    def with_flow(value):
        return lax.ppermute(value, "strip", down_pairs)

    def against_flow(value):
        return lax.ppermute(value, "strip", up_pairs)

    def both_z(value):
        return lax.ppermute(value, "strip", pair_a), lax.ppermute(value, "strip", pair_b)

    def sum_groups(value):
        total = value
        for shift in range(1, groups):
            total = total + lax.ppermute(
                value, "vel", [(g, (g + shift) % groups) for g in range(groups)]
            )
        return total

    flat = dist.reshape(count * rows, cols)
    wall = (cell_type == 1).astype(F32)
    cell_pair = jnp.concatenate([collision_rate, wall])
    other_cells = swap(cell_pair)

    packed = pack(side, flat, half, chunks[:1], 0, size)
    packed += pack(side, flat, half, chunks[1:], firsts[1], size)
    got, above = [], []
    for edge, mid in packed:
        edge = swap(edge)
        mid = swap(mid)
        above.append(with_flow(edge))
        got.append((mid, edge))
    tables = prepare(points, vel_index)
    table, _, weights = tables
    home, lowest = home_moments(side, flat, weights, half // 3)
    below = against_flow(lowest)
    gram = jnp.asarray(target_moments(points))
    mat = jnp.asarray(macro_matrix())

    def flow(own, other):
        odd = strip % 2 == 1
        return jnp.concatenate(
            [jnp.where(odd, own[::-1], own), jnp.where(odd, other[::-1], other)]
        )

    flow_rate = flow(collision_rate, other_cells[:rows])
    flow_fluid = 1.0 - flow(wall, other_cells[rows:])
    cells = jnp.concatenate([flow_fluid * (1.0 - flow_rate), flow_fluid])

    home = sum_groups(home)
    home = jnp.concatenate(
        [home[:13], collision_rate.reshape(1, -1), wall.reshape(1, -1), jnp.zeros((1, rows * cols), F32)]
    )
    near_home = jnp.stack([home, *both_z(home)])
    far_home = swap(near_home)

    width = BLOCK_ROWS * LANES
    sums = jnp.zeros((16, width), F32)
    kept = []
    for number, members in enumerate(groups_of):
        start = firsts[members[0]]
        length = sum(chunks[c] for c in members)
        held = None
        for c in members:
            *held, sums = transport(
                side, [flat, *got[c], above[c], below], tables, cells, sums, half,
                chunks[c], firsts[c], size, skip=firsts[c] - start, group=length, into=held,
            )
        next_above = with_flow(held[2])
        next_below = against_flow(held[0])
        kept.append((*held, next_above, next_below))

    total = sum_groups(sums)
    total = total + swap(total)
    sum_a, sum_b = both_z(total)
    change, keep = macro(
        first_macro_kernel, info,
        [total, sum_a, sum_b, near_home, far_home, gram, mat],
        [
            jax.ShapeDtypeStruct((48, 11 * LANES), BF16),
            jax.ShapeDtypeStruct((16, SPAN * LANES), F32),
        ],
        [pltpu.VMEM((16, SPAN * LANES), F32)] * 2,
    )

    sums = jnp.zeros((16, width), F32)
    near, back = None, {}
    for c in later:
        number = int(c >= cut)
        start = firsts[groups_of[number][0]]
        near, far, sums = transport(
            side, list(kept[number]), tables, cells, sums, half,
            chunks[c], firsts[c], size, change, skip=firsts[c] - start,
            into=None if near is None else [near],
        )
        back[c] = swap(far)
    total = sum_groups(sums)
    total = total + swap(total)
    sum_a, sum_b = both_z(total)
    change, state = macro(
        second_macro_kernel, info,
        [total, sum_a, sum_b, keep, gram, mat],
        [
            jax.ShapeDtypeStruct((48, STRIP_ROWS * LANES), BF16),
            jax.ShapeDtypeStruct((5, STRIP_ROWS, LANES), F32),
        ],
        [pltpu.VMEM((16, SPAN * LANES), F32)],
    )
    pieces = [(near, True, 0), *[(back[c], False, firsts[c]) for c in later[:cut]]]
    out = finish(side, None, pieces, table, change, half, size)
    for c in later[cut:]:
        out = finish(side, out, [(back[c], False, firsts[c])], table, change, half, size)
    return out.reshape(dist.shape), state


def solution(mesh):
    def whole(dist, cell_type, collision_rate, vel_index):
        points = round(vel_index.shape[1] ** (1.0 / 3.0))
        in_specs = (P("vel", "strip", None), P("strip", None), P("strip", None), P(None, "vel"))
        out_specs = (P("vel", "strip", None), P(None, "strip", None))

        def body(*args):
            return per_device(points, *args)

        run = jax.shard_map(
            body, mesh=mesh, in_specs=in_specs, out_specs=out_specs, check_vma=False
        )
        return run(dist, cell_type, collision_rate, vel_index)

    return whole
```

```python
import functools
import math

import jax
import jax.numpy as jnp
import numpy as np
from jax import lax
from jax.experimental import pallas as pl
from jax.experimental.pallas import tpu as pltpu
from jax.sharding import PartitionSpec as P


STEP_RATIO = 0.1
SOURCE_WEIGHT = 0.5
HEAT_WEIGHT = 4.0 / 15.0
SWEEPS = 3
HIGH = lax.Precision.HIGHEST
LANES = 128
STRIP_ROWS = 4
BLOCK_ROWS = 2 * STRIP_ROWS
SPAN = 3 * BLOCK_ROWS
F32 = jnp.float32
BF16 = jnp.bfloat16


def params(limit=67043328):
    return pltpu.CompilerParams(vmem_limit_bytes=limit)


def plan(half):
    block = 288 if half % 288 == 0 else 144
    blocks = half // block
    if blocks % 6 == 0:
        unit = block * (blocks // 6)
        return block, [2 * unit, unit, unit, unit, unit]
    return block, [block * (blocks - 2), block, block]


def second_order(pieces):
    cut = (pieces + 1) // 2
    return [*range(1, cut), 0, *range(cut, pieces)], cut


def moment_rows(vel_x, vel_y, vel_z, volume, lib):
    energy = vel_x * vel_x + vel_y * vel_y + vel_z * vel_z
    weight = volume * math.pi ** (-1.5) * lib.exp(-energy)
    rows = [
        lib.ones_like(vel_x),
        vel_x,
        vel_y,
        vel_z,
        energy,
        vel_x * vel_x,
        vel_y * vel_y,
        vel_x * vel_y,
        vel_x * vel_z,
        vel_y * vel_z,
        energy * vel_x,
        energy * vel_y,
        energy * vel_z,
    ]
    return lib.concatenate([(row * weight).reshape(1, -1) for row in rows])


def state_rows(vel_x, vel_y, vel_z, lib):
    energy = vel_x * vel_x + vel_y * vel_y + vel_z * vel_z
    shape_heat = HEAT_WEIGHT * (energy - 2.5)
    rows = [
        lib.ones_like(vel_x),
        2.0 * vel_x,
        2.0 * vel_y,
        2.0 * vel_z,
        energy - 1.5,
        shape_heat * vel_x,
        shape_heat * vel_y,
        shape_heat * vel_z,
    ]
    return lib.concatenate([row.reshape(1, -1) for row in rows])


def target_moments(points):
    line = (np.arange(points) - (points - 1) / 2.0) * (8.0 / points)
    comps = [a.reshape(-1) for a in np.meshgrid(line, line, line, indexing="ij")]
    gram = moment_rows(*comps, (8.0 / points) ** 3, np) @ state_rows(*comps, np).T
    gram[np.abs(gram) < 1e-12] = 0.0
    full = np.zeros((16, 8), np.float32)
    full[:13] = gram
    return full


def macro_matrix():
    third = 2.0 / 3.0
    unit = np.eye(16, dtype=np.float64)
    start = [unit[0], unit[1], unit[2], unit[3], third * unit[4] - unit[0]]
    heat = [unit[10] - 2.5 * unit[1], unit[11] - 2.5 * unit[2], unit[12] - 2.5 * unit[3]]
    flux = [
        unit[1],
        unit[2],
        2.0 * unit[5] - third * unit[4],
        2.0 * unit[7],
        2.0 * unit[6] - third * unit[4],
        2.0 * unit[8],
        2.0 * unit[9],
        heat[0],
        heat[1],
    ]
    out = np.zeros((32, 16), np.float64)
    for row in range(5):
        out[row] = start[row]
        out[8 + row] = flux[(0, 2, 3, 5, 7)[row]]
        out[16 + row] = flux[(1, 3, 4, 6, 8)[row]]
    for row in range(3):
        out[24 + 5 + row] = heat[row]
    return out.astype(np.float32)


def minmod(left, right):
    return jnp.maximum(jnp.minimum(right, jnp.maximum(left, 0.0)), jnp.minimum(left, 0.0))


def strided(start, count):
    return pl.ds(start, count, stride=STRIP_ROWS)


def pack_kernel(size, begins, counts, side_ref, far_ref, *rest):
    outs = rest[-2 * len(begins) :]
    side = side_ref[0]
    step = pl.program_id(0)
    for c, (begin, count) in enumerate(zip(begins, counts)):

        @pl.when((step >= begin) & (step < begin + count))
        def _():
            for i in range(STRIP_ROWS):
                row = jnp.where(side == 1, i, 3 - i)
                outs[2 * c + (1 if i < 2 else 0)][i % 2] = far_ref[strided(row, size), :]


def pack(side, flat, half, chunks, first, size):
    counts = [n // size for n in chunks]
    begins = [sum(counts[:c]) for c in range(len(chunks))]
    shift = half // size
    start = first // size

    def out_spec(c):
        return pl.BlockSpec(
            (2, size, LANES), lambda i, s: (0, jnp.clip(i - begins[c], 0, counts[c] - 1), 0)
        )

    outs = pl.pallas_call(
        functools.partial(pack_kernel, size, begins, counts),
        out_shape=[
            jax.ShapeDtypeStruct((2, n, LANES), F32) for n in chunks for _ in range(2)
        ],
        grid_spec=pltpu.PrefetchScalarGridSpec(
            num_scalar_prefetch=1,
            grid=(sum(counts),),
            in_specs=[
                pl.BlockSpec((4 * size, LANES), lambda i, s: ((1 - s[0]) * shift + start + i, 0))
            ],
            out_specs=[out_spec(c) for c in range(len(chunks)) for _ in range(2)],
        ),
        compiler_params=params(),
        name="pack",
        cost_estimate=pl.CostEstimate(
            flops=0, transcendentals=0, bytes_accessed=sum(chunks) * LANES * 4 * 8
        ),
    )(side, flat)
    return [(outs[2 * c], outs[2 * c + 1]) for c in range(len(chunks))]


def prepare_kernel(points, vel_ref, table_ref, const_ref, weight_ref):
    comps = (vel_ref[...].astype(F32) - (points - 1) / 2.0) * (8.0 / points)
    vel_x, vel_y, vel_z = comps[0:1], comps[1:2], comps[2:3]
    moments = moment_rows(vel_x, vel_y, vel_z, (8.0 / points) ** 3, jnp)
    high = moments.astype(BF16).astype(F32)
    shapes = state_rows(vel_x, vel_y, vel_z, jnp)
    part_a = shapes.astype(BF16).astype(F32)
    part_b = (shapes - part_a).astype(BF16).astype(F32)
    part_c = shapes - part_a - part_b
    width = vel_x.shape[1]
    rows = jnp.concatenate(
        [
            *[part_a] * 3,
            *[part_b] * 2,
            part_c,
            high,
            jnp.zeros((3, width), F32),
            moments - high,
            jnp.zeros((3, width), F32),
            STEP_RATIO * jnp.abs(vel_x),
            STEP_RATIO * jnp.abs(vel_y),
            jnp.where(vel_y > 0, 0.5, -0.5),
            jnp.zeros((45, width), F32),
        ]
    )
    columns = rows.T
    table_ref[...] = columns[:, :48].astype(BF16)
    weight_ref[...] = columns[:, 48:80].astype(BF16)
    const_ref[...] = columns[:, 80:88]


def prepare(points, vel_index):
    count = vel_index.shape[1]
    vmem = pl.BlockSpec(memory_space=pltpu.VMEM)
    return pl.pallas_call(
        functools.partial(prepare_kernel, points),
        out_shape=(
            jax.ShapeDtypeStruct((count, 48), BF16),
            jax.ShapeDtypeStruct((count, 8), F32),
            jax.ShapeDtypeStruct((count, 32), BF16),
        ),
        in_specs=[vmem],
        out_specs=[vmem] * 3,
        compiler_params=params(),
        name="prepare",
        cost_estimate=pl.CostEstimate(
            flops=200 * count, transcendentals=count, bytes_accessed=count * 1000
        ),
    )(vel_index)


def weighted(weight_ref, values):
    over_rows = (((0,), (0,)), ((), ()))
    total = None
    for start in range(0, weight_ref.shape[0], 144):
        weights = weight_ref[start : start + 144, :]
        value = jnp.concatenate(values(start), axis=1)
        high = value.astype(BF16)
        low = (value - high.astype(F32)).astype(BF16)
        both = lax.dot_general(weights, high, over_rows, preferred_element_type=F32)
        rest = lax.dot_general(weights, low, over_rows, preferred_element_type=F32)
        part = both[:16] + both[16:] + rest[:16]
        total = part if total is None else total + part
    return total


def moment_kernel(size, side_ref, dist_ref, weight_ref, out_ref, lowest_ref):
    side = side_ref[0]
    step = pl.program_id(0)
    half_steps = pl.num_programs(0) // 2

    @pl.when(step == 0)
    def _():
        out_ref[...] = jnp.zeros_like(out_ref)

    @pl.when(jnp.where(step >= half_steps, 1, 0) == side)
    def _():
        lowest_ref[...] = dist_ref[strided(jnp.where(side == 1, 3, 0), size), :]

    for pair in range(0, STRIP_ROWS, 2):
        def values(start, pair=pair):
            return [
                dist_ref[strided(STRIP_ROWS * start + row, 144), :] for row in (pair, pair + 1)
            ]

        out_ref[:, pair * LANES : (pair + 2) * LANES] += weighted(weight_ref, values)


def home_moments(side, flat, weights, size):
    count = flat.shape[0] // STRIP_ROWS
    width = STRIP_ROWS * LANES
    half_steps = count // size // 2
    return pl.pallas_call(
        functools.partial(moment_kernel, size),
        out_shape=(
            jax.ShapeDtypeStruct((16, width), F32),
            jax.ShapeDtypeStruct((count // 2, LANES), F32),
        ),
        grid_spec=pltpu.PrefetchScalarGridSpec(
            num_scalar_prefetch=1,
            grid=(2 * half_steps,),
            in_specs=[
                pl.BlockSpec((4 * size, LANES), lambda i, s: (i, 0)),
                pl.BlockSpec((size, 32), lambda i, s: (i, 0)),
            ],
            out_specs=[
                pl.BlockSpec((16, width), lambda i, s: (0, 0)),
                pl.BlockSpec(
                    (size, LANES), lambda i, s: (jnp.clip(i - s[0] * half_steps, 0, half_steps - 1), 0)
                ),
            ],
        ),
        compiler_params=params(),
        name="home_moments",
        cost_estimate=pl.CostEstimate(
            flops=2 * 64 * count * width, transcendentals=0, bytes_accessed=count * width * 4
        ),
    )(side, flat, weights)


def transport_kernel(size, second_pass, side_ref, *refs):
    if second_pass:
        (table_ref, change_ref, q_first, q_mid, q_edge, up_ref, down_ref, *rest) = refs
    else:
        (own_ref, mid_ref, edge_ref, up_ref, down_ref, *rest) = refs
    (const_ref, weight_ref, cell_ref, sum_in_ref, *rest) = rest
    if second_pass:
        (near_out, far_out, sum_ref, lift_ref) = rest[-4:]
    else:
        (first_out, mid_out, edge_out, sum_ref) = rest[-4:]
    side = side_ref[0]
    group_size = 32 if size % 32 == 0 else 16

    @pl.when(pl.program_id(0) == 0)
    def _():
        sum_ref[...] = sum_in_ref[...]

    if second_pass:
        lift_ref[...] = jnp.dot(table_ref[...], change_ref[...], preferred_element_type=F32)

    def row_out(row):
        if second_pass:
            return near_out.at[row] if row < 4 else far_out.at[row - 4]
        if row == 0:
            return first_out
        return mid_out.at[row - 1] if row < 6 else edge_out.at[row - 6]

    lane = lax.broadcasted_iota(jnp.int32, (group_size, LANES), 1)
    inner_low = jnp.where(lane == 0, 0.0, 1.0)
    inner_high = jnp.where(lane == LANES - 1, 0.0, 1.0)

    def body(group, carry):
        base = pl.multiple_of(group * group_size, group_size)
        rows = pl.ds(base, group_size)

        def load(row):
            if row < 0:
                value = up_ref[row + 2, rows, :]
            elif row == 8:
                value = down_ref[rows, :]
            elif second_pass:
                if row == 0:
                    value = q_first[rows, :]
                elif row < 6:
                    value = q_mid[row - 1, rows, :]
                else:
                    value = q_edge[row - 6, rows, :]
            elif row < 4:
                local = jnp.where(side == 1, 3 - row, row)
                value = own_ref[strided(base * STRIP_ROWS + local, group_size), :]
            elif row < 6:
                value = mid_ref[row - 4, rows, :]
            else:
                value = edge_ref[row - 6, rows, :]
            if second_pass:
                value = value + lift_ref[rows, pl.ds((row + 2) * LANES, LANES)]
            return value

        def wide(column):
            return jnp.broadcast_to(const_ref[rows, column : column + 1], (group_size, LANES))

        speed_x = wide(0)
        speed_y = wide(1)
        half_sign = wide(2)
        forward = half_sign > 0.0
        open_end = jnp.where(forward, inner_low, inner_high)

        behind = load(-2)
        here = load(-1)
        ahead = load(0)
        step = ahead - here
        upwind = here + 0.5 * minmod(here - behind, step)
        here = ahead
        for row in range(BLOCK_ROWS):
            ahead = load(row + 1)
            next_step = ahead - here
            next_upwind = here + 0.5 * minmod(step, next_step)
            drift = speed_x * (next_upwind - upwind)
            step = next_step
            upwind = next_upwind
            left = here - pltpu.roll(here, 1, 1) * inner_low
            right = pltpu.roll(here, LANES - 1, 1) * inner_high - here
            face = here + half_sign * minmod(left, right)
            other = jnp.where(forward, pltpu.roll(face, 1, 1), pltpu.roll(face, LANES - 1, 1))
            drift = drift + speed_y * (face - other * open_end)
            keep = jnp.broadcast_to(cell_ref[row : row + 1, :], (group_size, LANES))
            fluid = jnp.broadcast_to(cell_ref[row + 8 : row + 9, :], (group_size, LANES))
            value = keep * here - fluid * drift
            row_out(row)[rows, :] = value
            here = ahead
        return carry

    lax.fori_loop(0, size // group_size, body, 0)
    for pair in range(0, BLOCK_ROWS, 2):
        def values(start, pair=pair):
            return [row_out(row)[start : start + 144, :] for row in (pair, pair + 1)]

        part = weighted(weight_ref, values)
        for row in (pair, pair + 1):
            place = jnp.where(side == 1, 7 - row, row)
            columns = pl.ds(pl.multiple_of(place * LANES, LANES), LANES)
            sum_ref[:, columns] += part[:, (row - pair) * LANES : (row - pair + 1) * LANES]


def transport(
    side, sources, tables, cells, sums, half, chunk, first, size, change=None, skip=0, group=None, into=None
):
    second_pass = change is not None
    steps = chunk // size
    shift = half // size
    begin = first // size
    offset = skip // size
    table, const, weights = tables
    width = BLOCK_ROWS * LANES

    def mine(i, s):
        return s[0] * shift + begin + i

    def stack_of(count, at):
        return pl.BlockSpec((count, size, LANES), lambda i, s: (0, at + i, 0))

    aliases = {}
    if second_pass:
        args = [table, change]
        specs = [
            pl.BlockSpec((size, 48), lambda i, s: (mine(i, s), 0)),
            pl.BlockSpec(change.shape, lambda i, s: (0, 0)),
            stack_of(None, offset),
            stack_of(5, offset),
            stack_of(2, offset),
            stack_of(2, offset),
            stack_of(None, offset),
        ]
        outs = [jax.ShapeDtypeStruct((4, n, LANES), F32) for n in (half, chunk)]
        out_specs = [stack_of(4, begin), stack_of(4, 0)]
        scratch = [pltpu.VMEM((size, 11 * LANES), F32)]
    else:
        args = []
        specs = [
            pl.BlockSpec((4 * size, LANES), lambda i, s: (mine(i, s), 0)),
            stack_of(2, 0),
            stack_of(2, 0),
            stack_of(2, 0),
            pl.BlockSpec((size, LANES), lambda i, s: (begin + i, 0)),
        ]
        outs = [jax.ShapeDtypeStruct((n, group, LANES), F32) for n in (1, 5, 2)]
        out_specs = [stack_of(None, offset), stack_of(5, offset), stack_of(2, offset)]
        scratch = []
    whole = pl.BlockSpec((16, width), lambda i, s: (0, 0))
    args = [side, *args, *sources, const, weights, cells, sums]
    specs = [
        *specs,
        pl.BlockSpec((size, 8), lambda i, s: (mine(i, s), 0)),
        pl.BlockSpec((size, 32), lambda i, s: (mine(i, s), 0)),
        pl.BlockSpec((16, LANES), lambda i, s: (0, 0)),
        whole,
    ]
    if into is not None:
        aliases = {len(args) + n: n for n in range(len(into))}
        args = [*args, *into]
        specs = [*specs, *[pl.BlockSpec(memory_space=pl.ANY)] * len(into)]
    return pl.pallas_call(
        functools.partial(transport_kernel, size, second_pass),
        out_shape=(*outs, jax.ShapeDtypeStruct((16, width), F32)),
        grid_spec=pltpu.PrefetchScalarGridSpec(
            num_scalar_prefetch=1,
            grid=(steps,),
            in_specs=specs,
            out_specs=[*out_specs, whole],
            scratch_shapes=scratch,
        ),
        input_output_aliases=aliases,
        compiler_params=params(),
        name="transport_second" if second_pass else "transport_first",
        cost_estimate=pl.CostEstimate(
            flops=60 * chunk * width, transcendentals=0, bytes_accessed=chunk * LANES * 4 * 19
        ),
    )(*args)


def sweep_block(inputs, relax, rate):
    start, flux_x, flux_y = inputs
    lane = lax.broadcasted_iota(jnp.int32, (8, LANES), 1)
    inner_low = jnp.where(lane == 0, 0.0, 1.0)
    inner_high = jnp.where(lane == LANES - 1, 0.0, 1.0)

    def block(array, row):
        if row < 0 or row >= SPAN:
            return jnp.zeros((8, LANES), F32)
        return array[:, row * LANES : (row + 1) * LANES]

    def lower(value):
        return pltpu.roll(value, 1, 1) * inner_low

    def upper(value):
        return pltpu.roll(value, LANES - 1, 1) * inner_high

    source = []
    for row in range(SPAN):
        diff_x = 0.5 * (block(flux_x, row + 1) - block(flux_x, row - 1))
        side = block(flux_y, row)
        diff_y = 0.5 * (upper(side) - lower(side))
        source.append(block(start, row) - SOURCE_WEIGHT * (diff_x + diff_y))
    zero = jnp.zeros((8, LANES), F32)
    kappa = [block(rate, row) for row in range(SPAN)]
    scale = [block(relax, row) for row in range(SPAN)]
    state = [block(start, row) for row in range(SPAN)]
    for _ in range(SWEEPS):
        near = [zero, *state, zero]
        state = [
            (source[row] + kappa[row] * (near[row] + near[row + 2] + lower(near[row + 1]) + upper(near[row + 1])))
            * scale[row]
            for row in range(SPAN)
        ]
    return jnp.concatenate(state, axis=1)


def stacked(value):
    first = value.astype(BF16)
    rest = value - first.astype(F32)
    second = rest.astype(BF16)
    third = (rest - second.astype(F32)).astype(BF16)
    return jnp.concatenate([first, second, third, first, second, first], axis=0)


def relax_rows(rate):
    inside = rate > 0.0
    kappa = jnp.where(inside, 0.5 / jnp.where(inside, rate, 1.0), 0.0)
    scale = jnp.where(inside, 1.0 / (1.0 + 4.0 * kappa), 0.0)
    width = rate.shape[1]
    return jnp.broadcast_to(kappa, (8, width)), jnp.broadcast_to(scale, (8, width))


def place_blocks(info_ref, span_ref, own, pair_a, pair_b):
    odd = info_ref[1]
    width = BLOCK_ROWS * LANES
    span_ref[:, width : 2 * width] = own
    place_a = pl.multiple_of((1 - odd) * 2 * width, width)
    place_b = pl.multiple_of(odd * 2 * width, width)
    span_ref[:, pl.ds(place_a, width)] = pair_a
    span_ref[:, pl.ds(place_b, width)] = pair_b


def first_macro_kernel(
    info_ref, sum_ref, sum_a_ref, sum_b_ref, near_ref, far_ref, gram_ref, mat_ref,
    change_ref, keep_ref, span_ref, home_ref,
):
    side = info_ref[0]
    odd = info_ref[1]
    width = BLOCK_ROWS * LANES
    part = STRIP_ROWS * LANES
    place_blocks(info_ref, span_ref, sum_ref[...], sum_a_ref[...], sum_b_ref[...])
    for ref, where in ((near_ref, side), (far_ref, 1 - side)):
        for index, block in enumerate((1, (1 - odd) * 2, odd * 2)):
            spot = pl.multiple_of(block * width + where * part, part)
            home_ref[:, pl.ds(spot, part)] = ref[index]
    home = home_ref[...]
    rate = home[13:14, :]
    ratio = jnp.where(home[14:15, :] > 0.5, 1.0, rate)
    mat = mat_ref[...]
    first = jnp.dot(mat, jnp.where(lax.broadcasted_iota(jnp.int32, home.shape, 0) < 13, home, 0.0), precision=HIGH)
    fields = first[:8] + first[24:]
    moments = span_ref[...] + ratio * jnp.dot(gram_ref[...], fields, precision=HIGH)
    all_parts = jnp.dot(mat, moments, precision=HIGH)
    start = all_parts[:8]
    kappa, scale = relax_rows(rate)
    state = sweep_block((start, all_parts[8:16], all_parts[16:24]), scale, kappa)
    change = ratio * fields + (state - start)
    span_ref[0:8, :] = change
    keep_ref[0:8, :] = state + all_parts[24:]
    keep_ref[8:9, :] = rate
    keep_ref[9:10, :] = ratio
    keep_ref[10:16, :] = jnp.zeros((6, SPAN * LANES), F32)
    for row in range(-2, 9):
        spot = jnp.where(side == 1, 15 - row, 8 + row)
        piece = span_ref[0:8, pl.ds(pl.multiple_of(spot * LANES, LANES), LANES)]
        change_ref[:, (row + 2) * LANES : (row + 3) * LANES] = stacked(piece)


def last_kernel(
    size, half, blocks, info_ref, sum_ref, sum_a_ref, sum_b_ref, keep_ref, gram_ref, mat_ref,
    table_ref, *refs
):
    count = len({source for source, *_ in blocks})
    sources = refs[:count]
    out_ref, change_ref, state_ref, span_ref, held_ref, ready_ref, in_sems, out_sems = refs[count:]
    side = info_ref[0]

    def copy_in(k):
        source, offset, _, _ = blocks[k]
        return pltpu.make_async_copy(
            sources[source].at[:, pl.ds(offset, size), :], held_ref.at[k], in_sems.at[k]
        )

    for k in range(len(blocks)):
        copy_in(k).start()
    place_blocks(info_ref, span_ref, sum_ref[...], sum_a_ref[...], sum_b_ref[...])
    fields = keep_ref[0:8, :]
    rate = keep_ref[8:9, :]
    ratio = keep_ref[9:10, :]
    moments = span_ref[...] + ratio * jnp.dot(gram_ref[...], fields, precision=HIGH)
    all_parts = jnp.dot(mat_ref[...], moments, precision=HIGH)
    start = all_parts[:8]
    kappa, scale = relax_rows(rate)
    state = sweep_block((start, all_parts[8:16], all_parts[16:24]), scale, kappa)
    span_ref[0:8, :] = ratio * fields + (state - start)
    span_ref[8:16, :] = state
    part = STRIP_ROWS * LANES
    spot = pl.ds(pl.multiple_of(2 * part + side * part, part), part)
    change_ref[...] = stacked(span_ref[0:8, spot])
    state = span_ref[8:16, spot]
    for row in range(STRIP_ROWS):
        state_ref[:, row, :] = state[:5, row * LANES : (row + 1) * LANES]

    def copy_out(k):
        _, offset, own, first = blocks[k]
        begin = (side if own else 1 - side) * half + first + offset
        return begin, pltpu.make_async_copy(
            ready_ref.at[k],
            out_ref.at[pl.ds(pl.multiple_of(begin * STRIP_ROWS, STRIP_ROWS * size), STRIP_ROWS * size), :],
            out_sems.at[k],
        )

    for k, (_, _, own, _) in enumerate(blocks):
        begin, copy = copy_out(k)
        lift = jnp.dot(
            table_ref[pl.ds(pl.multiple_of(begin, size), size), :],
            change_ref[...],
            preferred_element_type=F32,
        )
        copy_in(k).wait()
        flipped = side == (1 if own else 0)
        for row in range(STRIP_ROWS):
            index = jnp.where(flipped, 3 - row, row)
            ready_ref[k, strided(row, size), :] = (
                held_ref[k, index] + lift[:, row * LANES : (row + 1) * LANES]
            )
        copy.start()
    for k in range(len(blocks)):
        copy_out(k)[1].wait()


def last_macro(info, args, table, pieces, half, size):
    blocks = [
        (source, offset, own, first)
        for source, (rows, own, first) in enumerate(pieces)
        for offset in range(0, rows.shape[1], size)
    ]
    whole = pl.BlockSpec(memory_space=pltpu.VMEM)
    anywhere = pl.BlockSpec(memory_space=pl.ANY)
    return pl.pallas_call(
        functools.partial(last_kernel, size, half, blocks),
        out_shape=[
            jax.ShapeDtypeStruct((2 * half * STRIP_ROWS, LANES), F32),
            jax.ShapeDtypeStruct((48, STRIP_ROWS * LANES), BF16),
            jax.ShapeDtypeStruct((5, STRIP_ROWS, LANES), F32),
        ],
        in_specs=[
            pl.BlockSpec(memory_space=pltpu.SMEM),
            *[whole] * (len(args) + 1),
            *[anywhere] * len(pieces),
        ],
        out_specs=[anywhere, whole, whole],
        scratch_shapes=[
            pltpu.VMEM((16, SPAN * LANES), F32),
            pltpu.VMEM((len(blocks), STRIP_ROWS, size, LANES), F32),
            pltpu.VMEM((len(blocks), STRIP_ROWS * size, LANES), F32),
            pltpu.SemaphoreType.DMA((len(blocks),)),
            pltpu.SemaphoreType.DMA((len(blocks),)),
        ],
        compiler_params=params(63 * 1024 * 1024),
        name="last_macro",
        cost_estimate=pl.CostEstimate(
            flops=4000000, transcendentals=0, bytes_accessed=len(blocks) * size * LANES * 32
        ),
    )(info, *args, table, *[rows for rows, _, _ in pieces])


def macro(kernel, info, args, outs, scratch):
    vmem = pl.BlockSpec(memory_space=pltpu.VMEM)
    return pl.pallas_call(
        kernel,
        out_shape=outs,
        in_specs=[pl.BlockSpec(memory_space=pltpu.SMEM)] + [vmem] * len(args),
        out_specs=[vmem] * len(outs),
        scratch_shapes=scratch,
        compiler_params=params(48 * 1024 * 1024),
        cost_estimate=pl.CostEstimate(flops=4000000, transcendentals=0, bytes_accessed=1000000),
    )(info, *args)


def finish_kernel(size, parts, side_ref, *refs):
    out_ref = refs[-1]
    rows = refs[: len(parts)]
    table_ref, change_ref = refs[len(parts) : len(parts) + 2]
    side = side_ref[0]
    step = pl.program_id(0)
    lift = jnp.dot(table_ref[...], change_ref[...], preferred_element_type=F32)
    for ref, (own, begin, count, _) in zip(rows, parts):

        @pl.when((step >= begin) & (step < begin + count))
        def _(ref=ref, flipped=(side == (1 if own else 0))):
            for row in range(STRIP_ROWS):
                index = jnp.where(flipped, 3 - row, row)
                out_ref[strided(row, size), :] = (
                    ref[index] + lift[:, row * LANES : (row + 1) * LANES]
                )


def finish(side, out, pieces, table, change, half, size):
    shift = half // size
    parts = []
    steps = 0
    for rows, own, first in pieces:
        count = rows.shape[1] // size
        parts.append((own, steps, count, first // size))
        steps += count

    def place(i, s):
        spot = 0
        for own, begin, count, at in parts:
            here = (s[0] if own else 1 - s[0]) * shift + at + i - begin
            spot = jnp.where(i >= begin, here, spot)
        return spot

    def rows_spec(begin, count):
        return pl.BlockSpec(
            (4, size, LANES), lambda i, s: (0, jnp.clip(i - begin, 0, count - 1), 0)
        )

    specs = [
        *[rows_spec(begin, count) for _, begin, count, _ in parts],
        pl.BlockSpec((size, 48), lambda i, s: (place(i, s), 0)),
        pl.BlockSpec(change.shape, lambda i, s: (0, 0)),
    ]
    args = [side, *[rows for rows, _, _ in pieces], table, change]
    aliases = {}
    if out is not None:
        specs.append(pl.BlockSpec(memory_space=pl.ANY))
        aliases = {len(args): 0}
        args.append(out)
    return pl.pallas_call(
        functools.partial(finish_kernel, size, parts),
        out_shape=jax.ShapeDtypeStruct((2 * half * STRIP_ROWS, LANES), F32),
        grid_spec=pltpu.PrefetchScalarGridSpec(
            num_scalar_prefetch=1,
            grid=(steps,),
            in_specs=specs,
            out_specs=pl.BlockSpec((4 * size, LANES), lambda i, s: (place(i, s), 0)),
        ),
        input_output_aliases=aliases,
        compiler_params=params(),
        name="finish",
        cost_estimate=pl.CostEstimate(
            flops=2 * 48 * 4 * LANES * steps * size,
            transcendentals=0,
            bytes_accessed=steps * size * LANES * 4 * 8,
        ),
    )(*args)


def per_device(points, dist, cell_type, collision_rate, vel_index):
    count, rows, cols = dist.shape
    half = count // 2
    strips = lax.axis_size("strip")
    groups = lax.axis_size("vel")
    strip = lax.axis_index("strip")
    size, chunks = plan(half)
    firsts = [sum(chunks[:c]) for c in range(len(chunks))]
    order = range(len(chunks))
    later, cut = second_order(len(chunks))
    groups_of = [order[:cut], order[cut:]]
    side = (strip % 2).astype(jnp.int32).reshape(1)
    info = jnp.stack([strip % 2, (strip // 2) % 2]).astype(jnp.int32)

    swap_pairs = [(s, s ^ 1) for s in range(strips)]
    down_pairs = [
        (s, s + (2 if s % 2 == 0 else -2))
        for s in range(strips)
        if 0 <= s + (2 if s % 2 == 0 else -2) < strips
    ]
    up_pairs = [(b, a) for a, b in down_pairs]
    pair_a = [
        (s, s + (2 if (s // 2) % 2 == 0 else -2))
        for s in range(strips)
        if 0 <= s + (2 if (s // 2) % 2 == 0 else -2) < strips
    ]
    pair_b = [
        (s, s + (-2 if (s // 2) % 2 == 0 else 2))
        for s in range(strips)
        if 0 <= s + (-2 if (s // 2) % 2 == 0 else 2) < strips
    ]

    def swap(value):
        return lax.ppermute(value, "strip", swap_pairs)

    def with_flow(value):
        return lax.ppermute(value, "strip", down_pairs)

    def against_flow(value):
        return lax.ppermute(value, "strip", up_pairs)

    def both_z(value):
        return lax.ppermute(value, "strip", pair_a), lax.ppermute(value, "strip", pair_b)

    def sum_groups(value):
        total = value
        for shift in range(1, groups):
            total = total + lax.ppermute(
                value, "vel", [(g, (g + shift) % groups) for g in range(groups)]
            )
        return total

    flat = dist.reshape(count * rows, cols)
    wall = (cell_type == 1).astype(F32)
    cell_pair = jnp.concatenate([collision_rate, wall])
    other_cells = swap(cell_pair)

    packed = pack(side, flat, half, chunks[:1], 0, size)
    packed += pack(side, flat, half, chunks[1:], firsts[1], size)
    got, above = [], []
    for edge, mid in packed:
        edge = swap(edge)
        mid = swap(mid)
        above.append(with_flow(edge))
        got.append((mid, edge))
    tables = prepare(points, vel_index)
    table, _, weights = tables
    home, lowest = home_moments(side, flat, weights, half // 3)
    below = against_flow(lowest)
    gram = jnp.asarray(target_moments(points))
    mat = jnp.asarray(macro_matrix())

    def flow(own, other):
        odd = strip % 2 == 1
        return jnp.concatenate(
            [jnp.where(odd, own[::-1], own), jnp.where(odd, other[::-1], other)]
        )

    flow_rate = flow(collision_rate, other_cells[:rows])
    flow_fluid = 1.0 - flow(wall, other_cells[rows:])
    cells = jnp.concatenate([flow_fluid * (1.0 - flow_rate), flow_fluid])

    home = sum_groups(home)
    home = jnp.concatenate(
        [home[:13], collision_rate.reshape(1, -1), wall.reshape(1, -1), jnp.zeros((1, rows * cols), F32)]
    )
    near_home = jnp.stack([home, *both_z(home)])
    far_home = swap(near_home)

    width = BLOCK_ROWS * LANES
    sums = jnp.zeros((16, width), F32)
    kept = []
    for number, members in enumerate(groups_of):
        start = firsts[members[0]]
        length = sum(chunks[c] for c in members)
        held = None
        for c in members:
            *held, sums = transport(
                side, [flat, *got[c], above[c], below], tables, cells, sums, half,
                chunks[c], firsts[c], size, skip=firsts[c] - start, group=length, into=held,
            )
        next_above = with_flow(held[2])
        next_below = against_flow(held[0])
        kept.append((*held, next_above, next_below))

    total = sum_groups(sums)
    total = total + swap(total)
    sum_a, sum_b = both_z(total)
    change, keep = macro(
        first_macro_kernel, info,
        [total, sum_a, sum_b, near_home, far_home, gram, mat],
        [
            jax.ShapeDtypeStruct((48, 11 * LANES), BF16),
            jax.ShapeDtypeStruct((16, SPAN * LANES), F32),
        ],
        [pltpu.VMEM((16, SPAN * LANES), F32)] * 2,
    )

    sums = jnp.zeros((16, width), F32)
    near, back = None, {}
    for c in later:
        number = int(c >= cut)
        start = firsts[groups_of[number][0]]
        near, far, sums = transport(
            side, list(kept[number]), tables, cells, sums, half,
            chunks[c], firsts[c], size, change, skip=firsts[c] - start,
            into=None if near is None else [near],
        )
        back[c] = swap(far)
    total = sum_groups(sums)
    total = total + swap(total)
    sum_a, sum_b = both_z(total)
    pieces = [(near, True, 0), *[(back[c], False, firsts[c]) for c in later[:cut]]]
    out, change, state = last_macro(
        info, [total, sum_a, sum_b, keep, gram, mat], table, pieces, half, size
    )
    for c in later[cut:]:
        out = finish(side, out, [(back[c], False, firsts[c])], table, change, half, size)
    return out.reshape(dist.shape), state


def solution(mesh):
    def whole(dist, cell_type, collision_rate, vel_index):
        points = round(vel_index.shape[1] ** (1.0 / 3.0))
        in_specs = (P("vel", "strip", None), P("strip", None), P("strip", None), P(None, "vel"))
        out_specs = (P("vel", "strip", None), P(None, "strip", None))

        def body(*args):
            return per_device(points, *args)

        run = jax.shard_map(
            body, mesh=mesh, in_specs=in_specs, out_specs=out_specs, check_vma=False
        )
        return run(dist, cell_type, collision_rate, vel_index)

    return whole
```

```python
import functools
import math

import jax
import jax.numpy as jnp
import numpy as np
from jax import lax
from jax.experimental import pallas as pl
from jax.experimental.pallas import tpu as pltpu
from jax.sharding import PartitionSpec as P


STEP_RATIO = 0.1
SOURCE_WEIGHT = 0.5
HEAT_WEIGHT = 4.0 / 15.0
SWEEPS = 3
HIGH = lax.Precision.HIGHEST
LANES = 128
STRIP_ROWS = 4
BLOCK_ROWS = 2 * STRIP_ROWS
SPAN = 3 * BLOCK_ROWS
F32 = jnp.float32
BF16 = jnp.bfloat16


def params(limit=66584576):
    return pltpu.CompilerParams(vmem_limit_bytes=limit)


def plan(half):
    block = 288 if half % 288 == 0 else 144
    blocks = half // block
    if blocks % 6 == 0:
        unit = block * (blocks // 6)
        return block, [2 * unit, 2 * unit, unit, unit]
    return block, [block * (blocks - 2), block, block]


def second_items(chunks):
    firsts = [sum(chunks[:c]) for c in range(len(chunks))]
    unit = chunks[-1]
    items = [(1, first, unit) for first in range(firsts[1], firsts[2], unit)]
    items.append((0, 0, chunks[0]))
    return items + [(2, firsts[c], chunks[c]) for c in range(2, len(chunks))]


def moment_rows(vel_x, vel_y, vel_z, volume, lib):
    energy = vel_x * vel_x + vel_y * vel_y + vel_z * vel_z
    weight = volume * math.pi ** (-1.5) * lib.exp(-energy)
    rows = [
        lib.ones_like(vel_x),
        vel_x,
        vel_y,
        vel_z,
        energy,
        vel_x * vel_x,
        vel_y * vel_y,
        vel_x * vel_y,
        vel_x * vel_z,
        vel_y * vel_z,
        energy * vel_x,
        energy * vel_y,
        energy * vel_z,
    ]
    return lib.concatenate([(row * weight).reshape(1, -1) for row in rows])


def state_rows(vel_x, vel_y, vel_z, lib):
    energy = vel_x * vel_x + vel_y * vel_y + vel_z * vel_z
    shape_heat = HEAT_WEIGHT * (energy - 2.5)
    rows = [
        lib.ones_like(vel_x),
        2.0 * vel_x,
        2.0 * vel_y,
        2.0 * vel_z,
        energy - 1.5,
        shape_heat * vel_x,
        shape_heat * vel_y,
        shape_heat * vel_z,
    ]
    return lib.concatenate([row.reshape(1, -1) for row in rows])


def target_moments(points):
    line = (np.arange(points) - (points - 1) / 2.0) * (8.0 / points)
    comps = [a.reshape(-1) for a in np.meshgrid(line, line, line, indexing="ij")]
    gram = moment_rows(*comps, (8.0 / points) ** 3, np) @ state_rows(*comps, np).T
    gram[np.abs(gram) < 1e-12] = 0.0
    full = np.zeros((16, 8), np.float32)
    full[:13] = gram
    return full


def macro_matrix():
    third = 2.0 / 3.0
    unit = np.eye(16, dtype=np.float64)
    start = [unit[0], unit[1], unit[2], unit[3], third * unit[4] - unit[0]]
    heat = [unit[10] - 2.5 * unit[1], unit[11] - 2.5 * unit[2], unit[12] - 2.5 * unit[3]]
    flux = [
        unit[1],
        unit[2],
        2.0 * unit[5] - third * unit[4],
        2.0 * unit[7],
        2.0 * unit[6] - third * unit[4],
        2.0 * unit[8],
        2.0 * unit[9],
        heat[0],
        heat[1],
    ]
    out = np.zeros((32, 16), np.float64)
    for row in range(5):
        out[row] = start[row]
        out[8 + row] = flux[(0, 2, 3, 5, 7)[row]]
        out[16 + row] = flux[(1, 3, 4, 6, 8)[row]]
    for row in range(3):
        out[24 + 5 + row] = heat[row]
    return out.astype(np.float32)


def minmod(left, right):
    return jnp.maximum(jnp.minimum(right, jnp.maximum(left, 0.0)), jnp.minimum(left, 0.0))


def strided(start, count):
    return pl.ds(start, count, stride=STRIP_ROWS)


def pack_kernel(size, begins, counts, side_ref, far_ref, *rest):
    outs = rest[-2 * len(begins) :]
    side = side_ref[0]
    step = pl.program_id(0)
    for c, (begin, count) in enumerate(zip(begins, counts)):

        @pl.when((step >= begin) & (step < begin + count))
        def _():
            for i in range(STRIP_ROWS):
                row = jnp.where(side == 1, i, 3 - i)
                outs[2 * c + (1 if i < 2 else 0)][i % 2] = far_ref[strided(row, size), :]


def pack(side, flat, half, chunks, first, size):
    counts = [n // size for n in chunks]
    begins = [sum(counts[:c]) for c in range(len(chunks))]
    shift = half // size
    start = first // size

    def out_spec(c):
        return pl.BlockSpec(
            (2, size, LANES), lambda i, s: (0, jnp.clip(i - begins[c], 0, counts[c] - 1), 0)
        )

    outs = pl.pallas_call(
        functools.partial(pack_kernel, size, begins, counts),
        out_shape=[
            jax.ShapeDtypeStruct((2, n, LANES), F32) for n in chunks for _ in range(2)
        ],
        grid_spec=pltpu.PrefetchScalarGridSpec(
            num_scalar_prefetch=1,
            grid=(sum(counts),),
            in_specs=[
                pl.BlockSpec((4 * size, LANES), lambda i, s: ((1 - s[0]) * shift + start + i, 0))
            ],
            out_specs=[out_spec(c) for c in range(len(chunks)) for _ in range(2)],
        ),
        compiler_params=params(),
        name="pack",
        cost_estimate=pl.CostEstimate(
            flops=0, transcendentals=0, bytes_accessed=sum(chunks) * LANES * 4 * 8
        ),
    )(side, flat)
    return [(outs[2 * c], outs[2 * c + 1]) for c in range(len(chunks))]


def prepare_kernel(points, vel_ref, table_ref, const_ref, weight_ref):
    comps = (vel_ref[...].astype(F32) - (points - 1) / 2.0) * (8.0 / points)
    vel_x, vel_y, vel_z = comps[0:1], comps[1:2], comps[2:3]
    moments = moment_rows(vel_x, vel_y, vel_z, (8.0 / points) ** 3, jnp)
    high = moments.astype(BF16).astype(F32)
    shapes = state_rows(vel_x, vel_y, vel_z, jnp)
    part_a = shapes.astype(BF16).astype(F32)
    part_b = (shapes - part_a).astype(BF16).astype(F32)
    part_c = shapes - part_a - part_b
    width = vel_x.shape[1]
    rows = jnp.concatenate(
        [
            *[part_a] * 3,
            *[part_b] * 2,
            part_c,
            high,
            jnp.zeros((3, width), F32),
            moments - high,
            jnp.zeros((3, width), F32),
            STEP_RATIO * jnp.abs(vel_x),
            STEP_RATIO * jnp.abs(vel_y),
            jnp.where(vel_y > 0, 0.5, -0.5),
            jnp.zeros((45, width), F32),
        ]
    )
    columns = rows.T
    table_ref[...] = columns[:, :48].astype(BF16)
    weight_ref[...] = columns[:, 48:80].astype(BF16)
    const_ref[...] = columns[:, 80:88]


def prepare(points, vel_index):
    count = vel_index.shape[1]
    vmem = pl.BlockSpec(memory_space=pltpu.VMEM)
    return pl.pallas_call(
        functools.partial(prepare_kernel, points),
        out_shape=(
            jax.ShapeDtypeStruct((count, 48), BF16),
            jax.ShapeDtypeStruct((count, 8), F32),
            jax.ShapeDtypeStruct((count, 32), BF16),
        ),
        in_specs=[vmem],
        out_specs=[vmem] * 3,
        compiler_params=params(),
        name="prepare",
        cost_estimate=pl.CostEstimate(
            flops=200 * count, transcendentals=count, bytes_accessed=count * 1000
        ),
    )(vel_index)


def weighted(weight_ref, values):
    over_rows = (((0,), (0,)), ((), ()))
    total = None
    for start in range(0, weight_ref.shape[0], 144):
        weights = weight_ref[start : start + 144, :]
        value = jnp.concatenate(values(start), axis=1)
        high = value.astype(BF16)
        low = (value - high.astype(F32)).astype(BF16)
        both = lax.dot_general(weights, high, over_rows, preferred_element_type=F32)
        rest = lax.dot_general(weights, low, over_rows, preferred_element_type=F32)
        part = both[:16] + both[16:] + rest[:16]
        total = part if total is None else total + part
    return total


def moment_kernel(size, side_ref, dist_ref, weight_ref, out_ref, lowest_ref):
    side = side_ref[0]
    step = pl.program_id(0)
    half_steps = pl.num_programs(0) // 2

    @pl.when(step == 0)
    def _():
        out_ref[...] = jnp.zeros_like(out_ref)

    @pl.when(jnp.where(step >= half_steps, 1, 0) == side)
    def _():
        lowest_ref[...] = dist_ref[strided(jnp.where(side == 1, 3, 0), size), :]

    for pair in range(0, STRIP_ROWS, 2):
        def values(start, pair=pair):
            return [
                dist_ref[strided(STRIP_ROWS * start + row, 144), :] for row in (pair, pair + 1)
            ]

        out_ref[:, pair * LANES : (pair + 2) * LANES] += weighted(weight_ref, values)


def home_moments(side, flat, weights, size):
    count = flat.shape[0] // STRIP_ROWS
    width = STRIP_ROWS * LANES
    half_steps = count // size // 2
    return pl.pallas_call(
        functools.partial(moment_kernel, size),
        out_shape=(
            jax.ShapeDtypeStruct((16, width), F32),
            jax.ShapeDtypeStruct((count // 2, LANES), F32),
        ),
        grid_spec=pltpu.PrefetchScalarGridSpec(
            num_scalar_prefetch=1,
            grid=(2 * half_steps,),
            in_specs=[
                pl.BlockSpec((4 * size, LANES), lambda i, s: (i, 0)),
                pl.BlockSpec((size, 32), lambda i, s: (i, 0)),
            ],
            out_specs=[
                pl.BlockSpec((16, width), lambda i, s: (0, 0)),
                pl.BlockSpec(
                    (size, LANES), lambda i, s: (jnp.clip(i - s[0] * half_steps, 0, half_steps - 1), 0)
                ),
            ],
        ),
        compiler_params=params(),
        name="home_moments",
        cost_estimate=pl.CostEstimate(
            flops=2 * 64 * count * width, transcendentals=0, bytes_accessed=count * width * 4
        ),
    )(side, flat, weights)


def transport_kernel(size, second_pass, side_ref, *refs):
    if second_pass:
        (table_ref, change_ref, q_first, q_mid, q_edge, up_ref, down_ref, *rest) = refs
    else:
        (own_ref, mid_ref, edge_ref, up_ref, down_ref, *rest) = refs
    (const_ref, weight_ref, cell_ref, sum_in_ref, *rest) = rest
    if second_pass:
        (near_out, far_out, sum_ref, lift_ref) = rest[-4:]
    else:
        (first_out, mid_out, edge_out, sum_ref) = rest[-4:]
    side = side_ref[0]
    group_size = 32 if size % 32 == 0 else 16

    @pl.when(pl.program_id(0) == 0)
    def _():
        sum_ref[...] = sum_in_ref[...]

    if second_pass:
        lift_ref[...] = jnp.dot(table_ref[...], change_ref[...], preferred_element_type=F32)

    def row_out(row):
        if second_pass:
            return near_out.at[row] if row < 4 else far_out.at[row - 4]
        if row == 0:
            return first_out
        return mid_out.at[row - 1] if row < 6 else edge_out.at[row - 6]

    lane = lax.broadcasted_iota(jnp.int32, (group_size, LANES), 1)
    inner_low = jnp.where(lane == 0, 0.0, 1.0)
    inner_high = jnp.where(lane == LANES - 1, 0.0, 1.0)

    def body(group, carry):
        base = pl.multiple_of(group * group_size, group_size)
        rows = pl.ds(base, group_size)

        def load(row):
            if row < 0:
                value = up_ref[row + 2, rows, :]
            elif row == 8:
                value = down_ref[rows, :]
            elif second_pass:
                if row == 0:
                    value = q_first[rows, :]
                elif row < 6:
                    value = q_mid[row - 1, rows, :]
                else:
                    value = q_edge[row - 6, rows, :]
            elif row < 4:
                local = jnp.where(side == 1, 3 - row, row)
                value = own_ref[strided(base * STRIP_ROWS + local, group_size), :]
            elif row < 6:
                value = mid_ref[row - 4, rows, :]
            else:
                value = edge_ref[row - 6, rows, :]
            if second_pass:
                value = value + lift_ref[rows, pl.ds((row + 2) * LANES, LANES)]
            return value

        def wide(column):
            return jnp.broadcast_to(const_ref[rows, column : column + 1], (group_size, LANES))

        speed_x = wide(0)
        speed_y = wide(1)
        half_sign = wide(2)
        forward = half_sign > 0.0
        open_end = jnp.where(forward, inner_low, inner_high)

        behind = load(-2)
        here = load(-1)
        ahead = load(0)
        step = ahead - here
        upwind = here + 0.5 * minmod(here - behind, step)
        here = ahead
        for row in range(BLOCK_ROWS):
            ahead = load(row + 1)
            next_step = ahead - here
            next_upwind = here + 0.5 * minmod(step, next_step)
            drift = speed_x * (next_upwind - upwind)
            step = next_step
            upwind = next_upwind
            left = here - pltpu.roll(here, 1, 1) * inner_low
            right = pltpu.roll(here, LANES - 1, 1) * inner_high - here
            face = here + half_sign * minmod(left, right)
            other = jnp.where(forward, pltpu.roll(face, 1, 1), pltpu.roll(face, LANES - 1, 1))
            drift = drift + speed_y * (face - other * open_end)
            keep = jnp.broadcast_to(cell_ref[row : row + 1, :], (group_size, LANES))
            fluid = jnp.broadcast_to(cell_ref[row + 8 : row + 9, :], (group_size, LANES))
            value = keep * here - fluid * drift
            row_out(row)[rows, :] = value
            here = ahead
        return carry

    lax.fori_loop(0, size // group_size, body, 0)
    for pair in range(0, BLOCK_ROWS, 2):
        def values(start, pair=pair):
            return [row_out(row)[start : start + 144, :] for row in (pair, pair + 1)]

        part = weighted(weight_ref, values)
        for row in (pair, pair + 1):
            place = jnp.where(side == 1, 7 - row, row)
            columns = pl.ds(pl.multiple_of(place * LANES, LANES), LANES)
            sum_ref[:, columns] += part[:, (row - pair) * LANES : (row - pair + 1) * LANES]


def transport(
    side, sources, tables, cells, sums, half, chunk, first, size, change=None, skip=0, group=None, into=None
):
    second_pass = change is not None
    steps = chunk // size
    shift = half // size
    begin = first // size
    offset = skip // size
    table, const, weights = tables
    width = BLOCK_ROWS * LANES

    def mine(i, s):
        return s[0] * shift + begin + i

    def stack_of(count, at):
        return pl.BlockSpec((count, size, LANES), lambda i, s: (0, at + i, 0))

    aliases = {}
    if second_pass:
        args = [table, change]
        specs = [
            pl.BlockSpec((size, 48), lambda i, s: (mine(i, s), 0)),
            pl.BlockSpec(change.shape, lambda i, s: (0, 0)),
            stack_of(None, offset),
            stack_of(5, offset),
            stack_of(2, offset),
            stack_of(2, offset),
            stack_of(None, offset),
        ]
        outs = [jax.ShapeDtypeStruct((4, n, LANES), F32) for n in (half, chunk)]
        out_specs = [stack_of(4, begin), stack_of(4, 0)]
        scratch = [pltpu.VMEM((size, 11 * LANES), F32)]
    else:
        args = []
        specs = [
            pl.BlockSpec((4 * size, LANES), lambda i, s: (mine(i, s), 0)),
            stack_of(2, 0),
            stack_of(2, 0),
            stack_of(2, 0),
            pl.BlockSpec((size, LANES), lambda i, s: (begin + i, 0)),
        ]
        outs = [jax.ShapeDtypeStruct((n, group, LANES), F32) for n in (1, 5, 2)]
        out_specs = [stack_of(None, offset), stack_of(5, offset), stack_of(2, offset)]
        scratch = []
    whole = pl.BlockSpec((16, width), lambda i, s: (0, 0))
    args = [side, *args, *sources, const, weights, cells, sums]
    specs = [
        *specs,
        pl.BlockSpec((size, 8), lambda i, s: (mine(i, s), 0)),
        pl.BlockSpec((size, 32), lambda i, s: (mine(i, s), 0)),
        pl.BlockSpec((16, LANES), lambda i, s: (0, 0)),
        whole,
    ]
    if into is not None:
        aliases = {len(args) + n: n for n in range(len(into))}
        args = [*args, *into]
        specs = [*specs, *[pl.BlockSpec(memory_space=pl.ANY)] * len(into)]
    return pl.pallas_call(
        functools.partial(transport_kernel, size, second_pass),
        out_shape=(*outs, jax.ShapeDtypeStruct((16, width), F32)),
        grid_spec=pltpu.PrefetchScalarGridSpec(
            num_scalar_prefetch=1,
            grid=(steps,),
            in_specs=specs,
            out_specs=[*out_specs, whole],
            scratch_shapes=scratch,
        ),
        input_output_aliases=aliases,
        compiler_params=params(),
        name="transport_second" if second_pass else "transport_first",
        cost_estimate=pl.CostEstimate(
            flops=60 * chunk * width, transcendentals=0, bytes_accessed=chunk * LANES * 4 * 19
        ),
    )(*args)


def sweep_block(inputs, relax, rate):
    start, flux_x, flux_y = inputs
    lane = lax.broadcasted_iota(jnp.int32, (8, LANES), 1)
    inner_low = jnp.where(lane == 0, 0.0, 1.0)
    inner_high = jnp.where(lane == LANES - 1, 0.0, 1.0)

    def block(array, row):
        if row < 0 or row >= SPAN:
            return jnp.zeros((8, LANES), F32)
        return array[:, row * LANES : (row + 1) * LANES]

    def lower(value):
        return pltpu.roll(value, 1, 1) * inner_low

    def upper(value):
        return pltpu.roll(value, LANES - 1, 1) * inner_high

    source = []
    for row in range(SPAN):
        diff_x = 0.5 * (block(flux_x, row + 1) - block(flux_x, row - 1))
        side = block(flux_y, row)
        diff_y = 0.5 * (upper(side) - lower(side))
        source.append(block(start, row) - SOURCE_WEIGHT * (diff_x + diff_y))
    zero = jnp.zeros((8, LANES), F32)
    kappa = [block(rate, row) for row in range(SPAN)]
    scale = [block(relax, row) for row in range(SPAN)]
    state = [block(start, row) for row in range(SPAN)]
    for _ in range(SWEEPS):
        near = [zero, *state, zero]
        state = [
            (source[row] + kappa[row] * (near[row] + near[row + 2] + lower(near[row + 1]) + upper(near[row + 1])))
            * scale[row]
            for row in range(SPAN)
        ]
    return jnp.concatenate(state, axis=1)


def stacked(value):
    first = value.astype(BF16)
    rest = value - first.astype(F32)
    second = rest.astype(BF16)
    third = (rest - second.astype(F32)).astype(BF16)
    return jnp.concatenate([first, second, third, first, second, first], axis=0)


def relax_rows(rate):
    inside = rate > 0.0
    kappa = jnp.where(inside, 0.5 / jnp.where(inside, rate, 1.0), 0.0)
    scale = jnp.where(inside, 1.0 / (1.0 + 4.0 * kappa), 0.0)
    width = rate.shape[1]
    return jnp.broadcast_to(kappa, (8, width)), jnp.broadcast_to(scale, (8, width))


def place_blocks(info_ref, span_ref, own, pair_a, pair_b):
    odd = info_ref[1]
    width = BLOCK_ROWS * LANES
    span_ref[:, width : 2 * width] = own
    place_a = pl.multiple_of((1 - odd) * 2 * width, width)
    place_b = pl.multiple_of(odd * 2 * width, width)
    span_ref[:, pl.ds(place_a, width)] = pair_a
    span_ref[:, pl.ds(place_b, width)] = pair_b


def first_macro_kernel(
    info_ref, sum_ref, home_own_ref, both_a_ref, both_b_ref, gram_ref, mat_ref,
    change_ref, keep_ref, span_ref, home_ref,
):
    side = info_ref[0]
    odd = info_ref[1]
    width = BLOCK_ROWS * LANES
    part = STRIP_ROWS * LANES
    place_blocks(info_ref, span_ref, sum_ref[...], both_a_ref[:16, :], both_b_ref[:16, :])
    homes = (home_own_ref[...], both_a_ref[16:, :], both_b_ref[16:, :])
    for block, both in zip((1, (1 - odd) * 2, odd * 2), homes):
        for where, rows in ((side, both[:, :part]), (1 - side, both[:, part:])):
            spot = pl.multiple_of(block * width + where * part, part)
            home_ref[:, pl.ds(spot, part)] = rows
    home = home_ref[...]
    rate = home[13:14, :]
    ratio = jnp.where(home[14:15, :] > 0.5, 1.0, rate)
    mat = mat_ref[...]
    first = jnp.dot(mat, jnp.where(lax.broadcasted_iota(jnp.int32, home.shape, 0) < 13, home, 0.0), precision=HIGH)
    fields = first[:8] + first[24:]
    moments = span_ref[...] + ratio * jnp.dot(gram_ref[...], fields, precision=HIGH)
    all_parts = jnp.dot(mat, moments, precision=HIGH)
    start = all_parts[:8]
    kappa, scale = relax_rows(rate)
    state = sweep_block((start, all_parts[8:16], all_parts[16:24]), scale, kappa)
    change = ratio * fields + (state - start)
    span_ref[0:8, :] = change
    keep_ref[0:8, :] = state + all_parts[24:]
    keep_ref[8:9, :] = rate
    keep_ref[9:10, :] = ratio
    keep_ref[10:16, :] = jnp.zeros((6, SPAN * LANES), F32)
    for row in range(-2, 9):
        spot = jnp.where(side == 1, 15 - row, 8 + row)
        piece = span_ref[0:8, pl.ds(pl.multiple_of(spot * LANES, LANES), LANES)]
        change_ref[:, (row + 2) * LANES : (row + 3) * LANES] = stacked(piece)


def last_kernel(
    size, half, blocks, info_ref, sum_ref, sum_a_ref, sum_b_ref, keep_ref, gram_ref, mat_ref,
    table_ref, *refs
):
    count = len({source for source, *_ in blocks})
    sources = refs[:count]
    out_ref, change_ref, state_ref, span_ref, held_ref, ready_ref, in_sems, out_sems = refs[count:]
    side = info_ref[0]

    def copy_in(k):
        source, offset, _, _ = blocks[k]
        return pltpu.make_async_copy(
            sources[source].at[:, pl.ds(offset, size), :], held_ref.at[k], in_sems.at[k]
        )

    for k in range(len(blocks)):
        copy_in(k).start()
    place_blocks(info_ref, span_ref, sum_ref[...], sum_a_ref[...], sum_b_ref[...])
    fields = keep_ref[0:8, :]
    rate = keep_ref[8:9, :]
    ratio = keep_ref[9:10, :]
    moments = span_ref[...] + ratio * jnp.dot(gram_ref[...], fields, precision=HIGH)
    all_parts = jnp.dot(mat_ref[...], moments, precision=HIGH)
    start = all_parts[:8]
    kappa, scale = relax_rows(rate)
    state = sweep_block((start, all_parts[8:16], all_parts[16:24]), scale, kappa)
    span_ref[0:8, :] = ratio * fields + (state - start)
    span_ref[8:16, :] = state
    part = STRIP_ROWS * LANES
    spot = pl.ds(pl.multiple_of(2 * part + side * part, part), part)
    change_ref[...] = stacked(span_ref[0:8, spot])
    state = span_ref[8:16, spot]
    for row in range(STRIP_ROWS):
        state_ref[:, row, :] = state[:5, row * LANES : (row + 1) * LANES]

    def copy_out(k):
        _, offset, own, first = blocks[k]
        begin = (side if own else 1 - side) * half + first + offset
        return begin, pltpu.make_async_copy(
            ready_ref.at[k],
            out_ref.at[pl.ds(pl.multiple_of(begin * STRIP_ROWS, STRIP_ROWS * size), STRIP_ROWS * size), :],
            out_sems.at[k],
        )

    for k, (_, _, own, _) in enumerate(blocks):
        begin, copy = copy_out(k)
        lift = jnp.dot(
            table_ref[pl.ds(pl.multiple_of(begin, size), size), :],
            change_ref[...],
            preferred_element_type=F32,
        )
        copy_in(k).wait()
        flipped = side == (1 if own else 0)
        for row in range(STRIP_ROWS):
            index = jnp.where(flipped, 3 - row, row)
            ready_ref[k, strided(row, size), :] = (
                held_ref[k, index] + lift[:, row * LANES : (row + 1) * LANES]
            )
        copy.start()
    for k in range(len(blocks)):
        copy_out(k)[1].wait()


def last_macro(info, args, table, pieces, half, size):
    blocks = [
        (source, offset, own, first)
        for source, (rows, own, first) in enumerate(pieces)
        for offset in range(0, rows.shape[1], size)
    ]
    whole = pl.BlockSpec(memory_space=pltpu.VMEM)
    anywhere = pl.BlockSpec(memory_space=pl.ANY)
    return pl.pallas_call(
        functools.partial(last_kernel, size, half, blocks),
        out_shape=[
            jax.ShapeDtypeStruct((2 * half * STRIP_ROWS, LANES), F32),
            jax.ShapeDtypeStruct((48, STRIP_ROWS * LANES), BF16),
            jax.ShapeDtypeStruct((5, STRIP_ROWS, LANES), F32),
        ],
        in_specs=[
            pl.BlockSpec(memory_space=pltpu.SMEM),
            *[whole] * (len(args) + 1),
            *[anywhere] * len(pieces),
        ],
        out_specs=[anywhere, whole, whole],
        scratch_shapes=[
            pltpu.VMEM((16, SPAN * LANES), F32),
            pltpu.VMEM((len(blocks), STRIP_ROWS, size, LANES), F32),
            pltpu.VMEM((len(blocks), STRIP_ROWS * size, LANES), F32),
            pltpu.SemaphoreType.DMA((len(blocks),)),
            pltpu.SemaphoreType.DMA((len(blocks),)),
        ],
        compiler_params=params(63 * 1024 * 1024),
        name="last_macro",
        cost_estimate=pl.CostEstimate(
            flops=4000000, transcendentals=0, bytes_accessed=len(blocks) * size * LANES * 32
        ),
    )(info, *args, table, *[rows for rows, _, _ in pieces])


def macro(kernel, info, args, outs, scratch):
    vmem = pl.BlockSpec(memory_space=pltpu.VMEM)
    return pl.pallas_call(
        kernel,
        out_shape=outs,
        in_specs=[pl.BlockSpec(memory_space=pltpu.SMEM)] + [vmem] * len(args),
        out_specs=[vmem] * len(outs),
        scratch_shapes=scratch,
        compiler_params=params(),
        cost_estimate=pl.CostEstimate(flops=4000000, transcendentals=0, bytes_accessed=1000000),
    )(info, *args)


def finish_kernel(size, parts, side_ref, *refs):
    out_ref = refs[-1]
    rows = refs[: len(parts)]
    table_ref, change_ref = refs[len(parts) : len(parts) + 2]
    side = side_ref[0]
    step = pl.program_id(0)
    lift = jnp.dot(table_ref[...], change_ref[...], preferred_element_type=F32)
    for ref, (own, begin, count, _) in zip(rows, parts):

        @pl.when((step >= begin) & (step < begin + count))
        def _(ref=ref, flipped=(side == (1 if own else 0))):
            for row in range(STRIP_ROWS):
                index = jnp.where(flipped, 3 - row, row)
                out_ref[strided(row, size), :] = (
                    ref[index] + lift[:, row * LANES : (row + 1) * LANES]
                )


def finish(side, out, pieces, table, change, half, size):
    shift = half // size
    parts = []
    steps = 0
    for rows, own, first in pieces:
        count = rows.shape[1] // size
        parts.append((own, steps, count, first // size))
        steps += count

    def place(i, s):
        spot = 0
        for own, begin, count, at in parts:
            here = (s[0] if own else 1 - s[0]) * shift + at + i - begin
            spot = jnp.where(i >= begin, here, spot)
        return spot

    def rows_spec(begin, count):
        return pl.BlockSpec(
            (4, size, LANES), lambda i, s: (0, jnp.clip(i - begin, 0, count - 1), 0)
        )

    specs = [
        *[rows_spec(begin, count) for _, begin, count, _ in parts],
        pl.BlockSpec((size, 48), lambda i, s: (place(i, s), 0)),
        pl.BlockSpec(change.shape, lambda i, s: (0, 0)),
    ]
    args = [side, *[rows for rows, _, _ in pieces], table, change]
    aliases = {}
    if out is not None:
        specs.append(pl.BlockSpec(memory_space=pl.ANY))
        aliases = {len(args): 0}
        args.append(out)
    return pl.pallas_call(
        functools.partial(finish_kernel, size, parts),
        out_shape=jax.ShapeDtypeStruct((2 * half * STRIP_ROWS, LANES), F32),
        grid_spec=pltpu.PrefetchScalarGridSpec(
            num_scalar_prefetch=1,
            grid=(steps,),
            in_specs=specs,
            out_specs=pl.BlockSpec((4 * size, LANES), lambda i, s: (place(i, s), 0)),
        ),
        input_output_aliases=aliases,
        compiler_params=params(67043328),
        name="finish",
        cost_estimate=pl.CostEstimate(
            flops=2 * 48 * 4 * LANES * steps * size,
            transcendentals=0,
            bytes_accessed=steps * size * LANES * 4 * 8,
        ),
    )(*args)


def per_device(points, dist, cell_type, collision_rate, vel_index):
    count, rows, cols = dist.shape
    half = count // 2
    strips = lax.axis_size("strip")
    groups = lax.axis_size("vel")
    strip = lax.axis_index("strip")
    size, chunks = plan(half)
    firsts = [sum(chunks[:c]) for c in range(len(chunks))]
    order = range(len(chunks))
    groups_of = [order[:1], order[1:2], order[2:]]
    items = second_items(chunks)
    early = len(items) - len(groups_of[2])
    side = (strip % 2).astype(jnp.int32).reshape(1)
    info = jnp.stack([strip % 2, (strip // 2) % 2]).astype(jnp.int32)

    swap_pairs = [(s, s ^ 1) for s in range(strips)]
    down_pairs = [
        (s, s + (2 if s % 2 == 0 else -2))
        for s in range(strips)
        if 0 <= s + (2 if s % 2 == 0 else -2) < strips
    ]
    up_pairs = [(b, a) for a, b in down_pairs]
    pair_a = [
        (s, s + (2 if (s // 2) % 2 == 0 else -2))
        for s in range(strips)
        if 0 <= s + (2 if (s // 2) % 2 == 0 else -2) < strips
    ]
    pair_b = [
        (s, s + (-2 if (s // 2) % 2 == 0 else 2))
        for s in range(strips)
        if 0 <= s + (-2 if (s // 2) % 2 == 0 else 2) < strips
    ]

    def swap(value):
        return lax.ppermute(value, "strip", swap_pairs)

    def with_flow(value):
        return lax.ppermute(value, "strip", down_pairs)

    def against_flow(value):
        return lax.ppermute(value, "strip", up_pairs)

    def both_z(value):
        return lax.ppermute(value, "strip", pair_a), lax.ppermute(value, "strip", pair_b)

    def sum_groups(value):
        total = value
        for shift in range(1, groups):
            total = total + lax.ppermute(
                value, "vel", [(g, (g + shift) % groups) for g in range(groups)]
            )
        return total

    flat = dist.reshape(count * rows, cols)
    wall = (cell_type == 1).astype(F32)
    cell_pair = jnp.concatenate([collision_rate, wall])
    other_cells = swap(cell_pair)

    packed = pack(side, flat, half, chunks[:1], 0, size)
    packed += pack(side, flat, half, chunks[1:], firsts[1], size)
    got, above = [], []
    for edge, mid in packed:
        edge = swap(edge)
        mid = swap(mid)
        above.append(with_flow(edge))
        got.append((mid, edge))
    tables = prepare(points, vel_index)
    table, _, weights = tables
    home, lowest = home_moments(side, flat, weights, half // 3)
    below = against_flow(lowest)
    gram = jnp.asarray(target_moments(points))
    mat = jnp.asarray(macro_matrix())

    def flow(own, other):
        odd = strip % 2 == 1
        return jnp.concatenate(
            [jnp.where(odd, own[::-1], own), jnp.where(odd, other[::-1], other)]
        )

    flow_rate = flow(collision_rate, other_cells[:rows])
    flow_fluid = 1.0 - flow(wall, other_cells[rows:])
    cells = jnp.concatenate([flow_fluid * (1.0 - flow_rate), flow_fluid])

    home = sum_groups(home)
    home = jnp.concatenate(
        [home[:13], collision_rate.reshape(1, -1), wall.reshape(1, -1), jnp.zeros((1, rows * cols), F32)]
    )
    home = jnp.concatenate([home, swap(home)], axis=1)

    width = BLOCK_ROWS * LANES
    sums = jnp.zeros((16, width), F32)
    kept = []
    for members in groups_of:
        start = firsts[members[0]]
        length = sum(chunks[c] for c in members)
        held = None
        for c in members:
            *held, sums = transport(
                side, [flat, *got[c], above[c], below], tables, cells, sums, half,
                chunks[c], firsts[c], size, skip=firsts[c] - start, group=length, into=held,
            )
        next_above = with_flow(held[2])
        next_below = against_flow(held[0])
        kept.append((*held, next_above, next_below))

    total = sum_groups(sums)
    total = total + swap(total)
    both_a, both_b = both_z(jnp.concatenate([total, home]))
    change, keep = macro(
        first_macro_kernel, info,
        [total, home, both_a, both_b, gram, mat],
        [
            jax.ShapeDtypeStruct((48, 11 * LANES), BF16),
            jax.ShapeDtypeStruct((16, SPAN * LANES), F32),
        ],
        [pltpu.VMEM((16, SPAN * LANES), F32)] * 2,
    )

    sums = jnp.zeros((16, width), F32)
    near, back = None, []
    for number, first, length in items:
        start = firsts[groups_of[number][0]]
        near, far, sums = transport(
            side, list(kept[number]), tables, cells, sums, half, length, first, size, change,
            skip=first - start, into=None if near is None else [near],
        )
        back.append(swap(far))
    total = sum_groups(sums)
    total = total + swap(total)
    sum_a, sum_b = both_z(total)
    returned = [(rows, False, first) for rows, (_, first, _) in zip(back, items)]
    pieces = [(near, True, 0), *returned[:early]]
    out, change, state = last_macro(
        info, [total, sum_a, sum_b, keep, gram, mat], table, pieces, half, size
    )
    for piece in returned[early:]:
        out = finish(side, out, [piece], table, change, half, size)
    return out.reshape(dist.shape), state


def solution(mesh):
    def whole(dist, cell_type, collision_rate, vel_index):
        points = round(vel_index.shape[1] ** (1.0 / 3.0))
        in_specs = (P("vel", "strip", None), P("strip", None), P("strip", None), P(None, "vel"))
        out_specs = (P("vel", "strip", None), P(None, "strip", None))

        def body(*args):
            return per_device(points, *args)

        run = jax.shard_map(
            body, mesh=mesh, in_specs=in_specs, out_specs=out_specs, check_vma=False
        )
        return run(dist, cell_type, collision_rate, vel_index)

    return whole
```

```python
import functools
import math

import jax
import jax.numpy as jnp
import numpy as np
from jax import lax
from jax.experimental import pallas as pl
from jax.experimental.pallas import tpu as pltpu
from jax.sharding import PartitionSpec as P


STEP_RATIO = 0.1
SOURCE_WEIGHT = 0.5
HEAT_WEIGHT = 4.0 / 15.0
SWEEPS = 3
HIGH = lax.Precision.HIGHEST
LANES = 128
STRIP_ROWS = 4
BLOCK_ROWS = 2 * STRIP_ROWS
SPAN = 3 * BLOCK_ROWS
F32 = jnp.float32
BF16 = jnp.bfloat16


def params(limit=66584576):
    return pltpu.CompilerParams(vmem_limit_bytes=limit)


def plan(half):
    block = 288 if half % 288 == 0 else 144
    blocks = half // block
    if blocks % 6 == 0:
        unit = block * (blocks // 6)
        return block, [2 * unit, unit, unit, unit, unit]
    return block, [block * (blocks - 2), block, block]


def second_order(pieces):
    cut = (pieces + 1) // 2
    return [*range(1, cut), 0, *range(cut, pieces)], cut


def moment_rows(vel_x, vel_y, vel_z, volume, lib):
    energy = vel_x * vel_x + vel_y * vel_y + vel_z * vel_z
    weight = volume * math.pi ** (-1.5) * lib.exp(-energy)
    rows = [
        lib.ones_like(vel_x),
        vel_x,
        vel_y,
        vel_z,
        energy,
        vel_x * vel_x,
        vel_y * vel_y,
        vel_x * vel_y,
        vel_x * vel_z,
        vel_y * vel_z,
        energy * vel_x,
        energy * vel_y,
        energy * vel_z,
    ]
    return lib.concatenate([(row * weight).reshape(1, -1) for row in rows])


def state_rows(vel_x, vel_y, vel_z, lib):
    energy = vel_x * vel_x + vel_y * vel_y + vel_z * vel_z
    shape_heat = HEAT_WEIGHT * (energy - 2.5)
    rows = [
        lib.ones_like(vel_x),
        2.0 * vel_x,
        2.0 * vel_y,
        2.0 * vel_z,
        energy - 1.5,
        shape_heat * vel_x,
        shape_heat * vel_y,
        shape_heat * vel_z,
    ]
    return lib.concatenate([row.reshape(1, -1) for row in rows])


def target_moments(points):
    line = (np.arange(points) - (points - 1) / 2.0) * (8.0 / points)
    comps = [a.reshape(-1) for a in np.meshgrid(line, line, line, indexing="ij")]
    gram = moment_rows(*comps, (8.0 / points) ** 3, np) @ state_rows(*comps, np).T
    gram[np.abs(gram) < 1e-12] = 0.0
    full = np.zeros((16, 8), np.float32)
    full[:13] = gram
    return full


def macro_matrix():
    third = 2.0 / 3.0
    unit = np.eye(16, dtype=np.float64)
    start = [unit[0], unit[1], unit[2], unit[3], third * unit[4] - unit[0]]
    heat = [unit[10] - 2.5 * unit[1], unit[11] - 2.5 * unit[2], unit[12] - 2.5 * unit[3]]
    flux = [
        unit[1],
        unit[2],
        2.0 * unit[5] - third * unit[4],
        2.0 * unit[7],
        2.0 * unit[6] - third * unit[4],
        2.0 * unit[8],
        2.0 * unit[9],
        heat[0],
        heat[1],
    ]
    out = np.zeros((32, 16), np.float64)
    for row in range(5):
        out[row] = start[row]
        out[8 + row] = flux[(0, 2, 3, 5, 7)[row]]
        out[16 + row] = flux[(1, 3, 4, 6, 8)[row]]
    for row in range(3):
        out[24 + 5 + row] = heat[row]
    return out.astype(np.float32)


def minmod(left, right):
    return jnp.maximum(jnp.minimum(right, jnp.maximum(left, 0.0)), jnp.minimum(left, 0.0))


def strided(start, count):
    return pl.ds(start, count, stride=STRIP_ROWS)


def pack_kernel(size, begins, counts, side_ref, far_ref, *rest):
    outs = rest[-2 * len(begins) :]
    side = side_ref[0]
    step = pl.program_id(0)
    for c, (begin, count) in enumerate(zip(begins, counts)):

        @pl.when((step >= begin) & (step < begin + count))
        def _():
            for i in range(STRIP_ROWS):
                row = jnp.where(side == 1, i, 3 - i)
                outs[2 * c + (1 if i < 2 else 0)][i % 2] = far_ref[strided(row, size), :]


def pack(side, flat, half, chunks, first, size):
    counts = [n // size for n in chunks]
    begins = [sum(counts[:c]) for c in range(len(chunks))]
    shift = half // size
    start = first // size

    def out_spec(c):
        return pl.BlockSpec(
            (2, size, LANES), lambda i, s: (0, jnp.clip(i - begins[c], 0, counts[c] - 1), 0)
        )

    outs = pl.pallas_call(
        functools.partial(pack_kernel, size, begins, counts),
        out_shape=[
            jax.ShapeDtypeStruct((2, n, LANES), F32) for n in chunks for _ in range(2)
        ],
        grid_spec=pltpu.PrefetchScalarGridSpec(
            num_scalar_prefetch=1,
            grid=(sum(counts),),
            in_specs=[
                pl.BlockSpec((4 * size, LANES), lambda i, s: ((1 - s[0]) * shift + start + i, 0))
            ],
            out_specs=[out_spec(c) for c in range(len(chunks)) for _ in range(2)],
        ),
        compiler_params=params(),
        name="pack",
        cost_estimate=pl.CostEstimate(
            flops=0, transcendentals=0, bytes_accessed=sum(chunks) * LANES * 4 * 8
        ),
    )(side, flat)
    return [(outs[2 * c], outs[2 * c + 1]) for c in range(len(chunks))]


def prepare_kernel(points, vel_ref, table_ref, const_ref, weight_ref):
    comps = (vel_ref[...].astype(F32) - (points - 1) / 2.0) * (8.0 / points)
    vel_x, vel_y, vel_z = comps[0:1], comps[1:2], comps[2:3]
    moments = moment_rows(vel_x, vel_y, vel_z, (8.0 / points) ** 3, jnp)
    high = moments.astype(BF16).astype(F32)
    shapes = state_rows(vel_x, vel_y, vel_z, jnp)
    part_a = shapes.astype(BF16).astype(F32)
    part_b = (shapes - part_a).astype(BF16).astype(F32)
    part_c = shapes - part_a - part_b
    width = vel_x.shape[1]
    rows = jnp.concatenate(
        [
            *[part_a] * 3,
            *[part_b] * 2,
            part_c,
            high,
            jnp.zeros((3, width), F32),
            moments - high,
            jnp.zeros((3, width), F32),
            STEP_RATIO * jnp.abs(vel_x),
            STEP_RATIO * jnp.abs(vel_y),
            jnp.where(vel_y > 0, 0.5, -0.5),
            jnp.zeros((45, width), F32),
        ]
    )
    columns = rows.T
    table_ref[...] = columns[:, :48].astype(BF16)
    weight_ref[...] = columns[:, 48:80].astype(BF16)
    const_ref[...] = columns[:, 80:88]


def prepare(points, vel_index):
    count = vel_index.shape[1]
    vmem = pl.BlockSpec(memory_space=pltpu.VMEM)
    return pl.pallas_call(
        functools.partial(prepare_kernel, points),
        out_shape=(
            jax.ShapeDtypeStruct((count, 48), BF16),
            jax.ShapeDtypeStruct((count, 8), F32),
            jax.ShapeDtypeStruct((count, 32), BF16),
        ),
        in_specs=[vmem],
        out_specs=[vmem] * 3,
        compiler_params=params(),
        name="prepare",
        cost_estimate=pl.CostEstimate(
            flops=200 * count, transcendentals=count, bytes_accessed=count * 1000
        ),
    )(vel_index)


def weighted(weight_ref, values):
    over_rows = (((0,), (0,)), ((), ()))
    total = None
    for start in range(0, weight_ref.shape[0], 144):
        weights = weight_ref[start : start + 144, :]
        value = jnp.concatenate(values(start), axis=1)
        high = value.astype(BF16)
        low = (value - high.astype(F32)).astype(BF16)
        both = lax.dot_general(weights, high, over_rows, preferred_element_type=F32)
        rest = lax.dot_general(weights, low, over_rows, preferred_element_type=F32)
        part = both[:16] + both[16:] + rest[:16]
        total = part if total is None else total + part
    return total


def moment_kernel(size, side_ref, dist_ref, weight_ref, out_ref, lowest_ref):
    side = side_ref[0]
    step = pl.program_id(0)
    half_steps = pl.num_programs(0) // 2

    @pl.when(step == 0)
    def _():
        out_ref[...] = jnp.zeros_like(out_ref)

    @pl.when(jnp.where(step >= half_steps, 1, 0) == side)
    def _():
        lowest_ref[...] = dist_ref[strided(jnp.where(side == 1, 3, 0), size), :]

    for pair in range(0, STRIP_ROWS, 2):
        def values(start, pair=pair):
            return [
                dist_ref[strided(STRIP_ROWS * start + row, 144), :] for row in (pair, pair + 1)
            ]

        out_ref[:, pair * LANES : (pair + 2) * LANES] += weighted(weight_ref, values)


def home_moments(side, flat, weights, size):
    count = flat.shape[0] // STRIP_ROWS
    width = STRIP_ROWS * LANES
    half_steps = count // size // 2
    return pl.pallas_call(
        functools.partial(moment_kernel, size),
        out_shape=(
            jax.ShapeDtypeStruct((16, width), F32),
            jax.ShapeDtypeStruct((count // 2, LANES), F32),
        ),
        grid_spec=pltpu.PrefetchScalarGridSpec(
            num_scalar_prefetch=1,
            grid=(2 * half_steps,),
            in_specs=[
                pl.BlockSpec((4 * size, LANES), lambda i, s: (i, 0)),
                pl.BlockSpec((size, 32), lambda i, s: (i, 0)),
            ],
            out_specs=[
                pl.BlockSpec((16, width), lambda i, s: (0, 0)),
                pl.BlockSpec(
                    (size, LANES), lambda i, s: (jnp.clip(i - s[0] * half_steps, 0, half_steps - 1), 0)
                ),
            ],
        ),
        compiler_params=params(),
        name="home_moments",
        cost_estimate=pl.CostEstimate(
            flops=2 * 64 * count * width, transcendentals=0, bytes_accessed=count * width * 4
        ),
    )(side, flat, weights)


def transport_kernel(size, second_pass, side_ref, *refs):
    if second_pass:
        (table_ref, change_ref, q_first, q_mid, q_edge, up_ref, down_ref, *rest) = refs
    else:
        (own_ref, mid_ref, edge_ref, up_ref, down_ref, *rest) = refs
    (const_ref, weight_ref, cell_ref, sum_in_ref, *rest) = rest
    if second_pass:
        (near_out, far_out, sum_ref, lift_ref) = rest[-4:]
    else:
        (first_out, mid_out, edge_out, sum_ref) = rest[-4:]
    side = side_ref[0]
    group_size = 32 if size % 32 == 0 else 16

    @pl.when(pl.program_id(0) == 0)
    def _():
        sum_ref[...] = sum_in_ref[...]

    if second_pass:
        lift_ref[...] = jnp.dot(table_ref[...], change_ref[...], preferred_element_type=F32)

    def row_out(row):
        if second_pass:
            return near_out.at[row] if row < 4 else far_out.at[row - 4]
        if row == 0:
            return first_out
        return mid_out.at[row - 1] if row < 6 else edge_out.at[row - 6]

    lane = lax.broadcasted_iota(jnp.int32, (group_size, LANES), 1)
    inner_low = jnp.where(lane == 0, 0.0, 1.0)
    inner_high = jnp.where(lane == LANES - 1, 0.0, 1.0)

    def body(group, carry):
        base = pl.multiple_of(group * group_size, group_size)
        rows = pl.ds(base, group_size)

        def load(row):
            if row < 0:
                value = up_ref[row + 2, rows, :]
            elif row == 8:
                value = down_ref[rows, :]
            elif second_pass:
                if row == 0:
                    value = q_first[rows, :]
                elif row < 6:
                    value = q_mid[row - 1, rows, :]
                else:
                    value = q_edge[row - 6, rows, :]
            elif row < 4:
                local = jnp.where(side == 1, 3 - row, row)
                value = own_ref[strided(base * STRIP_ROWS + local, group_size), :]
            elif row < 6:
                value = mid_ref[row - 4, rows, :]
            else:
                value = edge_ref[row - 6, rows, :]
            if second_pass:
                value = value + lift_ref[rows, pl.ds((row + 2) * LANES, LANES)]
            return value

        def wide(column):
            return jnp.broadcast_to(const_ref[rows, column : column + 1], (group_size, LANES))

        speed_x = wide(0)
        speed_y = wide(1)
        half_sign = wide(2)
        forward = half_sign > 0.0
        open_end = jnp.where(forward, inner_low, inner_high)

        behind = load(-2)
        here = load(-1)
        ahead = load(0)
        step = ahead - here
        upwind = here + 0.5 * minmod(here - behind, step)
        here = ahead
        for row in range(BLOCK_ROWS):
            ahead = load(row + 1)
            next_step = ahead - here
            next_upwind = here + 0.5 * minmod(step, next_step)
            drift = speed_x * (next_upwind - upwind)
            step = next_step
            upwind = next_upwind
            left = here - pltpu.roll(here, 1, 1) * inner_low
            right = pltpu.roll(here, LANES - 1, 1) * inner_high - here
            face = here + half_sign * minmod(left, right)
            other = jnp.where(forward, pltpu.roll(face, 1, 1), pltpu.roll(face, LANES - 1, 1))
            drift = drift + speed_y * (face - other * open_end)
            keep = jnp.broadcast_to(cell_ref[row : row + 1, :], (group_size, LANES))
            fluid = jnp.broadcast_to(cell_ref[row + 8 : row + 9, :], (group_size, LANES))
            value = keep * here - fluid * drift
            row_out(row)[rows, :] = value
            here = ahead
        return carry

    lax.fori_loop(0, size // group_size, body, 0)
    for pair in range(0, BLOCK_ROWS, 2):
        def values(start, pair=pair):
            return [row_out(row)[start : start + 144, :] for row in (pair, pair + 1)]

        part = weighted(weight_ref, values)
        for row in (pair, pair + 1):
            place = jnp.where(side == 1, 7 - row, row)
            columns = pl.ds(pl.multiple_of(place * LANES, LANES), LANES)
            sum_ref[:, columns] += part[:, (row - pair) * LANES : (row - pair + 1) * LANES]


def transport(
    side, sources, tables, cells, sums, half, chunk, first, size, change=None, skip=0, group=None, into=None
):
    second_pass = change is not None
    steps = chunk // size
    shift = half // size
    begin = first // size
    offset = skip // size
    table, const, weights = tables
    width = BLOCK_ROWS * LANES

    def mine(i, s):
        return s[0] * shift + begin + i

    def stack_of(count, at):
        return pl.BlockSpec((count, size, LANES), lambda i, s: (0, at + i, 0))

    aliases = {}
    if second_pass:
        args = [table, change]
        specs = [
            pl.BlockSpec((size, 48), lambda i, s: (mine(i, s), 0)),
            pl.BlockSpec(change.shape, lambda i, s: (0, 0)),
            stack_of(None, offset),
            stack_of(5, offset),
            stack_of(2, offset),
            stack_of(2, offset),
            stack_of(None, offset),
        ]
        outs = [jax.ShapeDtypeStruct((4, n, LANES), F32) for n in (half, chunk)]
        out_specs = [stack_of(4, begin), stack_of(4, 0)]
        scratch = [pltpu.VMEM((size, 11 * LANES), F32)]
    else:
        args = []
        specs = [
            pl.BlockSpec((4 * size, LANES), lambda i, s: (mine(i, s), 0)),
            stack_of(2, 0),
            stack_of(2, 0),
            stack_of(2, 0),
            pl.BlockSpec((size, LANES), lambda i, s: (begin + i, 0)),
        ]
        outs = [jax.ShapeDtypeStruct((n, group, LANES), F32) for n in (1, 5, 2)]
        out_specs = [stack_of(None, offset), stack_of(5, offset), stack_of(2, offset)]
        scratch = []
    whole = pl.BlockSpec((16, width), lambda i, s: (0, 0))
    args = [side, *args, *sources, const, weights, cells, sums]
    specs = [
        *specs,
        pl.BlockSpec((size, 8), lambda i, s: (mine(i, s), 0)),
        pl.BlockSpec((size, 32), lambda i, s: (mine(i, s), 0)),
        pl.BlockSpec((16, LANES), lambda i, s: (0, 0)),
        whole,
    ]
    if into is not None:
        aliases = {len(args) + n: n for n in range(len(into))}
        args = [*args, *into]
        specs = [*specs, *[pl.BlockSpec(memory_space=pl.ANY)] * len(into)]
    return pl.pallas_call(
        functools.partial(transport_kernel, size, second_pass),
        out_shape=(*outs, jax.ShapeDtypeStruct((16, width), F32)),
        grid_spec=pltpu.PrefetchScalarGridSpec(
            num_scalar_prefetch=1,
            grid=(steps,),
            in_specs=specs,
            out_specs=[*out_specs, whole],
            scratch_shapes=scratch,
        ),
        input_output_aliases=aliases,
        compiler_params=params(),
        name="transport_second" if second_pass else "transport_first",
        cost_estimate=pl.CostEstimate(
            flops=60 * chunk * width, transcendentals=0, bytes_accessed=chunk * LANES * 4 * 19
        ),
    )(*args)


def sweep_block(inputs, relax, rate):
    start, flux_x, flux_y = inputs
    lane = lax.broadcasted_iota(jnp.int32, (8, LANES), 1)
    inner_low = jnp.where(lane == 0, 0.0, 1.0)
    inner_high = jnp.where(lane == LANES - 1, 0.0, 1.0)

    def block(array, row):
        if row < 0 or row >= SPAN:
            return jnp.zeros((8, LANES), F32)
        return array[:, row * LANES : (row + 1) * LANES]

    def lower(value):
        return pltpu.roll(value, 1, 1) * inner_low

    def upper(value):
        return pltpu.roll(value, LANES - 1, 1) * inner_high

    source = []
    for row in range(SPAN):
        diff_x = 0.5 * (block(flux_x, row + 1) - block(flux_x, row - 1))
        side = block(flux_y, row)
        diff_y = 0.5 * (upper(side) - lower(side))
        source.append(block(start, row) - SOURCE_WEIGHT * (diff_x + diff_y))
    zero = jnp.zeros((8, LANES), F32)
    kappa = [block(rate, row) for row in range(SPAN)]
    scale = [block(relax, row) for row in range(SPAN)]
    state = [block(start, row) for row in range(SPAN)]
    for _ in range(SWEEPS):
        near = [zero, *state, zero]
        state = [
            (source[row] + kappa[row] * (near[row] + near[row + 2] + lower(near[row + 1]) + upper(near[row + 1])))
            * scale[row]
            for row in range(SPAN)
        ]
    return jnp.concatenate(state, axis=1)


def stacked(value):
    first = value.astype(BF16)
    rest = value - first.astype(F32)
    second = rest.astype(BF16)
    third = (rest - second.astype(F32)).astype(BF16)
    return jnp.concatenate([first, second, third, first, second, first], axis=0)


def relax_rows(rate):
    inside = rate > 0.0
    kappa = jnp.where(inside, 0.5 / jnp.where(inside, rate, 1.0), 0.0)
    scale = jnp.where(inside, 1.0 / (1.0 + 4.0 * kappa), 0.0)
    width = rate.shape[1]
    return jnp.broadcast_to(kappa, (8, width)), jnp.broadcast_to(scale, (8, width))


def place_blocks(info_ref, span_ref, own, pair_a, pair_b):
    odd = info_ref[1]
    width = BLOCK_ROWS * LANES
    span_ref[:, width : 2 * width] = own
    place_a = pl.multiple_of((1 - odd) * 2 * width, width)
    place_b = pl.multiple_of(odd * 2 * width, width)
    span_ref[:, pl.ds(place_a, width)] = pair_a
    span_ref[:, pl.ds(place_b, width)] = pair_b


def first_macro_kernel(
    info_ref, sum_ref, home_own_ref, both_a_ref, both_b_ref, gram_ref, mat_ref,
    change_ref, keep_ref, span_ref, home_ref,
):
    side = info_ref[0]
    odd = info_ref[1]
    width = BLOCK_ROWS * LANES
    part = STRIP_ROWS * LANES
    place_blocks(info_ref, span_ref, sum_ref[...], both_a_ref[:16, :], both_b_ref[:16, :])
    homes = (home_own_ref[...], both_a_ref[16:, :], both_b_ref[16:, :])
    for block, both in zip((1, (1 - odd) * 2, odd * 2), homes):
        for where, rows in ((side, both[:, :part]), (1 - side, both[:, part:])):
            spot = pl.multiple_of(block * width + where * part, part)
            home_ref[:, pl.ds(spot, part)] = rows
    home = home_ref[...]
    rate = home[13:14, :]
    ratio = jnp.where(home[14:15, :] > 0.5, 1.0, rate)
    mat = mat_ref[...]
    first = jnp.dot(mat, jnp.where(lax.broadcasted_iota(jnp.int32, home.shape, 0) < 13, home, 0.0), precision=HIGH)
    fields = first[:8] + first[24:]
    moments = span_ref[...] + ratio * jnp.dot(gram_ref[...], fields, precision=HIGH)
    all_parts = jnp.dot(mat, moments, precision=HIGH)
    start = all_parts[:8]
    kappa, scale = relax_rows(rate)
    state = sweep_block((start, all_parts[8:16], all_parts[16:24]), scale, kappa)
    change = ratio * fields + (state - start)
    span_ref[0:8, :] = change
    keep_ref[0:8, :] = state + all_parts[24:]
    keep_ref[8:9, :] = rate
    keep_ref[9:10, :] = ratio
    keep_ref[10:16, :] = jnp.zeros((6, SPAN * LANES), F32)
    for row in range(-2, 9):
        spot = jnp.where(side == 1, 15 - row, 8 + row)
        piece = span_ref[0:8, pl.ds(pl.multiple_of(spot * LANES, LANES), LANES)]
        change_ref[:, (row + 2) * LANES : (row + 3) * LANES] = stacked(piece)


def last_kernel(
    size, half, blocks, info_ref, sum_ref, sum_a_ref, sum_b_ref, keep_ref, gram_ref, mat_ref,
    table_ref, *refs
):
    count = len({source for source, *_ in blocks})
    sources = refs[:count]
    out_ref, change_ref, state_ref, span_ref, held_ref, ready_ref, in_sems, out_sems = refs[count:]
    side = info_ref[0]

    def copy_in(k):
        source, offset, _, _ = blocks[k]
        return pltpu.make_async_copy(
            sources[source].at[:, pl.ds(offset, size), :], held_ref.at[k], in_sems.at[k]
        )

    for k in range(len(blocks)):
        copy_in(k).start()
    place_blocks(info_ref, span_ref, sum_ref[...], sum_a_ref[...], sum_b_ref[...])
    fields = keep_ref[0:8, :]
    rate = keep_ref[8:9, :]
    ratio = keep_ref[9:10, :]
    moments = span_ref[...] + ratio * jnp.dot(gram_ref[...], fields, precision=HIGH)
    all_parts = jnp.dot(mat_ref[...], moments, precision=HIGH)
    start = all_parts[:8]
    kappa, scale = relax_rows(rate)
    state = sweep_block((start, all_parts[8:16], all_parts[16:24]), scale, kappa)
    span_ref[0:8, :] = ratio * fields + (state - start)
    span_ref[8:16, :] = state
    part = STRIP_ROWS * LANES
    spot = pl.ds(pl.multiple_of(2 * part + side * part, part), part)
    change_ref[...] = stacked(span_ref[0:8, spot])
    state = span_ref[8:16, spot]
    for row in range(STRIP_ROWS):
        state_ref[:, row, :] = state[:5, row * LANES : (row + 1) * LANES]

    def copy_out(k):
        _, offset, own, first = blocks[k]
        begin = (side if own else 1 - side) * half + first + offset
        return begin, pltpu.make_async_copy(
            ready_ref.at[k],
            out_ref.at[pl.ds(pl.multiple_of(begin * STRIP_ROWS, STRIP_ROWS * size), STRIP_ROWS * size), :],
            out_sems.at[k],
        )

    for k, (_, _, own, _) in enumerate(blocks):
        begin, copy = copy_out(k)
        lift = jnp.dot(
            table_ref[pl.ds(pl.multiple_of(begin, size), size), :],
            change_ref[...],
            preferred_element_type=F32,
        )
        copy_in(k).wait()
        flipped = side == (1 if own else 0)
        for row in range(STRIP_ROWS):
            index = jnp.where(flipped, 3 - row, row)
            ready_ref[k, strided(row, size), :] = (
                held_ref[k, index] + lift[:, row * LANES : (row + 1) * LANES]
            )
        copy.start()
    for k in range(len(blocks)):
        copy_out(k)[1].wait()


def last_macro(info, args, table, pieces, half, size):
    blocks = [
        (source, offset, own, first)
        for source, (rows, own, first) in enumerate(pieces)
        for offset in range(0, rows.shape[1], size)
    ]
    whole = pl.BlockSpec(memory_space=pltpu.VMEM)
    anywhere = pl.BlockSpec(memory_space=pl.ANY)
    return pl.pallas_call(
        functools.partial(last_kernel, size, half, blocks),
        out_shape=[
            jax.ShapeDtypeStruct((2 * half * STRIP_ROWS, LANES), F32),
            jax.ShapeDtypeStruct((48, STRIP_ROWS * LANES), BF16),
            jax.ShapeDtypeStruct((5, STRIP_ROWS, LANES), F32),
        ],
        in_specs=[
            pl.BlockSpec(memory_space=pltpu.SMEM),
            *[whole] * (len(args) + 1),
            *[anywhere] * len(pieces),
        ],
        out_specs=[anywhere, whole, whole],
        scratch_shapes=[
            pltpu.VMEM((16, SPAN * LANES), F32),
            pltpu.VMEM((len(blocks), STRIP_ROWS, size, LANES), F32),
            pltpu.VMEM((len(blocks), STRIP_ROWS * size, LANES), F32),
            pltpu.SemaphoreType.DMA((len(blocks),)),
            pltpu.SemaphoreType.DMA((len(blocks),)),
        ],
        compiler_params=params(63 * 1024 * 1024),
        name="last_macro",
        cost_estimate=pl.CostEstimate(
            flops=4000000, transcendentals=0, bytes_accessed=len(blocks) * size * LANES * 32
        ),
    )(info, *args, table, *[rows for rows, _, _ in pieces])


def macro(kernel, info, args, outs, scratch):
    vmem = pl.BlockSpec(memory_space=pltpu.VMEM)
    return pl.pallas_call(
        kernel,
        out_shape=outs,
        in_specs=[pl.BlockSpec(memory_space=pltpu.SMEM)] + [vmem] * len(args),
        out_specs=[vmem] * len(outs),
        scratch_shapes=scratch,
        compiler_params=params(),
        cost_estimate=pl.CostEstimate(flops=4000000, transcendentals=0, bytes_accessed=1000000),
    )(info, *args)


def finish_kernel(size, parts, side_ref, *refs):
    out_ref = refs[-1]
    rows = refs[: len(parts)]
    table_ref, change_ref = refs[len(parts) : len(parts) + 2]
    side = side_ref[0]
    step = pl.program_id(0)
    lift = jnp.dot(table_ref[...], change_ref[...], preferred_element_type=F32)
    for ref, (own, begin, count, _) in zip(rows, parts):

        @pl.when((step >= begin) & (step < begin + count))
        def _(ref=ref, flipped=(side == (1 if own else 0))):
            for row in range(STRIP_ROWS):
                index = jnp.where(flipped, 3 - row, row)
                out_ref[strided(row, size), :] = (
                    ref[index] + lift[:, row * LANES : (row + 1) * LANES]
                )


def finish(side, out, pieces, table, change, half, size):
    shift = half // size
    parts = []
    steps = 0
    for rows, own, first in pieces:
        count = rows.shape[1] // size
        parts.append((own, steps, count, first // size))
        steps += count

    def place(i, s):
        spot = 0
        for own, begin, count, at in parts:
            here = (s[0] if own else 1 - s[0]) * shift + at + i - begin
            spot = jnp.where(i >= begin, here, spot)
        return spot

    def rows_spec(begin, count):
        return pl.BlockSpec(
            (4, size, LANES), lambda i, s: (0, jnp.clip(i - begin, 0, count - 1), 0)
        )

    specs = [
        *[rows_spec(begin, count) for _, begin, count, _ in parts],
        pl.BlockSpec((size, 48), lambda i, s: (place(i, s), 0)),
        pl.BlockSpec(change.shape, lambda i, s: (0, 0)),
    ]
    args = [side, *[rows for rows, _, _ in pieces], table, change]
    aliases = {}
    if out is not None:
        specs.append(pl.BlockSpec(memory_space=pl.ANY))
        aliases = {len(args): 0}
        args.append(out)
    return pl.pallas_call(
        functools.partial(finish_kernel, size, parts),
        out_shape=jax.ShapeDtypeStruct((2 * half * STRIP_ROWS, LANES), F32),
        grid_spec=pltpu.PrefetchScalarGridSpec(
            num_scalar_prefetch=1,
            grid=(steps,),
            in_specs=specs,
            out_specs=pl.BlockSpec((4 * size, LANES), lambda i, s: (place(i, s), 0)),
        ),
        input_output_aliases=aliases,
        compiler_params=params(67043328),
        name="finish",
        cost_estimate=pl.CostEstimate(
            flops=2 * 48 * 4 * LANES * steps * size,
            transcendentals=0,
            bytes_accessed=steps * size * LANES * 4 * 8,
        ),
    )(*args)


def per_device(points, dist, cell_type, collision_rate, vel_index):
    count, rows, cols = dist.shape
    half = count // 2
    strips = lax.axis_size("strip")
    groups = lax.axis_size("vel")
    strip = lax.axis_index("strip")
    size, chunks = plan(half)
    firsts = [sum(chunks[:c]) for c in range(len(chunks))]
    order = range(len(chunks))
    later, cut = second_order(len(chunks))
    groups_of = [order[:cut], order[cut:]]
    side = (strip % 2).astype(jnp.int32).reshape(1)
    info = jnp.stack([strip % 2, (strip // 2) % 2]).astype(jnp.int32)

    swap_pairs = [(s, s ^ 1) for s in range(strips)]
    down_pairs = [
        (s, s + (2 if s % 2 == 0 else -2))
        for s in range(strips)
        if 0 <= s + (2 if s % 2 == 0 else -2) < strips
    ]
    up_pairs = [(b, a) for a, b in down_pairs]
    pair_a = [
        (s, s + (2 if (s // 2) % 2 == 0 else -2))
        for s in range(strips)
        if 0 <= s + (2 if (s // 2) % 2 == 0 else -2) < strips
    ]
    pair_b = [
        (s, s + (-2 if (s // 2) % 2 == 0 else 2))
        for s in range(strips)
        if 0 <= s + (-2 if (s // 2) % 2 == 0 else 2) < strips
    ]

    def swap(value):
        return lax.ppermute(value, "strip", swap_pairs)

    def with_flow(value):
        return lax.ppermute(value, "strip", down_pairs)

    def against_flow(value):
        return lax.ppermute(value, "strip", up_pairs)

    def both_z(value):
        return lax.ppermute(value, "strip", pair_a), lax.ppermute(value, "strip", pair_b)

    def sum_groups(value):
        total = value
        for shift in range(1, groups):
            total = total + lax.ppermute(
                value, "vel", [(g, (g + shift) % groups) for g in range(groups)]
            )
        return total

    flat = dist.reshape(count * rows, cols)
    wall = (cell_type == 1).astype(F32)
    cell_pair = jnp.concatenate([collision_rate, wall])
    other_cells = swap(cell_pair)

    packed = pack(side, flat, half, chunks[:1], 0, size)
    packed += pack(side, flat, half, chunks[1:], firsts[1], size)
    got, above = [], []
    for edge, mid in packed:
        edge = swap(edge)
        mid = swap(mid)
        above.append(with_flow(edge))
        got.append((mid, edge))
    tables = prepare(points, vel_index)
    table, _, weights = tables
    home, lowest = home_moments(side, flat, weights, half // 3)
    below = against_flow(lowest)
    gram = jnp.asarray(target_moments(points))
    mat = jnp.asarray(macro_matrix())

    def flow(own, other):
        odd = strip % 2 == 1
        return jnp.concatenate(
            [jnp.where(odd, own[::-1], own), jnp.where(odd, other[::-1], other)]
        )

    flow_rate = flow(collision_rate, other_cells[:rows])
    flow_fluid = 1.0 - flow(wall, other_cells[rows:])
    cells = jnp.concatenate([flow_fluid * (1.0 - flow_rate), flow_fluid])

    home = sum_groups(home)
    home = jnp.concatenate(
        [home[:13], collision_rate.reshape(1, -1), wall.reshape(1, -1), jnp.zeros((1, rows * cols), F32)]
    )
    home = jnp.concatenate([home, swap(home)], axis=1)

    width = BLOCK_ROWS * LANES
    sums = jnp.zeros((16, width), F32)
    kept = []
    for number, members in enumerate(groups_of):
        start = firsts[members[0]]
        length = sum(chunks[c] for c in members)
        held = None
        for c in members:
            *held, sums = transport(
                side, [flat, *got[c], above[c], below], tables, cells, sums, half,
                chunks[c], firsts[c], size, skip=firsts[c] - start, group=length, into=held,
            )
        next_above = with_flow(held[2])
        next_below = against_flow(held[0])
        kept.append((*held, next_above, next_below))

    total = sum_groups(sums)
    total = total + swap(total)
    both_a, both_b = both_z(jnp.concatenate([total, home]))
    change, keep = macro(
        first_macro_kernel, info,
        [total, home, both_a, both_b, gram, mat],
        [
            jax.ShapeDtypeStruct((48, 11 * LANES), BF16),
            jax.ShapeDtypeStruct((16, SPAN * LANES), F32),
        ],
        [pltpu.VMEM((16, SPAN * LANES), F32)] * 2,
    )

    sums = jnp.zeros((16, width), F32)
    near, back = None, {}
    for c in later:
        number = int(c >= cut)
        start = firsts[groups_of[number][0]]
        near, far, sums = transport(
            side, list(kept[number]), tables, cells, sums, half,
            chunks[c], firsts[c], size, change, skip=firsts[c] - start,
            into=None if near is None else [near],
        )
        back[c] = swap(far)
    total = sum_groups(sums)
    total = total + swap(total)
    sum_a, sum_b = both_z(total)
    pieces = [(near, True, 0), *[(back[c], False, firsts[c]) for c in later[:cut]]]
    out, change, state = last_macro(
        info, [total, sum_a, sum_b, keep, gram, mat], table, pieces, half, size
    )
    for c in later[cut:]:
        out = finish(side, out, [(back[c], False, firsts[c])], table, change, half, size)
    return out.reshape(dist.shape), state


def solution(mesh):
    def whole(dist, cell_type, collision_rate, vel_index):
        points = round(vel_index.shape[1] ** (1.0 / 3.0))
        in_specs = (P("vel", "strip", None), P("strip", None), P("strip", None), P(None, "vel"))
        out_specs = (P("vel", "strip", None), P(None, "strip", None))

        def body(*args):
            return per_device(points, *args)

        run = jax.shard_map(
            body, mesh=mesh, in_specs=in_specs, out_specs=out_specs, check_vma=False
        )
        return run(dist, cell_type, collision_rate, vel_index)

    return whole
```
